32 devices in a mesh: group: 4 (over y, x), row: 8 (over z, core).
Axes of the slice: x: 2, y: 2, z: 4, core: 2. Of those that a mesh axis runs over, the one named last changes fastest.
Arguments:
- snapshots: bfloat16 [1024, 8192], P(('group', 'row')), may hold values from -6 to 6
- bnd_index: int32 [16, 1024], replicated, may hold values from 0 to 8191
- recovery: bfloat16 [512, 512, 1024], P(('group', 'row')), may hold values from -0.1875 to 0.1875
- block_se: int32 [512], P(('group', 'row')), may hold values from 0 to 3
- connect: int32 [16384, 24], P(('group', 'row')), may hold values from 0 to 8703, as said below
- stress_mat: bfloat16 [16384, 6, 24], P(('group', 'row')), may hold values from -1.25 to 1.25
Outputs:
- stresses: bfloat16 [16384, 6, 1024], P(('group', 'row'))
The draws below stay inside these ranges and needn't reach their ends.
Inputs may be any that keep to these rules, and one draw needn't show every extreme that they name: `connect`: among one device's elements, the first 8192 entries of its connectivity, read element by element, name each of rows 256 to 8447 once.
All inputs are finite; a program needn't handle non-finite values.
Results may differ from the reference program's by a relative error of at most 0.0049.
Values may be sent and summed in bfloat16 or wider, within the bound.
No kernel may reach another device: no remote copies, remote signals or barrier semaphores. Data moves between devices by JAX's collectives and lax.ppermute only.
A program may use at most 128 MiB of HBM per device.

```python
import jax
import jax.numpy as jnp
from jax import lax

NB = 1024
SE_GRP = 4
BLK = 512
NBLK_DEV = 16
SNAP = 1024
HW = 256
NEL_DEV = 512
NC = 6
NDOF = 24
SE = 16
NBG = 8192
RBLOCKS = 512
ELEMS = 16384
N_GROUP = 4
N_ROW = 8


def draw_connect(key, part):
    device_count = ELEMS // NEL_DEV
    keys = jax.random.split(jax.random.fold_in(key, 11), device_count)

    def one_device(device_key):
        first_key, second_key = jax.random.split(device_key)
        own_rows = jax.random.permutation(first_key, BLK * NBLK_DEV).astype(jnp.int32) + HW
        others = jax.random.randint(second_key, (NEL_DEV * NDOF - BLK * NBLK_DEV,), 0, BLK * NBLK_DEV + 2 * HW).astype(jnp.int32)
        others = others.at[0].set(0).at[-1].set(BLK * NBLK_DEV + 2 * HW - 1)
        return jnp.concatenate([own_rows, others]).astype(jnp.int32)
    flat = jax.vmap(one_device)(keys)
    return flat.reshape(ELEMS, NDOF)


def with_ends(array, key, least, top_value):
    longest = array.shape.index(max(array.shape))
    spots = []
    for shift in (0, 1):
        where = [jax.random.randint(jax.random.fold_in(key, axis), (), 0, length) for axis, length in enumerate(array.shape)]
        where[longest] = (where[longest] + shift) % array.shape[longest]
        spots.append(tuple(where))
    return array.at[spots[0]].set(least).at[spots[1]].set(top_value)


def block_scale(rng, shape, pieces, smallest, top_value):
    def one(position, shards_of):
        draws = jax.random.uniform(jax.random.fold_in(jax.random.fold_in(rng, 6), position), (shards_of,), jnp.float32, smallest / len(pieces), top_value / len(pieces))
        return jnp.repeat(jnp.exp(draws), shape[position] // shards_of).reshape((-1,) + (1,) * (len(shape) - position - 1))

    factor_of = one(*pieces[0])
    for cut in pieces[1:]:
        factor_of = factor_of * one(*cut)
    return factor_of


def bell_draw(stream_key, extent, spread, limit, cuts=(), kind=jnp.bfloat16):
    array = spread * jax.random.normal(stream_key, extent, jnp.float32)
    if cuts:
        array = array * block_scale(stream_key, extent, cuts, -0.22, 0.18)
    return jnp.clip(array, -limit, limit).astype(kind)


def setup_inputs(seed: int = 0) -> dict:
    arg_keys = jax.random.split(jax.random.key(seed), 7)
    return {
        "snapshots": bell_draw(arg_keys[0], (SNAP, NBG), 1.0, 6.0, ((0, 32),)),
        "bnd_index": with_ends(jax.random.randint(arg_keys[1], (SE, NB), 0, NBG), jax.random.fold_in(arg_keys[1], 1), 0, NBG - 1).astype(jnp.int32),
        "recovery": bell_draw(arg_keys[2], (RBLOCKS, BLK, NB), NB ** -0.5, 0.1875, ((0, 32),)),
        "block_se": with_ends(jax.random.randint(arg_keys[3], (RBLOCKS,), 0, SE_GRP), jax.random.fold_in(arg_keys[3], 1), 0, SE_GRP - 1).astype(jnp.int32),
        "connect": draw_connect(jax.random.fold_in(arg_keys[6], 71), 0),
        "stress_mat": bell_draw(arg_keys[5], (ELEMS, NC, NDOF), NDOF ** -0.5, 1.25, ((0, 32),)),
    }


def reference(snapshots, bnd_index, recovery, block_se, connect, stress_mat):
    group_rows = N_ROW * BLK * NBLK_DEV
    group_blocks = N_ROW * NBLK_DEV
    group_elems = N_ROW * NEL_DEV

    def group_work(group_id):
        chosen = lax.dynamic_slice_in_dim(bnd_index, group_id * SE_GRP, SE_GRP, 0)
        picked = jnp.take(snapshots, chosen, axis=1)
        bvals = jnp.transpose(picked, (1, 0, 2))
        blocks = lax.dynamic_slice_in_dim(recovery, group_id * group_blocks, group_blocks, 0)
        owners = lax.dynamic_slice_in_dim(block_se, group_id * group_blocks, group_blocks, 0)

        def one_block(entry):
            matrix, which = entry
            sliced = lax.dynamic_index_in_dim(bvals, which, 0, keepdims=False)
            result = lax.dot_general(matrix, sliced, (((1,), (1,)), ((), ())), preferred_element_type=jnp.float32)
            return result.astype(jnp.bfloat16)

        interior = lax.map(one_block, (blocks, owners)).reshape(group_rows, SNAP)
        padded = jnp.pad(interior, ((HW, HW), (0, 0)))
        links = lax.dynamic_slice_in_dim(connect, group_id * group_elems, group_elems, 0).reshape(N_ROW, NEL_DEV, NDOF)
        mats = lax.dynamic_slice_in_dim(stress_mat, group_id * group_elems, group_elems, 0).reshape(N_ROW, NEL_DEV, NC, NDOF)
        row_ids = jnp.arange(N_ROW, dtype=jnp.int32)

        def one_device(entry):
            row_id, link_rows, mat_rows = entry
            values = jnp.take(padded, link_rows + row_id * (BLK * NBLK_DEV), axis=0)
            result = jnp.einsum('eck,ekt->ect', mat_rows.astype(jnp.float32), values.astype(jnp.float32))
            return result.astype(jnp.bfloat16)

        return lax.map(one_device, (row_ids, links, mats))

    results = lax.map(group_work, jnp.arange(N_GROUP, dtype=jnp.int32))
    return results.reshape(ELEMS, NC, SNAP)
```

```python
import functools

import jax
import jax.numpy as jnp
from jax import lax
from jax.experimental import pallas as pl
from jax.experimental.pallas import tpu as pltpu
from jax.sharding import PartitionSpec as P

HW = 256
SUB = 8
LANES = 128


def combine_kernel(
    conn, tags_ref, s_ref, rec_ref, head_ref, tail_ref, w_ref, tbl, gat,
    *, nfill, blk, nlt, nse, nc, ndof, inner
):
    step = pl.program_id(0)
    rows = SUB * ndof
    out_rows = SUB * nc

    def fill(src, base, count):
        def one(i, carry):
            at = pl.multiple_of(i * 16, 16)
            for j in range(nlt):
                part = src[pl.ds(at, 16), j * LANES:(j + 1) * LANES].astype(jnp.float32)
                tbl[pl.ds((base + at) * nlt + j, 16, stride=nlt), :] = part
            return carry

        lax.fori_loop(0, count // 16, one, 0, unroll=2)

    @pl.when(step < nfill)
    def _():
        fill(rec_ref.at[0], HW + step * blk, blk)

    @pl.when(step == 0)
    def _():
        fill(head_ref, 0, HW)
        fill(tail_ref, HW + nfill * blk, HW)

    @pl.when(step >= nfill)
    def _():
        spread = (
            lax.broadcasted_iota(jnp.int32, (ndof, rows), 1) % ndof
            == lax.broadcasted_iota(jnp.int32, (ndof, rows), 0)
        ).astype(jnp.bfloat16)
        own = (
            lax.broadcasted_iota(jnp.int32, (out_rows, rows), 1) // ndof
            == lax.broadcasted_iota(jnp.int32, (out_rows, rows), 0) // nc
        )

        def one(i, carry):
            first = ((step - nfill) * inner + i) * rows
            for q in range(rows):
                at = pl.multiple_of(conn[first + q] * nlt, nlt)
                gat[pl.ds(q, nlt, stride=rows), :] = tbl[pl.ds(at, nlt), :]
            at = pl.multiple_of(i * out_rows, out_rows)
            wide = jnp.dot(s_ref[pl.ds(at, out_rows), :], spread, preferred_element_type=jnp.float32)
            wide = jnp.where(own, wide, 0.0)
            tag = jnp.broadcast_to(tags_ref[i], (out_rows, rows))
            parts = [jnp.where(tag == se, wide, 0.0).astype(jnp.bfloat16) for se in range(nse)]
            lhs = jnp.concatenate(parts, axis=0)
            for j in range(0, nlt, 2):
                rhs = jnp.concatenate(
                    [gat[(j + d) * rows:(j + d + 1) * rows, :].astype(jnp.bfloat16) for d in range(2)], axis=1
                )
                res = jnp.dot(lhs, rhs, preferred_element_type=jnp.float32).astype(jnp.bfloat16)
                for se in range(nse):
                    col = (se * nlt + j) * LANES
                    w_ref[pl.ds(at, out_rows), col:col + 2 * LANES] = res[se * out_rows:(se + 1) * out_rows]
            return carry

        lax.fori_loop(0, inner, one, 0)


def combine(conn, tags, smat, recovery, head, tail, nse):
    nblk, blk, nb = recovery.shape
    nel = conn.shape[0]
    ndof = conn.shape[1]
    nc = smat.shape[1]
    nlt = nb // LANES
    inner = 4
    rows = SUB * ndof
    steps = nel // (SUB * inner)
    kern = functools.partial(
        combine_kernel, nfill=nblk, blk=blk, nlt=nlt, nse=nse, nc=nc, ndof=ndof, inner=inner
    )
    later = lambda i: jnp.maximum(i - nblk, 0)
    return pl.pallas_call(
        kern,
        out_shape=jax.ShapeDtypeStruct((nel * nc, nse * nb), jnp.bfloat16),
        grid_spec=pltpu.PrefetchScalarGridSpec(
            num_scalar_prefetch=1,
            grid=(nblk + steps,),
            in_specs=[
                pl.BlockSpec((inner, 1, rows), lambda i, c: (later(i), 0, 0)),
                pl.BlockSpec((SUB * inner * nc, ndof), lambda i, c: (later(i), 0)),
                pl.BlockSpec((1, blk, nb), lambda i, c: (jnp.minimum(i, nblk - 1), 0, 0)),
                pl.BlockSpec((HW, nb), lambda i, c: (0, 0)),
                pl.BlockSpec((HW, nb), lambda i, c: (0, 0)),
            ],
            out_specs=pl.BlockSpec((SUB * inner * nc, nse * nb), lambda i, c: (later(i), 0)),
            scratch_shapes=[
                pltpu.VMEM(((nblk * blk + 2 * HW) * nlt, LANES), jnp.float32),
                pltpu.VMEM((rows * nlt, LANES), jnp.float32),
            ],
        ),
        compiler_params=pltpu.CompilerParams(
            dimension_semantics=("arbitrary",), vmem_limit_bytes=60 << 20
        ),
        name="combine",
    )(conn.reshape(-1), tags.reshape(-1, 1, rows), smat.reshape(nel * nc, ndof), recovery, head, tail)


def pick_kernel(idx, *refs, nsrc, tper, chunk):
    srcs = refs[:nsrc]
    o_ref, tbl, buf = refs[nsrc:]
    step = pl.program_id(0)
    nd = tbl.shape[0]

    @pl.when(step == 0)
    def _():
        def one(i, carry):
            at = pl.multiple_of(i * LANES, LANES)
            parts = [s[:, pl.ds(at, LANES)].astype(jnp.float32) for s in srcs]
            short = LANES - nsrc * tper
            if short:
                parts.append(jnp.zeros((short, LANES), jnp.float32))
            tbl[pl.ds(at, LANES), :] = jnp.concatenate(parts, axis=0).T
            return carry

        lax.fori_loop(0, nd // LANES, one, 0)

    def some(i, carry):
        at = pl.multiple_of(i * 64, 64)
        for q in range(64):
            buf[pl.ds(at + q, 1), :] = tbl[pl.ds(idx[step * chunk + at + q], 1), :]
        return carry

    lax.fori_loop(0, chunk // 64, some, 0)
    o_ref[...] = buf[...].astype(jnp.bfloat16)


def pick(idx, srcs):
    tper, nd = srcs[0].shape
    n = idx.shape[0]
    chunk = 1024
    return pl.pallas_call(
        functools.partial(pick_kernel, nsrc=len(srcs), tper=tper, chunk=chunk),
        out_shape=jax.ShapeDtypeStruct((n, LANES), jnp.bfloat16),
        grid_spec=pltpu.PrefetchScalarGridSpec(
            num_scalar_prefetch=1,
            grid=(n // chunk,),
            in_specs=[pl.BlockSpec((tper, nd), lambda i, c: (0, 0)) for _ in srcs],
            out_specs=pl.BlockSpec((chunk, LANES), lambda i, c: (i, 0)),
            scratch_shapes=[pltpu.VMEM((nd, LANES), jnp.float32), pltpu.VMEM((chunk, LANES), jnp.float32)],
        ),
        compiler_params=pltpu.CompilerParams(
            dimension_semantics=("arbitrary",), vmem_limit_bytes=40 << 20
        ),
        name="pick",
    )(idx, *srcs)


def product_kernel(w_ref, b_hbm, o_ref, bt, sem, *, nchunk, ngroup, tper):
    @pl.when(pl.program_id(0) == 0)
    def _():
        copies = [
            pltpu.make_async_copy(b_hbm.at[r], bt.at[:, r * LANES:(r + 1) * LANES], sem.at[r])
            for r in range(nchunk)
        ]
        for c in copies:
            c.start()
        for c in copies:
            c.wait()

    res = jnp.dot(w_ref[...], bt[...], preferred_element_type=jnp.float32)
    per = LANES // tper
    lane = lax.broadcasted_iota(jnp.int32, (res.shape[0], LANES), 1) // tper
    for g in range(ngroup):
        for h in range(nchunk // per):
            tile = None
            for j in range(per):
                src = (h * per + j) * LANES
                moved = pltpu.roll(res[:, src:src + LANES], ((j - g) * tper) % LANES, 1)
                tile = moved if tile is None else jnp.where(lane == j, moved, tile)
            col = (g * (nchunk // per) + h) * LANES
            o_ref[:, col:col + LANES] = tile.astype(jnp.bfloat16)


def product(w, chunks, ngroup, tper, snap):
    m, k = w.shape
    nchunk = chunks.shape[0]
    mb = 256
    return pl.pallas_call(
        functools.partial(product_kernel, nchunk=nchunk, ngroup=ngroup, tper=tper),
        out_shape=jax.ShapeDtypeStruct((m, snap), jnp.bfloat16),
        grid=(m // mb,),
        in_specs=[pl.BlockSpec((mb, k), lambda i: (i, 0)), pl.BlockSpec(memory_space=pl.ANY)],
        out_specs=pl.BlockSpec((mb, snap), lambda i: (i, 0)),
        scratch_shapes=[
            pltpu.VMEM((k, nchunk * LANES), jnp.bfloat16),
            pltpu.SemaphoreType.DMA((nchunk,)),
        ],
        compiler_params=pltpu.CompilerParams(
            dimension_semantics=("arbitrary",), vmem_limit_bytes=56 << 20
        ),
        name="product",
    )(w, chunks)


def body(snapshots, bnd_index, recovery, block_se, connect, stress_mat):
    ngroup = lax.axis_size("group")
    nrow = lax.axis_size("row")
    nse = bnd_index.shape[0] // ngroup
    nblk, blk, nb = recovery.shape
    tper = snapshots.shape[0]
    snap = tper * ngroup * nrow
    group = lax.axis_index("group")

    gathered = lax.all_gather(snapshots, "group", axis=0, tiled=False)
    idx = lax.dynamic_slice_in_dim(bnd_index, group * nse, nse, 0).reshape(-1)
    picked = pick(idx, [gathered[g] for g in range(ngroup)])
    chunks = lax.all_gather(picked, "row", axis=0, tiled=False)

    ends = nrow - 1
    up = [(i, i + 1) for i in range(ends)]
    down = [(i + 1, i) for i in range(ends)]
    head = lax.ppermute(recovery[nblk - 1, blk - HW:], "row", up)
    tail = lax.ppermute(recovery[0, :HW], "row", down)
    se_f = block_se.astype(jnp.float32)
    ends_se = jnp.stack([se_f[-1:], se_f[:1]])
    head_se = lax.ppermute(se_f[-1:], "row", up)
    tail_se = lax.ppermute(se_f[:1], "row", down)
    se_all = jnp.concatenate([head_se, se_f, tail_se]).astype(jnp.int32)
    where = (connect + (blk - HW)) // blk
    tags = jnp.zeros_like(connect)
    for b in range(nblk + 2):
        tags = jnp.where(where == b, se_all[b], tags)
    w = combine(connect, tags, stress_mat, recovery, head, tail, nse)
    out = product(w, chunks, ngroup, tper, snap)
    return out.reshape(connect.shape[0], stress_mat.shape[1], snap)


def solution(mesh):
    in_specs = (
        P(("group", "row"), None),
        P(),
        P(("group", "row"), None, None),
        P(("group", "row")),
        P(("group", "row"), None),
        P(("group", "row"), None, None),
    )
    out_specs = P(("group", "row"), None, None)
    return jax.shard_map(body, mesh=mesh, in_specs=in_specs, out_specs=out_specs, check_vma=False)
```

```python
import functools

import jax
import jax.numpy as jnp
from jax import lax
from jax.experimental import pallas as pl
from jax.experimental.pallas import tpu as pltpu
from jax.sharding import PartitionSpec as P

HW = 256
SUB = 8
LANES = 128


def combine_kernel(conn, se, grow_ref, s_ref, rec_ref, head_ref, tail_ref, w_ref, tbl, g0, g1,
    *, nfill, blk, nlt, nse, nc, ndof, inner, ts, gs,
):
    step = pl.program_id(0)
    rows = SUB * ndof
    out_rows = SUB * nc
    steps = pl.num_programs(0) - nfill

    def fill(src, base, count):
        def one(i, carry):
            at = pl.multiple_of(i * 16, 16)
            for j in range(nlt):
                part = src[pl.ds(at, 16), j * LANES:(j + 1) * LANES].astype(jnp.float32)
                tbl[pl.ds((base + at) * ts + j, 16, stride=ts), :] = part
            return carry
        lax.fori_loop(0, count // 16, one, 0, unroll=2)

    def gather(group, dst):
        first = group * rows
        for q in range(rows):
            dst[pl.ds(q, nlt, stride=gs), :] = tbl[pl.ds(conn[first + q] * ts, nlt), :]

    def matmul(i, src):
        own = (
            lax.broadcasted_iota(jnp.int32, (SUB, rows), 1) % SUB
            == lax.broadcasted_iota(jnp.int32, (SUB, rows), 0)
        )
        where = (grow_ref[i] + (blk - HW)) // blk
        tag = jnp.zeros((1, rows), jnp.int32)
        for b in range(nfill + 2):
            tag = jnp.where(where == b, se[b], tag)
        tag = jnp.where(own, jnp.broadcast_to(tag, (SUB, rows)), -1)
        parts = []
        smat = s_ref[i].astype(jnp.float32)
        for s in range(nse):
            hit = tag == s
            for c in range(nc):
                parts.append(jnp.where(hit, jnp.broadcast_to(smat[c:c + 1], (SUB, rows)), 0.0))
        lhs = jnp.concatenate(parts, axis=0).astype(jnp.bfloat16)
        at = pl.multiple_of(i * SUB, SUB)
        for j in range(0, nlt, 2):
            rhs = jnp.concatenate(
                [src[(j + d) * gs:(j + d) * gs + rows, :].astype(jnp.bfloat16) for d in range(2)], axis=1)
            res = jnp.dot(lhs, rhs, preferred_element_type=jnp.float32).astype(jnp.bfloat16)
            for s in range(nse):
                col = (s * nlt + j) * LANES
                for c in range(nc):
                    w_ref[c, pl.ds(at, SUB), col:col + 2 * LANES] = res[(s * nc + c) * SUB:(s * nc + c + 1) * SUB]

    @pl.when(step < nfill)
    def _():
        fill(rec_ref.at[0], HW + step * blk, blk)

    @pl.when(step == 0)
    def _():
        fill(head_ref, 0, HW)
        fill(tail_ref, HW + nfill * blk, HW)

    @pl.when(step >= nfill)
    def _():
        base = (step - nfill) * inner
        last = steps * inner - 1

        @pl.when(step == nfill)
        def _():
            gather(0, g0)

        def two(i, carry):
            n = base + 2 * i
            gather(n + 1, g1)
            matmul(2 * i, g0)
            gather(jnp.minimum(n + 2, last), g0)
            matmul(2 * i + 1, g1)
            return carry
        lax.fori_loop(0, inner // 2, two, 0)

def combine(conn, se, grow, smat, recovery, head, tail, nse, inner=4):
    nblk, blk, nb = recovery.shape
    ngrp, _, rows = grow.shape
    nel = ngrp * SUB
    ndof = rows // SUB
    nc = smat.shape[1]
    nlt = nb // LANES
    steps = ngrp // inner
    ts = nlt + 1
    gs = rows + 1
    kern = functools.partial(
        combine_kernel, nfill=nblk, blk=blk, nlt=nlt, nse=nse, nc=nc, ndof=ndof, inner=inner, ts=ts, gs=gs
    )
    later = lambda i: jnp.maximum(i - nblk, 0)
    return pl.pallas_call(
        kern,
        out_shape=jax.ShapeDtypeStruct((nc, nel, nse * nb), jnp.bfloat16),
        grid_spec=pltpu.PrefetchScalarGridSpec(
            num_scalar_prefetch=2,
            grid=(nblk + steps,),
            in_specs=[
                pl.BlockSpec((inner, 1, rows), lambda i, c, s: (later(i), 0, 0)),
                pl.BlockSpec((inner, nc, rows), lambda i, c, s: (later(i), 0, 0)),
                pl.BlockSpec((1, blk, nb), lambda i, c, s: (jnp.minimum(i, nblk - 1), 0, 0)),
                pl.BlockSpec((HW, nb), lambda i, c, s: (0, 0)),
                pl.BlockSpec((HW, nb), lambda i, c, s: (0, 0)),
            ],
            out_specs=pl.BlockSpec((nc, SUB * inner, nse * nb), lambda i, c, s: (0, later(i), 0)),
            scratch_shapes=[
                pltpu.VMEM(((nblk * blk + 2 * HW) * ts, LANES), jnp.float32),
                pltpu.VMEM((gs * nlt, LANES), jnp.float32),
                pltpu.VMEM((gs * nlt, LANES), jnp.float32),
            ],
        ),
        compiler_params=pltpu.CompilerParams(dimension_semantics=("arbitrary",), vmem_limit_bytes=60 << 20),
        name="combine",
    )(conn, se, grow, smat, recovery, head, tail)


def pick_near_kernel(idx, *refs, nsrc, half, parts, chunk):
    srcs = refs[:nsrc]
    o_ref, tbl = refs[nsrc:nsrc + 2]
    bufs = refs[nsrc + 2:]
    step = pl.program_id(0)
    nd = tbl.shape[0]
    total = chunk * pl.num_programs(0)

    @pl.when(step == 0)
    def _():
        def one(i, carry):
            at = pl.multiple_of(i * LANES, LANES)
            rows = jnp.concatenate([s[:, pl.ds(at, LANES)].astype(jnp.float32) for s in srcs] * parts, axis=0)
            tbl[pl.ds(at, LANES), :] = rows.T
            return carry

        lax.fori_loop(0, nd // LANES, one, 0, unroll=2)

    def some(i, carry):
        at = pl.multiple_of(i * 64, 64)
        for p in range(parts):
            for q in range(64):
                k = idx[p * total + step * chunk + at + q]
                bufs[p][pl.ds(at + q, 1), :] = tbl[pl.ds(k, 1), :]
        return carry

    lax.fori_loop(0, chunk // 64, some, 0)
    piece = lax.broadcasted_iota(jnp.int32, (chunk, LANES), 1) // (LANES // parts)
    out = bufs[0][...]
    for p in range(1, parts):
        out = jnp.where(piece == p, bufs[p][...], out)
    o_ref[...] = out.astype(jnp.bfloat16)


def pick_near(idx, srcs):
    half, nd = srcs[0].shape
    parts = LANES // (half * len(srcs))
    n = idx.shape[0] // parts
    chunk = min(n, 1024)
    return pl.pallas_call(
        functools.partial(pick_near_kernel, nsrc=len(srcs), half=half, parts=parts, chunk=chunk),
        out_shape=jax.ShapeDtypeStruct((n, LANES), jnp.bfloat16),
        grid_spec=pltpu.PrefetchScalarGridSpec(
            num_scalar_prefetch=1,
            grid=(n // chunk,),
            in_specs=[pl.BlockSpec((half, nd), lambda i, c: (0, 0)) for _ in srcs],
            out_specs=pl.BlockSpec((chunk, LANES), lambda i, c: (i, 0)),
            scratch_shapes=[pltpu.VMEM((nd, LANES), jnp.float32)]
            + [pltpu.VMEM((chunk, LANES), jnp.float32) for _ in range(parts)],
        ),
        compiler_params=pltpu.CompilerParams(
            dimension_semantics=("arbitrary",), vmem_limit_bytes=40 << 20
        ),
        name="pick_near",
    )(idx, *srcs)


def pick_far_kernel(idx, src, *refs, nout, order, half, chunk, per_out):
    outs = refs[:nout]
    tbl, buf = refs[nout:]
    step = pl.program_id(0)
    nd = tbl.shape[0]

    @pl.when(step == 0)
    def _():
        def one(i, carry):
            at = pl.multiple_of(i * LANES, LANES)
            rows = jnp.concatenate([src[r, :, pl.ds(at, LANES)].astype(jnp.float32) for r in order], axis=0)
            tbl[pl.ds(at, LANES), :] = rows.T
            return carry

        lax.fori_loop(0, nd // LANES, one, 0, unroll=2)

    def some(i, carry):
        at = pl.multiple_of(i * 64, 64)
        for q in range(64):
            buf[pl.ds(at + q, 1), :] = tbl[pl.ds(idx[step * chunk + at + q], 1), :]
        return carry

    lax.fori_loop(0, chunk // 64, some, 0)
    for s in range(nout):
        @pl.when(step // per_out == s)
        def _():
            outs[s][...] = buf[...].astype(jnp.bfloat16)


def pick_far(idx, src, order):
    nrow, half, nd = src.shape
    nout, n = idx.shape
    chunk = min(n, 1024)
    per_out = n // chunk

    def place(s):
        return lambda i, c: (jnp.clip(i - s * per_out, 0, per_out - 1), 0)

    return pl.pallas_call(
        functools.partial(
            pick_far_kernel, nout=nout, order=order, half=half, chunk=chunk, per_out=per_out
        ),
        out_shape=[jax.ShapeDtypeStruct((n, LANES), jnp.bfloat16) for _ in range(nout)],
        grid_spec=pltpu.PrefetchScalarGridSpec(
            num_scalar_prefetch=1,
            grid=(nout * per_out,),
            in_specs=[pl.BlockSpec((nrow, half, nd), lambda i, c: (0, 0, 0))],
            out_specs=[pl.BlockSpec((chunk, LANES), place(s)) for s in range(nout)],
            scratch_shapes=[pltpu.VMEM((nd, LANES), jnp.float32), pltpu.VMEM((chunk, LANES), jnp.float32)],
        ),
        compiler_params=pltpu.CompilerParams(
            dimension_semantics=("arbitrary",), vmem_limit_bytes=40 << 20
        ),
        name="pick_far",
    )(idx.reshape(-1), src)


def product_kernel(
    where, w_ref, *refs, ngroup, nrow, tper, half, parts
):
    mine = refs[:ngroup]
    theirs = refs[ngroup:2 * ngroup]
    near_hbm, o_ref, bt, near, sem = refs[2 * ngroup:]
    group = where[0]
    core = where[1]
    nh = tper * nrow // LANES
    per = LANES // tper
    npair = ngroup * half // tper
    rows = bt.shape[0] // 2
    nk = bt.shape[0] // parts

    @pl.when(pl.program_id(0) == 0)
    def _():
        last = pltpu.make_async_copy(near_hbm, near, sem.at[2 * ngroup])
        last.start()
        copies = []
        for s in range(ngroup):
            cols = slice(s * LANES, (s + 1) * LANES)
            for d, ref in ((0, mine[s]), (1, theirs[s])):
                at = pl.multiple_of(jnp.where(core == d, 0, 1) * rows, rows)
                copies.append(pltpu.make_async_copy(ref, bt.at[pl.ds(at, rows), cols], sem.at[2 * s + d]))
        for c in copies:
            c.start()
        last.wait()
        step_rows = min(nk, 256)
        lane = lax.broadcasted_iota(jnp.int32, (step_rows, LANES), 1) // tper

        def arrange(i, carry):
            at = pl.multiple_of(i * step_rows, step_rows)
            for h in range(nh):
                got = [near[h * per + j, pl.ds(at, step_rows), :].astype(jnp.float32) for j in range(per)]
                for p in range(npair):
                    for kp in range(parts):
                        tile = None
                        for j in range(per):
                            shift = (tper * j - (kp * (LANES // parts) + tper * p)) % LANES
                            moved = pltpu.roll(got[j], shift, 1) if shift else got[j]
                            tile = moved if tile is None else jnp.where(lane == j, moved, tile)
                        col = (ngroup + h * npair + p) * LANES
                        bt[pl.ds(kp * nk + at, step_rows), col:col + LANES] = tile.astype(jnp.bfloat16)
            return carry

        lax.fori_loop(0, nk // step_rows, arrange, 0)
        for c in copies:
            c.wait()

    res = jnp.dot(w_ref[...], bt[...], preferred_element_type=jnp.float32)
    slot = (lax.broadcasted_iota(jnp.int32, (res.shape[0], LANES), 1) // half) % 2
    for s in range(ngroup):
        far = res[:, s * LANES:(s + 1) * LANES]
        for h in range(nh):
            first = pltpu.roll(far, LANES - half * h, 1) if h else far
            at = (ngroup + h * npair + s // 2) * LANES
            second = res[:, at:at + LANES]
            if s % 2 == 0:
                second = pltpu.roll(second, half, 1)
            tile = jnp.where(slot == 0, first, second).astype(jnp.bfloat16)
            col = pl.multiple_of(((group ^ s) * nh + h) * LANES, LANES)
            o_ref[:, pl.ds(col, LANES)] = tile


def product(where, w, mine, theirs, near, tper, snap):
    m, k = w.shape
    ngroup = len(mine)
    nrow, nk, _ = near.shape
    mb = 256
    return pl.pallas_call(
        functools.partial(
            product_kernel, ngroup=ngroup, nrow=nrow, tper=tper, half=tper // 2, parts=k // nk
        ),
        out_shape=jax.ShapeDtypeStruct((m, snap), jnp.bfloat16),
        grid_spec=pltpu.PrefetchScalarGridSpec(
            num_scalar_prefetch=1,
            grid=(m // mb,),
            in_specs=[pl.BlockSpec((mb, k), lambda i, c: (i, 0))]
            + [pl.BlockSpec(memory_space=pl.ANY)] * (2 * ngroup + 1),
            out_specs=pl.BlockSpec((mb, snap), lambda i, c: (i, 0)),
            scratch_shapes=[
                pltpu.VMEM((k, snap), jnp.bfloat16),
                pltpu.VMEM(near.shape, jnp.bfloat16),
                pltpu.SemaphoreType.DMA((2 * ngroup + 1,)),
            ],
        ),
        compiler_params=pltpu.CompilerParams(
            dimension_semantics=("arbitrary",), vmem_limit_bytes=56 << 20
        ),
        name="product",
    )(where, w, *mine, *theirs, near)


def body(snapshots, bnd_index, recovery, block_se, connect, stress_mat):
    ngroup = lax.axis_size("group")
    nrow = lax.axis_size("row")
    nse = bnd_index.shape[0] // ngroup
    nblk, blk, nb = recovery.shape
    nel, nc, ndof = stress_mat.shape
    tper = snapshots.shape[0]
    half = tper // 2
    snap = tper * ngroup * nrow
    group = lax.axis_index("group")
    core = lax.axis_index("row") % 2
    swap = lambda s: [(i, i ^ s) for i in range(ngroup)]
    other = [(i, i ^ 1) for i in range(nrow)]

    top = snapshots[:half]
    bottom = snapshots[half:]
    along_row = lax.all_gather(top, "row", axis=0, tiled=False)
    along_group = [bottom] + [lax.ppermute(bottom, "group", swap(s)) for s in range(1, ngroup)]

    own_idx = lax.dynamic_slice_in_dim(bnd_index, group * nse, nse, 0).reshape(-1)
    near = lax.all_gather(pick_near(own_idx, along_group), "row", axis=0, tiled=False)

    rows = nse * nb // 2
    far_idx = jnp.stack([
        lax.dynamic_slice_in_dim(
            lax.dynamic_slice_in_dim(bnd_index, (group ^ s) * nse, nse, 0).reshape(-1), core * rows, rows, 0
        )
        for s in range(ngroup)
    ])
    per = LANES // tper
    order = [per * h + j for j in range(per) for h in range(nrow // per)]
    far = pick_far(far_idx, along_row, order)
    mine = [far[0]] + [lax.ppermute(far[s], "group", swap(s)) for s in range(1, ngroup)]
    theirs = [lax.ppermute(x, "row", other) for x in mine]

    ends = nrow - 1
    up = [(i, i + 1) for i in range(ends)]
    down = [(i + 1, i) for i in range(ends)]
    head = lax.ppermute(recovery[nblk - 1, blk - HW:], "row", up)
    tail = lax.ppermute(recovery[0, :HW], "row", down)
    head_se = lax.ppermute(block_se[-1:], "row", up)
    tail_se = lax.ppermute(block_se[:1], "row", down)
    se_all = jnp.concatenate([head_se, block_se, tail_se])

    ngrp = nel // SUB
    conn = connect.T.reshape(ndof, ngrp, SUB).transpose(1, 0, 2).reshape(ngrp, 1, ndof * SUB)
    smat = stress_mat.transpose(1, 2, 0).reshape(nc, ndof, ngrp, SUB).transpose(2, 0, 1, 3)
    smat = smat.reshape(ngrp, nc, ndof * SUB)
    flat, far0 = lax.optimization_barrier((conn.reshape(-1), far[0]))
    mine[0] = far0
    w = combine(flat, se_all, conn, smat, recovery, head, tail, nse)
    where = jnp.stack([group, core]).astype(jnp.int32)
    out = product(where, w.reshape(nc * nel, nse * nb), mine, theirs, near, tper, snap)
    return out.reshape(nc, nel, snap).transpose(1, 0, 2)


def solution(mesh):
    in_specs = (
        P(("group", "row"), None),
        P(),
        P(("group", "row"), None, None),
        P(("group", "row")),
        P(("group", "row"), None),
        P(("group", "row"), None, None),
    )
    out_specs = P(("group", "row"), None, None)
    return jax.shard_map(body, mesh=mesh, in_specs=in_specs, out_specs=out_specs, check_vma=False)
```

```python
import functools

import jax
import jax.numpy as jnp
from jax import lax
from jax.experimental import pallas as pl
from jax.experimental.pallas import tpu as pltpu
from jax.sharding import PartitionSpec as P

HW = 256
SUB = 8
LANES = 128


def combine_kernel(conn, se, grow_ref, s_ref, rec_ref, head_ref, tail_ref, w_ref, tbl, g0, g1, g2, g3,
    *, nfill, blk, nlt, nse, nc, ndof, inner, ts, gs,
):
    step = pl.program_id(0)
    rows = SUB * ndof
    out_rows = SUB * nc
    steps = pl.num_programs(0) - nfill

    def fill(src, base, count):
        def one(i, carry):
            at = pl.multiple_of(i * 16, 16)
            for j in range(nlt):
                part = src[pl.ds(at, 16), j * LANES:(j + 1) * LANES].astype(jnp.float32)
                tbl[pl.ds((base + at) * ts + j, 16, stride=ts), :] = part
            return carry
        lax.fori_loop(0, count // 16, one, 0, unroll=4)

    def gather(group, dst):
        first = group * rows
        for q in range(rows):
            dst[pl.ds(q, nlt, stride=gs), :] = tbl[pl.ds(conn[first + q] * ts, nlt), :]

    own = (
        lax.broadcasted_iota(jnp.int32, (SUB, rows), 1) % SUB
        == lax.broadcasted_iota(jnp.int32, (SUB, rows), 0)
    )

    def left(i):
        where = (grow_ref[i] + (blk - HW)) // blk
        tag = jnp.zeros((1, rows), jnp.int32)
        for b in range(nfill + 2):
            tag = jnp.where(where == b, se[b], tag)
        tag = jnp.where(own, jnp.broadcast_to(tag, (SUB, rows)), -1)
        smat = s_ref[i].astype(jnp.float32)
        parts = []
        for s in range(nse):
            hit = tag == s
            for c in range(nc):
                parts.append(jnp.where(hit, jnp.broadcast_to(smat[c:c + 1], (SUB, rows)), 0.0))
        return jnp.concatenate(parts, axis=0).astype(jnp.bfloat16)

    def matmul(i, srcs):
        lhs = [left(i), left(i + 1)]
        at = pl.multiple_of(i * SUB, 2 * SUB)
        for j in range(0, nlt, 2):
            res = []
            for l, src in zip(lhs, srcs):
                rhs = jnp.concatenate(
                    [src[(j + d) * gs:(j + d) * gs + rows, :].astype(jnp.bfloat16) for d in range(2)], axis=1)
                res.append(jnp.dot(l, rhs, preferred_element_type=jnp.float32))
            for s in range(nse):
                col = (s * nlt + j) * LANES
                for c in range(nc):
                    r0 = (s * nc + c) * SUB
                    both = jnp.concatenate([r[r0:r0 + SUB] for r in res], axis=0)
                    w_ref[c, pl.ds(at, 2 * SUB), col:col + 2 * LANES] = both.astype(jnp.bfloat16)

    @pl.when(step < nfill)
    def _():
        fill(rec_ref.at[0], HW + step * blk, blk)

    @pl.when(step == 0)
    def _():
        fill(head_ref, 0, HW)
        fill(tail_ref, HW + nfill * blk, HW)

    @pl.when(step >= nfill)
    def _():
        base = (step - nfill) * inner
        last = steps * inner - 1

        @pl.when(step == nfill)
        def _():
            gather(0, g0)
            gather(1, g1)

        def four(i, carry):
            n = base + 4 * i
            gather(n + 2, g2)
            gather(n + 3, g3)
            matmul(4 * i, (g0, g1))
            gather(jnp.minimum(n + 4, last), g0)
            gather(jnp.minimum(n + 5, last), g1)
            matmul(4 * i + 2, (g2, g3))
            return carry
        lax.fori_loop(0, inner // 4, four, 0)


def combine(conn, se, grow, smat, recovery, head, tail, nse, inner=4):
    nblk, blk, nb = recovery.shape
    ngrp, _, rows = grow.shape
    nel = ngrp * SUB
    ndof = rows // SUB
    nc = smat.shape[1]
    nlt = nb // LANES
    steps = ngrp // inner
    ts = nlt + 1
    gs = rows + 1
    kern = functools.partial(
        combine_kernel, nfill=nblk, blk=blk, nlt=nlt, nse=nse, nc=nc, ndof=ndof, inner=inner, ts=ts, gs=gs
    )
    later = lambda i: jnp.maximum(i - nblk, 0)
    return pl.pallas_call(
        kern,
        out_shape=jax.ShapeDtypeStruct((nc, nel, nse * nb), jnp.bfloat16),
        grid_spec=pltpu.PrefetchScalarGridSpec(
            num_scalar_prefetch=2,
            grid=(nblk + steps,),
            in_specs=[
                pl.BlockSpec((inner, 1, rows), lambda i, c, s: (later(i), 0, 0)),
                pl.BlockSpec((inner, nc, rows), lambda i, c, s: (later(i), 0, 0)),
                pl.BlockSpec((1, blk, nb), lambda i, c, s: (jnp.minimum(i, nblk - 1), 0, 0)),
                pl.BlockSpec((HW, nb), lambda i, c, s: (0, 0)),
                pl.BlockSpec((HW, nb), lambda i, c, s: (0, 0)),
            ],
            out_specs=pl.BlockSpec((nc, SUB * inner, nse * nb), lambda i, c, s: (0, later(i), 0)),
            scratch_shapes=[
                pltpu.VMEM(((nblk * blk + 2 * HW) * ts, LANES), jnp.float32),
            ] + [pltpu.VMEM((gs * nlt, LANES), jnp.float32)] * 4,
        ),
        compiler_params=pltpu.CompilerParams(dimension_semantics=("arbitrary",), vmem_limit_bytes=60 << 20),
        cost_estimate=pl.CostEstimate(flops=30 * 10**9, bytes_accessed=120 << 20, transcendentals=0),
        name="combine",
    )(conn, se, grow, smat, recovery, head, tail)


def pick_near_kernel(idx, *refs, nsrc, half, parts, chunk):
    srcs = refs[:nsrc]
    o_ref, tbl = refs[nsrc:nsrc + 2]
    bufs = refs[nsrc + 2:]
    step = pl.program_id(0)
    nd = tbl.shape[0]
    total = chunk * pl.num_programs(0)

    @pl.when(step == 0)
    def _():
        def one(i, carry):
            at = pl.multiple_of(i * LANES, LANES)
            rows = jnp.concatenate([s[:, pl.ds(at, LANES)].astype(jnp.float32) for s in srcs] * parts, axis=0)
            tbl[pl.ds(at, LANES), :] = rows.T
            return carry

        lax.fori_loop(0, nd // LANES, one, 0, unroll=2)

    def some(i, carry):
        at = pl.multiple_of(i * 64, 64)
        for p in range(parts):
            for q in range(64):
                k = idx[p * total + step * chunk + at + q]
                bufs[p][pl.ds(at + q, 1), :] = tbl[pl.ds(k, 1), :]
        return carry

    lax.fori_loop(0, chunk // 64, some, 0)
    piece = lax.broadcasted_iota(jnp.int32, (chunk, LANES), 1) // (LANES // parts)
    out = bufs[0][...]
    for p in range(1, parts):
        out = jnp.where(piece == p, bufs[p][...], out)
    o_ref[...] = out.astype(jnp.bfloat16)


def pick_near(idx, srcs):
    half, nd = srcs[0].shape
    parts = LANES // (half * len(srcs))
    n = idx.shape[0] // parts
    chunk = min(n, 1024)
    return pl.pallas_call(
        functools.partial(pick_near_kernel, nsrc=len(srcs), half=half, parts=parts, chunk=chunk),
        out_shape=jax.ShapeDtypeStruct((n, LANES), jnp.bfloat16),
        grid_spec=pltpu.PrefetchScalarGridSpec(
            num_scalar_prefetch=1,
            grid=(n // chunk,),
            in_specs=[pl.BlockSpec((half, nd), lambda i, c: (0, 0)) for _ in srcs],
            out_specs=pl.BlockSpec((chunk, LANES), lambda i, c: (i, 0)),
            scratch_shapes=[pltpu.VMEM((nd, LANES), jnp.float32)]
            + [pltpu.VMEM((chunk, LANES), jnp.float32) for _ in range(parts)],
        ),
        compiler_params=pltpu.CompilerParams(
            dimension_semantics=("arbitrary",), vmem_limit_bytes=40 << 20
        ),
        name="pick_near",
    )(idx, *srcs)


def pick_far_kernel(idx, src, *refs, nout, order, half, chunk, per_out):
    outs = refs[:nout]
    tbl, buf = refs[nout:]
    step = pl.program_id(0)
    nd = tbl.shape[0]

    @pl.when(step == 0)
    def _():
        def one(i, carry):
            at = pl.multiple_of(i * LANES, LANES)
            rows = jnp.concatenate([src[r, :, pl.ds(at, LANES)].astype(jnp.float32) for r in order], axis=0)
            tbl[pl.ds(at, LANES), :] = rows.T
            return carry

        lax.fori_loop(0, nd // LANES, one, 0, unroll=2)

    def some(i, carry):
        at = pl.multiple_of(i * 64, 64)
        for q in range(64):
            buf[pl.ds(at + q, 1), :] = tbl[pl.ds(idx[step * chunk + at + q], 1), :]
        return carry

    lax.fori_loop(0, chunk // 64, some, 0)
    for s in range(nout):
        @pl.when(step // per_out == s)
        def _():
            outs[s][...] = buf[...].astype(jnp.bfloat16)


def pick_far(idx, src, order):
    nrow, half, nd = src.shape
    nout, n = idx.shape
    chunk = min(n, 1024)
    per_out = n // chunk

    def place(s):
        return lambda i, c: (jnp.clip(i - s * per_out, 0, per_out - 1), 0)

    return pl.pallas_call(
        functools.partial(
            pick_far_kernel, nout=nout, order=order, half=half, chunk=chunk, per_out=per_out
        ),
        out_shape=[jax.ShapeDtypeStruct((n, LANES), jnp.bfloat16) for _ in range(nout)],
        grid_spec=pltpu.PrefetchScalarGridSpec(
            num_scalar_prefetch=1,
            grid=(nout * per_out,),
            in_specs=[pl.BlockSpec((nrow, half, nd), lambda i, c: (0, 0, 0))],
            out_specs=[pl.BlockSpec((chunk, LANES), place(s)) for s in range(nout)],
            scratch_shapes=[pltpu.VMEM((nd, LANES), jnp.float32), pltpu.VMEM((chunk, LANES), jnp.float32)],
        ),
        compiler_params=pltpu.CompilerParams(
            dimension_semantics=("arbitrary",), vmem_limit_bytes=40 << 20
        ),
        name="pick_far",
    )(idx.reshape(-1), src)


def product_near_kernel(w_ref, near_hbm, o_ref, bt, near, sem, *, tper, nh, npair, parts):
    per = LANES // tper
    nk = bt.shape[0] // parts

    @pl.when(pl.program_id(0) == 0)
    def _():
        copy = pltpu.make_async_copy(near_hbm, near, sem.at[0])
        copy.start()
        copy.wait()
        step_rows = min(nk, 256)
        lane = lax.broadcasted_iota(jnp.int32, (step_rows, LANES), 1) // tper

        def arrange(i, carry):
            at = pl.multiple_of(i * step_rows, step_rows)
            for h in range(nh):
                got = [near[h * per + j, pl.ds(at, step_rows), :].astype(jnp.float32) for j in range(per)]
                for p in range(npair):
                    for kp in range(parts):
                        tile = None
                        for j in range(per):
                            shift = (tper * j - (kp * (LANES // parts) + tper * p)) % LANES
                            moved = pltpu.roll(got[j], shift, 1) if shift else got[j]
                            tile = moved if tile is None else jnp.where(lane == j, moved, tile)
                        col = (h * npair + p) * LANES
                        bt[pl.ds(kp * nk + at, step_rows), col:col + LANES] = tile.astype(jnp.bfloat16)
            return carry

        lax.fori_loop(0, nk // step_rows, arrange, 0)

    o_ref[...] = jnp.dot(w_ref[...], bt[...], preferred_element_type=jnp.float32).astype(jnp.bfloat16)


def product_near(w, near, ngroup, tper):
    m, k = w.shape
    nrow, nk, _ = near.shape
    nh = tper * nrow // LANES
    npair = ngroup // 2
    cols = nh * npair * LANES
    mb = 512
    return pl.pallas_call(
        functools.partial(product_near_kernel, tper=tper, nh=nh, npair=npair, parts=k // nk),
        out_shape=jax.ShapeDtypeStruct((m, cols), jnp.bfloat16),
        grid=(m // mb,),
        in_specs=[pl.BlockSpec((mb, k), lambda i: (i, 0)), pl.BlockSpec(memory_space=pl.ANY)],
        out_specs=pl.BlockSpec((mb, cols), lambda i: (i, 0)),
        scratch_shapes=[
            pltpu.VMEM((k, cols), jnp.bfloat16),
            pltpu.VMEM(near.shape, jnp.bfloat16),
            pltpu.SemaphoreType.DMA((1,)),
        ],
        compiler_params=pltpu.CompilerParams(
            dimension_semantics=("arbitrary",), vmem_limit_bytes=56 << 20
        ),
        cost_estimate=pl.CostEstimate(flops=2 * m * k * cols, bytes_accessed=40 << 20, transcendentals=0),
        name="product_near",
    )(w, near)


def product_far_kernel(where, w_ref, near_ref, *refs, ngroup, nh, half):
    mine = refs[:ngroup]
    theirs = refs[ngroup:2 * ngroup]
    o_ref, bt, sem = refs[2 * ngroup:]
    group = where[0]
    core = where[1]
    npair = ngroup // 2
    rows = bt.shape[0] // 2

    @pl.when(pl.program_id(0) == 0)
    def _():
        copies = []
        for s in range(ngroup):
            cols = slice(s * LANES, (s + 1) * LANES)
            for d, ref in ((0, mine[s]), (1, theirs[s])):
                at = pl.multiple_of(jnp.where(core == d, 0, 1) * rows, rows)
                copies.append(pltpu.make_async_copy(ref, bt.at[pl.ds(at, rows), cols], sem.at[2 * s + d]))
        for c in copies:
            c.start()
        for c in copies:
            c.wait()

    res = jnp.dot(w_ref[...], bt[...], preferred_element_type=jnp.float32)
    slot = (lax.broadcasted_iota(jnp.int32, (res.shape[0], LANES), 1) // half) % 2
    for s in range(ngroup):
        far = res[:, s * LANES:(s + 1) * LANES]
        for h in range(nh):
            first = pltpu.roll(far, LANES - half * h, 1) if h else far
            at = (h * npair + s // 2) * LANES
            second = near_ref[:, at:at + LANES].astype(jnp.float32)
            if s % 2 == 0:
                second = pltpu.roll(second, half, 1)
            tile = jnp.where(slot == 0, first, second).astype(jnp.bfloat16)
            col = pl.multiple_of(((group ^ s) * nh + h) * LANES, LANES)
            o_ref[:, pl.ds(col, LANES)] = tile


def product_far(where, w, near, mine, theirs, half, snap):
    m, k = w.shape
    ngroup = len(mine)
    cols = near.shape[1]
    mb = 512
    return pl.pallas_call(
        functools.partial(product_far_kernel, ngroup=ngroup, nh=snap // (ngroup * LANES), half=half),
        out_shape=jax.ShapeDtypeStruct((m, snap), jnp.bfloat16),
        grid_spec=pltpu.PrefetchScalarGridSpec(
            num_scalar_prefetch=1,
            grid=(m // mb,),
            in_specs=[pl.BlockSpec((mb, k), lambda i, c: (i, 0)), pl.BlockSpec((mb, cols), lambda i, c: (i, 0))]
            + [pl.BlockSpec(memory_space=pl.ANY)] * (2 * ngroup),
            out_specs=pl.BlockSpec((mb, snap), lambda i, c: (i, 0)),
            scratch_shapes=[
                pltpu.VMEM((k, ngroup * LANES), jnp.bfloat16),
                pltpu.SemaphoreType.DMA((2 * ngroup,)),
            ],
        ),
        compiler_params=pltpu.CompilerParams(
            dimension_semantics=("arbitrary",), vmem_limit_bytes=56 << 20
        ),
        cost_estimate=pl.CostEstimate(flops=2 * m * k * cols, bytes_accessed=40 << 20, transcendentals=0),
        name="product_far",
    )(where, w, near, *mine, *theirs)


def body(snapshots, bnd_index, recovery, block_se, connect, stress_mat):
    ngroup = lax.axis_size("group")
    nrow = lax.axis_size("row")
    nse = bnd_index.shape[0] // ngroup
    nblk, blk, nb = recovery.shape
    nel, nc, ndof = stress_mat.shape
    tper = snapshots.shape[0]
    half = tper // 2
    snap = tper * ngroup * nrow
    group = lax.axis_index("group")
    core = lax.axis_index("row") % 2
    swap = lambda s: [(i, i ^ s) for i in range(ngroup)]
    other = [(i, i ^ 1) for i in range(nrow)]

    top = snapshots[:half]
    bottom = snapshots[half:]
    along_row = lax.all_gather(top, "row", axis=0, tiled=False)
    along_group = [bottom] + [lax.ppermute(bottom, "group", swap(s)) for s in range(1, ngroup)]

    ends = nrow - 1
    up = [(i, i + 1) for i in range(ends)]
    down = [(i + 1, i) for i in range(ends)]
    head = lax.ppermute(recovery[nblk - 1, blk - HW:], "row", up)
    tail = lax.ppermute(recovery[0, :HW], "row", down)
    head_se = lax.ppermute(block_se[-1:], "row", up)
    tail_se = lax.ppermute(block_se[:1], "row", down)
    se_all = jnp.concatenate([head_se, block_se, tail_se])

    ngrp = nel // SUB
    conn = connect.T.reshape(ndof, ngrp, SUB).transpose(1, 0, 2).reshape(ngrp, 1, ndof * SUB)
    smat = stress_mat.transpose(1, 2, 0).reshape(nc, ndof, ngrp, SUB).transpose(2, 0, 1, 3)
    smat = smat.reshape(ngrp, nc, ndof * SUB)
    flat = conn.reshape(-1)
    where = jnp.stack([group, core]).astype(jnp.int32)

    own_idx = lax.dynamic_slice_in_dim(bnd_index, group * nse, nse, 0).reshape(-1)
    rows = nse * nb // 2
    far_idx = jnp.stack([
        lax.dynamic_slice_in_dim(
            lax.dynamic_slice_in_dim(bnd_index, (group ^ s) * nse, nse, 0).reshape(-1), core * rows, rows, 0
        )
        for s in range(ngroup)
    ]).reshape(-1)

    own_idx, far_idx, flat, conn, smat, se_all, head, tail, where = lax.optimization_barrier(
        (own_idx, far_idx, flat, conn, smat, se_all, head, tail, where)
    )
    near = lax.all_gather(pick_near(own_idx, along_group), "row", axis=0, tiled=False)
    per = LANES // tper
    order = [per * h + j for j in range(per) for h in range(nrow // per)]
    far = pick_far(far_idx.reshape(ngroup, rows), along_row, order)
    mine = [far[0]] + [lax.ppermute(far[s], "group", swap(s)) for s in range(1, ngroup)]

    flat, mine[0] = lax.optimization_barrier((flat, mine[0]))
    w = combine(flat, se_all, conn, smat, recovery, head, tail, nse)
    *mine, w = lax.optimization_barrier((*mine, w))
    theirs = [lax.ppermute(x, "row", other) for x in mine]
    w = w.reshape(nc * nel, nse * nb)
    out = product_near(w, near, ngroup, tper)
    out = product_far(where, w, out, mine, theirs, half, snap)
    return out.reshape(nc, nel, snap).transpose(1, 0, 2)


def solution(mesh):
    in_specs = (
        P(("group", "row"), None),
        P(),
        P(("group", "row"), None, None),
        P(("group", "row")),
        P(("group", "row"), None),
        P(("group", "row"), None, None),
    )
    out_specs = P(("group", "row"), None, None)
    return jax.shard_map(body, mesh=mesh, in_specs=in_specs, out_specs=out_specs, check_vma=False)
```

```python
import functools

import jax
import jax.numpy as jnp
from jax import lax
from jax.experimental import pallas as pl
from jax.experimental.pallas import tpu as pltpu
from jax.sharding import PartitionSpec as P

HW = 256
SUB = 8
LANES = 128


def combine_kernel(conn, se, grow_ref, s_ref, rec_ref, head_ref, tail_ref, w_ref, tbl, g0, g1, g2, g3,
    *, nfill, blk, nlt, nse, nc, ndof, inner, ts, gs,
):
    step = pl.program_id(0)
    rows = SUB * ndof
    out_rows = SUB * nc
    steps = pl.num_programs(0) - nfill

    def fill(src, base, count):
        def one(i, carry):
            at = pl.multiple_of(i * 16, 16)
            for j in range(nlt):
                part = src[pl.ds(at, 16), j * LANES:(j + 1) * LANES].astype(jnp.float32)
                tbl[pl.ds((base + at) * ts + j, 16, stride=ts), :] = part
            return carry
        lax.fori_loop(0, count // 16, one, 0, unroll=4)

    def gather(group, dst):
        first = group * rows
        for q in range(rows):
            dst[pl.ds(q, nlt, stride=gs), :] = tbl[pl.ds(conn[first + q] * ts, nlt), :]

    own = (
        lax.broadcasted_iota(jnp.int32, (SUB, rows), 1) % SUB
        == lax.broadcasted_iota(jnp.int32, (SUB, rows), 0)
    )

    def left(i):
        where = (grow_ref[i] + (blk - HW)) // blk
        tag = jnp.zeros((1, rows), jnp.int32)
        for b in range(nfill + 2):
            tag = jnp.where(where == b, se[b], tag)
        tag = jnp.where(own, jnp.broadcast_to(tag, (SUB, rows)), -1)
        smat = s_ref[i].astype(jnp.float32)
        parts = []
        for s in range(nse):
            hit = tag == s
            for c in range(nc):
                parts.append(jnp.where(hit, jnp.broadcast_to(smat[c:c + 1], (SUB, rows)), 0.0))
        return jnp.concatenate(parts, axis=0).astype(jnp.bfloat16)

    def matmul(i, srcs):
        lhs = [left(i), left(i + 1)]
        at = pl.multiple_of(i * SUB, 2 * SUB)
        for j in range(0, nlt, 2):
            res = []
            for l, src in zip(lhs, srcs):
                rhs = jnp.concatenate(
                    [src[(j + d) * gs:(j + d) * gs + rows, :].astype(jnp.bfloat16) for d in range(2)], axis=1)
                res.append(jnp.dot(l, rhs, preferred_element_type=jnp.float32))
            for s in range(nse):
                col = (s * nlt + j) * LANES
                for c in range(nc):
                    r0 = (s * nc + c) * SUB
                    both = jnp.concatenate([r[r0:r0 + SUB] for r in res], axis=0)
                    w_ref[c, pl.ds(at, 2 * SUB), col:col + 2 * LANES] = both.astype(jnp.bfloat16)

    @pl.when(step < nfill)
    def _():
        fill(rec_ref.at[0], HW + step * blk, blk)

    @pl.when(step == 0)
    def _():
        fill(head_ref, 0, HW)
        fill(tail_ref, HW + nfill * blk, HW)

    @pl.when(step >= nfill)
    def _():
        base = (step - nfill) * inner
        last = steps * inner - 1

        @pl.when(step == nfill)
        def _():
            gather(0, g0)
            gather(1, g1)

        def four(i, carry):
            n = base + 4 * i
            gather(n + 2, g2)
            gather(n + 3, g3)
            matmul(4 * i, (g0, g1))
            gather(jnp.minimum(n + 4, last), g0)
            gather(jnp.minimum(n + 5, last), g1)
            matmul(4 * i + 2, (g2, g3))
            return carry
        lax.fori_loop(0, inner // 4, four, 0)


def combine(conn, se, grow, smat, recovery, head, tail, nse, part, inner=4):
    nblk, blk, nb = recovery.shape
    ngrp, _, rows = grow.shape
    nel = ngrp * SUB
    ndof = rows // SUB
    nc = smat.shape[1]
    width = nb // 2
    nlt = width // LANES
    steps = ngrp // inner
    ts = nlt + 1
    gs = rows + 1
    kern = functools.partial(
        combine_kernel, nfill=nblk, blk=blk, nlt=nlt, nse=nse, nc=nc, ndof=ndof, inner=inner, ts=ts, gs=gs
    )
    later = lambda i: jnp.maximum(i - nblk, 0)
    return pl.pallas_call(
        kern,
        out_shape=jax.ShapeDtypeStruct((nc, nel, nse * width), jnp.bfloat16),
        grid_spec=pltpu.PrefetchScalarGridSpec(
            num_scalar_prefetch=2,
            grid=(nblk + steps,),
            in_specs=[
                pl.BlockSpec((inner, 1, rows), lambda i, c, s: (later(i), 0, 0)),
                pl.BlockSpec((inner, nc, rows), lambda i, c, s: (later(i), 0, 0)),
                pl.BlockSpec((1, blk, width), lambda i, c, s: (jnp.minimum(i, nblk - 1), 0, part)),
                pl.BlockSpec((HW, width), lambda i, c, s: (0, part)),
                pl.BlockSpec((HW, width), lambda i, c, s: (0, part)),
            ],
            out_specs=pl.BlockSpec((nc, SUB * inner, nse * width), lambda i, c, s: (0, later(i), 0)),
            scratch_shapes=[
                pltpu.VMEM(((nblk * blk + 2 * HW) * ts, LANES), jnp.float32),
            ] + [pltpu.VMEM((gs * nlt, LANES), jnp.float32)] * 4,
        ),
        compiler_params=pltpu.CompilerParams(dimension_semantics=("arbitrary",), vmem_limit_bytes=40 << 20),
        cost_estimate=pl.CostEstimate(flops=15 * 10**9, bytes_accessed=60 << 20, transcendentals=0),
        name=f"combine_{part}",
    )(conn, se, grow, smat, recovery, head, tail)


def pick_near_kernel(idx, *refs, nsrc, half, parts, chunk):
    srcs = refs[:nsrc]
    o_ref, tbl = refs[nsrc:nsrc + 2]
    bufs = refs[nsrc + 2:]
    step = pl.program_id(0)
    nd = tbl.shape[0]
    total = chunk * pl.num_programs(0)

    @pl.when(step == 0)
    def _():
        def one(i, carry):
            at = pl.multiple_of(i * LANES, LANES)
            rows = jnp.concatenate([s[:, pl.ds(at, LANES)].astype(jnp.float32) for s in srcs] * parts, axis=0)
            tbl[pl.ds(at, LANES), :] = rows.T
            return carry

        lax.fori_loop(0, nd // LANES, one, 0, unroll=2)

    def some(i, carry):
        at = pl.multiple_of(i * 64, 64)
        for p in range(parts):
            for q in range(64):
                k = idx[p * total + step * chunk + at + q]
                bufs[p][pl.ds(at + q, 1), :] = tbl[pl.ds(k, 1), :]
        return carry

    lax.fori_loop(0, chunk // 64, some, 0)
    piece = lax.broadcasted_iota(jnp.int32, (chunk, LANES), 1) // (LANES // parts)
    out = bufs[0][...]
    for p in range(1, parts):
        out = jnp.where(piece == p, bufs[p][...], out)
    o_ref[...] = out.astype(jnp.bfloat16)


def pick_near(idx, srcs):
    half, nd = srcs[0].shape
    parts = LANES // (half * len(srcs))
    n = idx.shape[0] // parts
    chunk = min(n, 1024)
    return pl.pallas_call(
        functools.partial(pick_near_kernel, nsrc=len(srcs), half=half, parts=parts, chunk=chunk),
        out_shape=jax.ShapeDtypeStruct((n, LANES), jnp.bfloat16),
        grid_spec=pltpu.PrefetchScalarGridSpec(
            num_scalar_prefetch=1,
            grid=(n // chunk,),
            in_specs=[pl.BlockSpec((half, nd), lambda i, c: (0, 0)) for _ in srcs],
            out_specs=pl.BlockSpec((chunk, LANES), lambda i, c: (i, 0)),
            scratch_shapes=[pltpu.VMEM((nd, LANES), jnp.float32)]
            + [pltpu.VMEM((chunk, LANES), jnp.float32) for _ in range(parts)],
        ),
        compiler_params=pltpu.CompilerParams(
            dimension_semantics=("arbitrary",), vmem_limit_bytes=40 << 20
        ),
        name="pick_near",
    )(idx, *srcs)


def pick_far_kernel(idx, src, *refs, nout, order, half, chunk, per_out):
    outs = refs[:nout]
    tbl, buf = refs[nout:]
    step = pl.program_id(0)
    nd = tbl.shape[0]

    @pl.when(step == 0)
    def _():
        def one(i, carry):
            at = pl.multiple_of(i * LANES, LANES)
            rows = jnp.concatenate([src[r, :, pl.ds(at, LANES)].astype(jnp.float32) for r in order], axis=0)
            tbl[pl.ds(at, LANES), :] = rows.T
            return carry

        lax.fori_loop(0, nd // LANES, one, 0, unroll=2)

    def some(i, carry):
        at = pl.multiple_of(i * 64, 64)
        for q in range(64):
            buf[pl.ds(at + q, 1), :] = tbl[pl.ds(idx[step * chunk + at + q], 1), :]
        return carry

    lax.fori_loop(0, chunk // 64, some, 0)
    for s in range(nout):
        @pl.when(step // per_out == s)
        def _():
            outs[s][...] = buf[...].astype(jnp.bfloat16)


def pick_far(idx, src, order):
    nrow, half, nd = src.shape
    nout, n = idx.shape
    chunk = min(n, 1024)
    per_out = n // chunk

    def place(s):
        return lambda i, c: (jnp.clip(i - s * per_out, 0, per_out - 1), 0)

    return pl.pallas_call(
        functools.partial(
            pick_far_kernel, nout=nout, order=order, half=half, chunk=chunk, per_out=per_out
        ),
        out_shape=[jax.ShapeDtypeStruct((n, LANES), jnp.bfloat16) for _ in range(nout)],
        grid_spec=pltpu.PrefetchScalarGridSpec(
            num_scalar_prefetch=1,
            grid=(nout * per_out,),
            in_specs=[pl.BlockSpec((nrow, half, nd), lambda i, c: (0, 0, 0))],
            out_specs=[pl.BlockSpec((chunk, LANES), place(s)) for s in range(nout)],
            scratch_shapes=[pltpu.VMEM((nd, LANES), jnp.float32), pltpu.VMEM((chunk, LANES), jnp.float32)],
        ),
        compiler_params=pltpu.CompilerParams(
            dimension_semantics=("arbitrary",), vmem_limit_bytes=40 << 20
        ),
        name="pick_far",
    )(idx.reshape(-1), src)


def product_near_kernel(w0_ref, w1_ref, near_hbm, o_ref, bt, near, sem, *, tper, nh, npair, parts):
    per = LANES // tper
    nk = bt.shape[0] // parts

    @pl.when(pl.program_id(0) == 0)
    def _():
        copy = pltpu.make_async_copy(near_hbm, near, sem.at[0])
        copy.start()
        copy.wait()
        step_rows = min(nk, 256)
        lane = lax.broadcasted_iota(jnp.int32, (step_rows, LANES), 1) // tper

        def arrange(i, carry):
            at = pl.multiple_of(i * step_rows, step_rows)
            for h in range(nh):
                got = [near[h * per + j, pl.ds(at, step_rows), :].astype(jnp.float32) for j in range(per)]
                for p in range(npair):
                    for kp in range(parts):
                        tile = None
                        for j in range(per):
                            shift = (tper * j - (kp * (LANES // parts) + tper * p)) % LANES
                            moved = pltpu.roll(got[j], shift, 1) if shift else got[j]
                            tile = moved if tile is None else jnp.where(lane == j, moved, tile)
                        col = (h * npair + p) * LANES
                        bt[pl.ds(kp * nk + at, step_rows), col:col + LANES] = tile.astype(jnp.bfloat16)
            return carry

        lax.fori_loop(0, nk // step_rows, arrange, 0)

    k = w0_ref.shape[1]
    res = jnp.dot(w0_ref[...], bt[:k], preferred_element_type=jnp.float32)
    res = res + jnp.dot(w1_ref[...], bt[k:], preferred_element_type=jnp.float32)
    o_ref[...] = res.astype(jnp.bfloat16)


def product_near(w, near, ngroup, tper):
    m, k = w[0].shape
    k = 2 * k
    nrow, nk, _ = near.shape
    nh = tper * nrow // LANES
    npair = ngroup // 2
    cols = nh * npair * LANES
    mb = 512
    return pl.pallas_call(
        functools.partial(product_near_kernel, tper=tper, nh=nh, npair=npair, parts=k // nk),
        out_shape=jax.ShapeDtypeStruct((m, cols), jnp.bfloat16),
        grid=(m // mb,),
        in_specs=[pl.BlockSpec((mb, k // 2), lambda i: (i, 0))] * 2 + [pl.BlockSpec(memory_space=pl.ANY)],
        out_specs=pl.BlockSpec((mb, cols), lambda i: (i, 0)),
        scratch_shapes=[
            pltpu.VMEM((k, cols), jnp.bfloat16),
            pltpu.VMEM(near.shape, jnp.bfloat16),
            pltpu.SemaphoreType.DMA((1,)),
        ],
        compiler_params=pltpu.CompilerParams(
            dimension_semantics=("arbitrary",), vmem_limit_bytes=56 << 20
        ),
        cost_estimate=pl.CostEstimate(flops=2 * m * k * cols, bytes_accessed=40 << 20, transcendentals=0),
        name="product_near",
    )(*w, near)


def product_far_kernel(where, w0_ref, w1_ref, near_ref, *refs, ngroup, nh, half):
    mine = refs[:ngroup]
    theirs = refs[ngroup:2 * ngroup]
    o_ref, bt, sem = refs[2 * ngroup:]
    group = where[0]
    core = where[1]
    npair = ngroup // 2
    rows = bt.shape[0] // 2

    @pl.when(pl.program_id(0) == 0)
    def _():
        copies = []
        for s in range(ngroup):
            cols = slice(s * LANES, (s + 1) * LANES)
            for d, ref in ((0, mine[s]), (1, theirs[s])):
                at = pl.multiple_of(jnp.where(core == d, 0, 1) * rows, rows)
                copies.append(pltpu.make_async_copy(ref, bt.at[pl.ds(at, rows), cols], sem.at[2 * s + d]))
        for c in copies:
            c.start()
        for c in copies:
            c.wait()

    res = jnp.dot(w0_ref[...], bt[:rows], preferred_element_type=jnp.float32)
    res = res + jnp.dot(w1_ref[...], bt[rows:], preferred_element_type=jnp.float32)
    slot = (lax.broadcasted_iota(jnp.int32, (res.shape[0], LANES), 1) // half) % 2
    for s in range(ngroup):
        far = res[:, s * LANES:(s + 1) * LANES]
        for h in range(nh):
            first = pltpu.roll(far, LANES - half * h, 1) if h else far
            at = (h * npair + s // 2) * LANES
            second = near_ref[:, at:at + LANES].astype(jnp.float32)
            if s % 2 == 0:
                second = pltpu.roll(second, half, 1)
            tile = jnp.where(slot == 0, first, second).astype(jnp.bfloat16)
            col = pl.multiple_of(((group ^ s) * nh + h) * LANES, LANES)
            o_ref[:, pl.ds(col, LANES)] = tile


def product_far(where, w, near, mine, theirs, half, snap):
    m, k = w[0].shape
    k = 2 * k
    ngroup = len(mine)
    cols = near.shape[1]
    mb = 512
    return pl.pallas_call(
        functools.partial(product_far_kernel, ngroup=ngroup, nh=snap // (ngroup * LANES), half=half),
        out_shape=jax.ShapeDtypeStruct((m, snap), jnp.bfloat16),
        grid_spec=pltpu.PrefetchScalarGridSpec(
            num_scalar_prefetch=1,
            grid=(m // mb,),
            in_specs=[pl.BlockSpec((mb, k // 2), lambda i, c: (i, 0))] * 2
            + [pl.BlockSpec((mb, cols), lambda i, c: (i, 0))]
            + [pl.BlockSpec(memory_space=pl.ANY)] * (2 * ngroup),
            out_specs=pl.BlockSpec((mb, snap), lambda i, c: (i, 0)),
            scratch_shapes=[
                pltpu.VMEM((k, ngroup * LANES), jnp.bfloat16),
                pltpu.SemaphoreType.DMA((2 * ngroup,)),
            ],
        ),
        compiler_params=pltpu.CompilerParams(
            dimension_semantics=("arbitrary",), vmem_limit_bytes=56 << 20
        ),
        cost_estimate=pl.CostEstimate(flops=2 * m * k * cols, bytes_accessed=40 << 20, transcendentals=0),
        name="product_far",
    )(where, *w, near, *mine, *theirs)


def body(snapshots, bnd_index, recovery, block_se, connect, stress_mat):
    ngroup = lax.axis_size("group")
    nrow = lax.axis_size("row")
    nse = bnd_index.shape[0] // ngroup
    nblk, blk, nb = recovery.shape
    nel, nc, ndof = stress_mat.shape
    tper = snapshots.shape[0]
    half = tper // 2
    snap = tper * ngroup * nrow
    group = lax.axis_index("group")
    core = lax.axis_index("row") % 2
    swap = lambda s: [(i, i ^ s) for i in range(ngroup)]
    other = [(i, i ^ 1) for i in range(nrow)]

    top = snapshots[:half]
    bottom = snapshots[half:]
    along_row = lax.all_gather(top, "row", axis=0, tiled=False)
    along_group = [bottom] + [lax.ppermute(bottom, "group", swap(s)) for s in range(1, ngroup)]

    ends = nrow - 1
    up = [(i, i + 1) for i in range(ends)]
    down = [(i + 1, i) for i in range(ends)]
    head = lax.ppermute(recovery[nblk - 1, blk - HW:], "row", up)
    tail = lax.ppermute(recovery[0, :HW], "row", down)
    head_se = lax.ppermute(block_se[-1:], "row", up)
    tail_se = lax.ppermute(block_se[:1], "row", down)
    se_all = jnp.concatenate([head_se, block_se, tail_se])

    ngrp = nel // SUB
    conn = connect.T.reshape(ndof, ngrp, SUB).transpose(1, 0, 2).reshape(ngrp, 1, ndof * SUB)
    smat = stress_mat.transpose(1, 2, 0).reshape(nc, ndof, ngrp, SUB).transpose(2, 0, 1, 3)
    smat = smat.reshape(ngrp, nc, ndof * SUB)
    flat = conn.reshape(-1)
    where = jnp.stack([group, core]).astype(jnp.int32)

    parted = bnd_index.reshape(ngroup, nse, 2, nb // 2).transpose(0, 2, 1, 3)
    rows = nse * nb // 2
    own_idx = lax.dynamic_index_in_dim(parted, group, 0, keepdims=False).reshape(-1)
    mid = lax.dynamic_index_in_dim(parted, core, 1, keepdims=False).reshape(ngroup, rows)
    far_idx = jnp.concatenate([
        lax.dynamic_index_in_dim(mid, group ^ s, 0, keepdims=False) for s in range(ngroup)
    ])

    own_idx, far_idx, flat, conn, smat, where = lax.optimization_barrier(
        (own_idx, far_idx, flat, conn, smat, where)
    )
    picked = pick_near(own_idx, along_group)
    picked, flat, far_idx = lax.optimization_barrier((picked, flat, far_idx))
    near = lax.all_gather(picked, "row", axis=0, tiled=False)
    w0 = combine(flat, se_all, conn, smat, recovery, head, tail, nse, 0)
    w0, far_idx = lax.optimization_barrier((w0, far_idx))
    per = LANES // tper
    order = [per * h + j for j in range(per) for h in range(nrow // per)]
    far = pick_far(far_idx.reshape(ngroup, rows), along_row, order)
    mine = [far[0]] + [lax.ppermute(far[s], "group", swap(s)) for s in range(1, ngroup)]
    flat, mine[0] = lax.optimization_barrier((flat, mine[0]))
    w1 = combine(flat, se_all, conn, smat, recovery, head, tail, nse, 1)
    *mine, w1 = lax.optimization_barrier((*mine, w1))
    theirs = [lax.ppermute(x, "row", other) for x in mine]
    w = [x.reshape(nc * nel, -1) for x in (w0, w1)]
    out = product_near(w, near, ngroup, tper)
    out = product_far(where, w, out, mine, theirs, half, snap)
    return out.reshape(nc, nel, snap).transpose(1, 0, 2)


def solution(mesh):
    in_specs = (
        P(("group", "row"), None),
        P(),
        P(("group", "row"), None, None),
        P(("group", "row")),
        P(("group", "row"), None),
        P(("group", "row"), None, None),
    )
    out_specs = P(("group", "row"), None, None)
    return jax.shard_map(body, mesh=mesh, in_specs=in_specs, out_specs=out_specs, check_vma=False)
```

```python
import functools

import jax
import jax.numpy as jnp
from jax import lax
from jax.experimental import pallas as pl
from jax.experimental.pallas import tpu as pltpu
from jax.sharding import PartitionSpec as P

HW = 256
SUB = 8
LANES = 128


def combine_kernel(
    conn, se, grow_ref, s_ref, rec_hbm, head_ref, tail_ref, w_ref, tbl, buf, sem, g0, g1, g2, g3,
    *, nfill, blk, nlt, nse, nc, ndof, inner, ts, gs, nbuf
):
    step = pl.program_id(0)
    rows = SUB * ndof
    steps = pl.num_programs(0) - nfill

    def fetch(b):
        return pltpu.make_async_copy(rec_hbm.at[b], buf.at[b % nbuf], sem.at[b % nbuf])

    def fill(src, base, count):
        def one(i, carry):
            at = pl.multiple_of(i * 16, 16)
            for j in range(nlt):
                part = src[pl.ds(at, 16), j * LANES:(j + 1) * LANES].astype(jnp.float32)
                tbl[pl.ds((base + at) * ts + j, 16, stride=ts), :] = part
            return carry

        lax.fori_loop(0, count // 16, one, 0, unroll=4)

    def gather(group, dst, lo=0, hi=rows):
        first = group * rows
        for q in range(lo, hi):
            dst[pl.ds(q, nlt, stride=gs), :] = tbl[pl.ds(conn[first + q], nlt), :]

    own = (
        lax.broadcasted_iota(jnp.int32, (SUB, rows), 1) % SUB
        == lax.broadcasted_iota(jnp.int32, (SUB, rows), 0)
    )

    def left(i):
        where = (grow_ref[i] + (blk - HW)) // blk
        tag = jnp.zeros((1, rows), jnp.int32)
        for b in range(nfill + 2):
            tag = jnp.where(where == b, se[b], tag)
        tag = jnp.where(own, jnp.broadcast_to(tag, (SUB, rows)), -1)
        smat = s_ref[i].astype(jnp.float32)
        parts = []
        for s in range(nse):
            hit = tag == s
            for c in range(nc):
                parts.append(jnp.where(hit, jnp.broadcast_to(smat[c:c + 1], (SUB, rows)), 0.0))
        return jnp.concatenate(parts, axis=0).astype(jnp.bfloat16)

    def matmul(i, srcs, nxt, dsts):
        lhs = [left(i), left(i + 1)]
        at = pl.multiple_of(i * SUB, 2 * SUB)
        for j in range(0, nlt, 2):
            res = []
            for t in range(2):
                src = srcs[t]
                rhs = jnp.concatenate(
                    [src[(j + d) * gs:(j + d) * gs + rows, :].astype(jnp.bfloat16) for d in range(2)], axis=1
                )
                res.append(jnp.dot(lhs[t], rhs, preferred_element_type=jnp.float32))
                gather(nxt + t, dsts[t], rows * j // nlt, rows * (j + 2) // nlt)
            for s in range(nse):
                col = (s * nlt + j) * LANES
                for c in range(nc):
                    r0 = (s * nc + c) * SUB
                    both = jnp.concatenate([r[r0:r0 + SUB] for r in res], axis=0)
                    w_ref[c, pl.ds(at, 2 * SUB), col:col + 2 * LANES] = both.astype(jnp.bfloat16)

    @pl.when(step == 0)
    def _():
        for b in range(nbuf):
            fetch(b).start()
        fill(head_ref, 0, HW)
        fill(tail_ref, HW + nfill * blk, HW)

    @pl.when(step < nfill)
    def _():
        fetch(step).wait()
        fill(buf.at[step % nbuf], HW + step * blk, blk)

        @pl.when(step + nbuf < nfill)
        def _():
            fetch(step + nbuf).start()

    @pl.when(step >= nfill)
    def _():
        base = (step - nfill) * inner
        last = steps * inner - 2

        @pl.when(step == nfill)
        def _():
            gather(0, g0)
            gather(1, g1)

        def four(i, carry):
            n = base + 4 * i
            matmul(4 * i, (g0, g1), n + 2, (g2, g3))
            matmul(4 * i + 2, (g2, g3), jnp.minimum(n + 4, last), (g0, g1))
            return carry

        lax.fori_loop(0, inner // 4, four, 0)


def combine(conn, se, grow, smat, recovery, head, tail, nse, inner=4, nbuf=6):
    nblk, blk, nb = recovery.shape
    ngrp, _, rows = grow.shape
    nel = ngrp * SUB
    ndof = rows // SUB
    nc = smat.shape[1]
    nlt = nb // LANES
    steps = ngrp // inner
    ts = nlt + 1
    gs = rows + 1
    kern = functools.partial(
        combine_kernel, nfill=nblk, blk=blk, nlt=nlt, nse=nse, nc=nc, ndof=ndof, inner=inner, ts=ts, gs=gs,
        nbuf=nbuf,
    )
    later = lambda i: jnp.maximum(i - nblk, 0)
    return pl.pallas_call(
        kern,
        out_shape=jax.ShapeDtypeStruct((nc, nel, nse * nb), jnp.bfloat16),
        grid_spec=pltpu.PrefetchScalarGridSpec(
            num_scalar_prefetch=2,
            grid=(nblk + steps,),
            in_specs=[
                pl.BlockSpec((inner, 1, rows), lambda i, c, s: (later(i), 0, 0)),
                pl.BlockSpec((inner, nc, rows), lambda i, c, s: (later(i), 0, 0)),
                pl.BlockSpec(memory_space=pl.ANY),
                pl.BlockSpec((HW, nb), lambda i, c, s: (0, 0)),
                pl.BlockSpec((HW, nb), lambda i, c, s: (0, 0)),
            ],
            out_specs=pl.BlockSpec((nc, SUB * inner, nse * nb), lambda i, c, s: (0, later(i), 0)),
            scratch_shapes=[
                pltpu.VMEM(((nblk * blk + 2 * HW) * ts, LANES), jnp.float32),
                pltpu.VMEM((nbuf, blk, nb), jnp.bfloat16),
                pltpu.SemaphoreType.DMA((nbuf,)),
            ] + [pltpu.VMEM((gs * nlt, LANES), jnp.float32)] * 4,
        ),
        compiler_params=pltpu.CompilerParams(dimension_semantics=("arbitrary",), vmem_limit_bytes=60 << 20),
        cost_estimate=pl.CostEstimate(flops=30 * 10**9, bytes_accessed=120 << 20, transcendentals=0),
        name="combine",
    )(conn, se, grow, smat, recovery, head, tail)


def pick_near_kernel(idx, *refs, nsrc, half, parts, chunk):
    srcs = refs[:nsrc]
    o_ref, tbl = refs[nsrc:nsrc + 2]
    bufs = refs[nsrc + 2:]
    step = pl.program_id(0)
    nd = tbl.shape[0]
    total = chunk * pl.num_programs(0)

    @pl.when(step == 0)
    def _():
        def one(i, carry):
            at = pl.multiple_of(i * LANES, LANES)
            rows = jnp.concatenate([s[:, pl.ds(at, LANES)].astype(jnp.float32) for s in srcs] * parts, axis=0)
            tbl[pl.ds(at, LANES), :] = rows.T
            return carry

        lax.fori_loop(0, nd // LANES, one, 0, unroll=2)

    def some(i, carry):
        at = pl.multiple_of(i * 64, 64)
        for p in range(parts):
            for q in range(64):
                k = idx[p * total + step * chunk + at + q]
                bufs[p][pl.ds(at + q, 1), :] = tbl[pl.ds(k, 1), :]
        return carry

    lax.fori_loop(0, chunk // 64, some, 0)
    piece = lax.broadcasted_iota(jnp.int32, (chunk, LANES), 1) // (LANES // parts)
    out = bufs[0][...]
    for p in range(1, parts):
        out = jnp.where(piece == p, bufs[p][...], out)
    o_ref[...] = out.astype(jnp.bfloat16)


def pick_near(idx, srcs):
    half, nd = srcs[0].shape
    parts = LANES // (half * len(srcs))
    n = idx.shape[0] // parts
    chunk = min(n, 1024)
    return pl.pallas_call(
        functools.partial(pick_near_kernel, nsrc=len(srcs), half=half, parts=parts, chunk=chunk),
        out_shape=jax.ShapeDtypeStruct((n, LANES), jnp.bfloat16),
        grid_spec=pltpu.PrefetchScalarGridSpec(
            num_scalar_prefetch=1,
            grid=(n // chunk,),
            in_specs=[pl.BlockSpec((half, nd), lambda i, c: (0, 0)) for _ in srcs],
            out_specs=pl.BlockSpec((chunk, LANES), lambda i, c: (i, 0)),
            scratch_shapes=[pltpu.VMEM((nd, LANES), jnp.float32)]
            + [pltpu.VMEM((chunk, LANES), jnp.float32) for _ in range(parts)],
        ),
        compiler_params=pltpu.CompilerParams(
            dimension_semantics=("arbitrary",), vmem_limit_bytes=40 << 20
        ),
        name="pick_near",
    )(idx, *srcs)


def pick_far_kernel(idx, src, *refs, nout, order, half, chunk, per_out):
    outs = refs[:nout]
    tbl, buf = refs[nout:]
    step = pl.program_id(0)
    nd = tbl.shape[0]

    @pl.when(step == 0)
    def _():
        def one(i, carry):
            at = pl.multiple_of(i * LANES, LANES)
            rows = jnp.concatenate([src[r, :, pl.ds(at, LANES)].astype(jnp.float32) for r in order], axis=0)
            tbl[pl.ds(at, LANES), :] = rows.T
            return carry

        lax.fori_loop(0, nd // LANES, one, 0, unroll=2)

    def some(i, carry):
        at = pl.multiple_of(i * 64, 64)
        for q in range(64):
            buf[pl.ds(at + q, 1), :] = tbl[pl.ds(idx[step * chunk + at + q], 1), :]
        return carry

    lax.fori_loop(0, chunk // 64, some, 0)
    for s in range(nout):
        @pl.when(step // per_out == s)
        def _():
            outs[s][...] = buf[...].astype(jnp.bfloat16)


def pick_far(idx, src, order):
    nrow, half, nd = src.shape
    nout, n = idx.shape
    chunk = min(n, 1024)
    per_out = n // chunk

    def place(s):
        return lambda i, c: (jnp.clip(i - s * per_out, 0, per_out - 1), 0)

    return pl.pallas_call(
        functools.partial(
            pick_far_kernel, nout=nout, order=order, half=half, chunk=chunk, per_out=per_out
        ),
        out_shape=[jax.ShapeDtypeStruct((n, LANES), jnp.bfloat16) for _ in range(nout)],
        grid_spec=pltpu.PrefetchScalarGridSpec(
            num_scalar_prefetch=1,
            grid=(nout * per_out,),
            in_specs=[pl.BlockSpec((nrow, half, nd), lambda i, c: (0, 0, 0))],
            out_specs=[pl.BlockSpec((chunk, LANES), place(s)) for s in range(nout)],
            scratch_shapes=[pltpu.VMEM((nd, LANES), jnp.float32), pltpu.VMEM((chunk, LANES), jnp.float32)],
        ),
        compiler_params=pltpu.CompilerParams(
            dimension_semantics=("arbitrary",), vmem_limit_bytes=40 << 20
        ),
        name="pick_far",
    )(idx.reshape(-1), src)


def product_kernel(
    where, w_ref, *refs, ngroup, nrow, tper, half, parts
):
    mine = refs[:ngroup]
    theirs = refs[ngroup:2 * ngroup]
    near_hbm, o_ref, bt, near, sem = refs[2 * ngroup:]
    group = where[0]
    core = where[1]
    nh = tper * nrow // LANES
    per = LANES // tper
    npair = ngroup * half // tper
    rows = bt.shape[0] // 2
    nk = bt.shape[0] // parts

    @pl.when(pl.program_id(0) == 0)
    def _():
        last = pltpu.make_async_copy(near_hbm, near, sem.at[2 * ngroup])
        last.start()
        copies = []
        for s in range(ngroup):
            cols = slice(s * LANES, (s + 1) * LANES)
            for d, ref in ((0, mine[s]), (1, theirs[s])):
                at = pl.multiple_of(jnp.where(core == d, 0, 1) * rows, rows)
                copies.append(pltpu.make_async_copy(ref, bt.at[pl.ds(at, rows), cols], sem.at[2 * s + d]))
        for c in copies:
            c.start()
        last.wait()
        step_rows = min(nk, 128)
        lane = lax.broadcasted_iota(jnp.int32, (step_rows, LANES), 1) // tper

        def arrange(i, carry):
            at = pl.multiple_of(i * step_rows, step_rows)
            for h in range(nh):
                got = [near[h * per + j, pl.ds(at, step_rows), :].astype(jnp.float32) for j in range(per)]
                for p in range(npair):
                    for kp in range(parts):
                        tile = None
                        for j in range(per):
                            shift = (tper * j - (kp * (LANES // parts) + tper * p)) % LANES
                            moved = pltpu.roll(got[j], shift, 1) if shift else got[j]
                            tile = moved if tile is None else jnp.where(lane == j, moved, tile)
                        col = (ngroup + h * npair + p) * LANES
                        bt[pl.ds(kp * nk + at, step_rows), col:col + LANES] = tile.astype(jnp.bfloat16)
            return carry

        lax.fori_loop(0, nk // step_rows, arrange, 0)
        for c in copies:
            c.wait()

    res = jnp.dot(w_ref[...], bt[...], preferred_element_type=jnp.float32)
    slot = (lax.broadcasted_iota(jnp.int32, (res.shape[0], LANES), 1) // half) % 2
    for s in range(ngroup):
        far = res[:, s * LANES:(s + 1) * LANES]
        for h in range(nh):
            first = pltpu.roll(far, LANES - half * h, 1) if h else far
            at = (ngroup + h * npair + s // 2) * LANES
            second = res[:, at:at + LANES]
            if s % 2 == 0:
                second = pltpu.roll(second, half, 1)
            tile = jnp.where(slot == 0, first, second).astype(jnp.bfloat16)
            col = pl.multiple_of(((group ^ s) * nh + h) * LANES, LANES)
            o_ref[:, pl.ds(col, LANES)] = tile


def product(where, w, mine, theirs, near, tper, snap):
    m, k = w.shape
    ngroup = len(mine)
    nrow, nk, _ = near.shape
    mb = 256
    return pl.pallas_call(
        functools.partial(
            product_kernel, ngroup=ngroup, nrow=nrow, tper=tper, half=tper // 2, parts=k // nk
        ),
        out_shape=jax.ShapeDtypeStruct((m, snap), jnp.bfloat16),
        grid_spec=pltpu.PrefetchScalarGridSpec(
            num_scalar_prefetch=1,
            grid=(m // mb,),
            in_specs=[pl.BlockSpec((mb, k), lambda i, c: (i, 0))]
            + [pl.BlockSpec(memory_space=pl.ANY)] * (2 * ngroup + 1),
            out_specs=pl.BlockSpec((mb, snap), lambda i, c: (i, 0)),
            scratch_shapes=[
                pltpu.VMEM((k, snap), jnp.bfloat16),
                pltpu.VMEM(near.shape, jnp.bfloat16),
                pltpu.SemaphoreType.DMA((2 * ngroup + 1,)),
            ],
        ),
        compiler_params=pltpu.CompilerParams(
            dimension_semantics=("arbitrary",), vmem_limit_bytes=56 << 20
        ),
        name="product",
    )(where, w, *mine, *theirs, near)


def body(snapshots, bnd_index, recovery, block_se, connect, stress_mat):
    ngroup = lax.axis_size("group")
    nrow = lax.axis_size("row")
    nse = bnd_index.shape[0] // ngroup
    nblk, blk, nb = recovery.shape
    nel, nc, ndof = stress_mat.shape
    tper = snapshots.shape[0]
    half = tper // 2
    snap = tper * ngroup * nrow
    group = lax.axis_index("group")
    core = lax.axis_index("row") % 2
    swap = lambda s: [(i, i ^ s) for i in range(ngroup)]
    other = [(i, i ^ 1) for i in range(nrow)]

    top = snapshots[:half]
    bottom = snapshots[half:]
    along_row = lax.all_gather(top, "row", axis=0, tiled=False)
    along_group = [bottom] + [lax.ppermute(bottom, "group", swap(s)) for s in range(1, ngroup)]

    ends = nrow - 1
    up = [(i, i + 1) for i in range(ends)]
    down = [(i + 1, i) for i in range(ends)]
    head = lax.ppermute(recovery[nblk - 1, blk - HW:], "row", up)
    tail = lax.ppermute(recovery[0, :HW], "row", down)
    head_se = lax.ppermute(block_se[-1:], "row", up)
    tail_se = lax.ppermute(block_se[:1], "row", down)
    se_all = jnp.concatenate([head_se, block_se, tail_se])

    ngrp = nel // SUB
    conn = connect.T.reshape(ndof, ngrp, SUB).transpose(1, 0, 2).reshape(ngrp, 1, ndof * SUB)
    smat = stress_mat.transpose(1, 2, 0).reshape(nc, ndof, ngrp, SUB).transpose(2, 0, 1, 3)
    smat = smat.reshape(ngrp, nc, ndof * SUB)
    flat = conn.reshape(-1) * (nb // LANES + 1)
    where = jnp.stack([group, core]).astype(jnp.int32)

    rows = nse * nb // 2
    parted = bnd_index.reshape(ngroup, 2, rows)
    own_idx = lax.dynamic_index_in_dim(parted, group, 0, keepdims=False).reshape(-1)
    mid = lax.dynamic_index_in_dim(parted, core, 1, keepdims=False)
    far_idx = jnp.concatenate([
        lax.dynamic_index_in_dim(mid, group ^ s, 0, keepdims=False) for s in range(ngroup)
    ])

    own_idx, far_idx, flat, conn, smat, where = lax.optimization_barrier(
        (own_idx, far_idx, flat, conn, smat, where)
    )
    picked = pick_near(own_idx, along_group)
    picked, far_idx = lax.optimization_barrier((picked, far_idx))
    near = lax.all_gather(picked, "row", axis=0, tiled=False)
    per = LANES // tper
    order = [per * h + j for j in range(per) for h in range(nrow // per)]
    far = pick_far(far_idx.reshape(ngroup, rows), along_row, order)
    mine = [far[0]] + [lax.ppermute(far[s], "group", swap(s)) for s in range(1, ngroup)]
    flat, mine[0] = lax.optimization_barrier((flat, mine[0]))
    w = combine(flat, se_all, conn, smat, recovery, head, tail, nse)
    *mine, w = lax.optimization_barrier((*mine, w))
    theirs = [lax.ppermute(x, "row", other) for x in mine]
    out = product(where, w.reshape(nc * nel, nse * nb), mine, theirs, near, tper, snap)
    return out.reshape(nc, nel, snap).transpose(1, 0, 2)


def solution(mesh):
    in_specs = (
        P(("group", "row"), None),
        P(),
        P(("group", "row"), None, None),
        P(("group", "row")),
        P(("group", "row"), None),
        P(("group", "row"), None, None),
    )
    out_specs = P(("group", "row"), None, None)
    return jax.shard_map(body, mesh=mesh, in_specs=in_specs, out_specs=out_specs, check_vma=False)
```

```python
import functools

import jax
import jax.numpy as jnp
from jax import lax
from jax.experimental import pallas as pl
from jax.experimental.pallas import tpu as pltpu
from jax.sharding import PartitionSpec as P

HW = 256
SUB = 8
LANES = 128


def combine_kernel(
    conn, se, grow_ref, s_ref, rec_hbm, head_ref, tail_ref, w_ref, tbl, buf, sem, g0, g1, g2, g3,
    *, nfill, blk, nlt, nse, nc, ndof, inner, ts, gs, nbuf
):
    step = pl.program_id(0)
    rows = SUB * ndof
    steps = pl.num_programs(0) - nfill

    def fetch(b):
        return pltpu.make_async_copy(rec_hbm.at[b], buf.at[b % nbuf], sem.at[b % nbuf])

    def fill(src, base, count):
        def one(i, carry):
            at = pl.multiple_of(i * 16, 16)
            for j in range(nlt):
                part = src[pl.ds(at, 16), j * LANES:(j + 1) * LANES].astype(jnp.float32)
                tbl[pl.ds((base + at) * ts + j, 16, stride=ts), :] = part
            return carry

        lax.fori_loop(0, count // 16, one, 0, unroll=4)

    def gather(group, dst, lo=0, hi=rows):
        first = group * rows
        for q in range(lo, hi):
            dst[pl.ds(q, nlt, stride=gs), :] = tbl[pl.ds(conn[first + q], nlt), :]

    own = (
        lax.broadcasted_iota(jnp.int32, (SUB, rows), 1) % SUB
        == lax.broadcasted_iota(jnp.int32, (SUB, rows), 0)
    )

    def halo_tag(ref):
        wide = -(-rows // LANES) * LANES
        return ref[HW:HW + 16, :wide].astype(jnp.float32)[:1, :rows].astype(jnp.int32)

    head_tag = halo_tag(head_ref)
    tail_tag = halo_tag(tail_ref)

    def left(i):
        where = (grow_ref[pl.ds(i, 1), :] + (blk - HW)) // blk
        tag = jnp.where(where == 0, head_tag, tail_tag)
        for b in range(nfill):
            tag = jnp.where(where == b + 1, se[b], tag)
        tag = jnp.where(own, jnp.broadcast_to(tag, (SUB, rows)), -1)
        parts = []
        for s in range(nse):
            hit = tag == s
            for c in range(nc):
                parts.append(jnp.where(hit, jnp.broadcast_to(s_ref[c, pl.ds(i, 1), :], (SUB, rows)), 0.0))
        return jnp.concatenate(parts, axis=0).astype(jnp.bfloat16)

    def matmul(first, i, srcs, nxt, dsts):
        lhs = [left(first + i), left(first + i + 1)]
        at = pl.multiple_of(i * SUB, 2 * SUB)
        for j in range(0, nlt, 2):
            res = []
            for t in range(2):
                src = srcs[t]
                rhs = jnp.concatenate(
                    [src[(j + d) * gs:(j + d) * gs + rows, :].astype(jnp.bfloat16) for d in range(2)], axis=1
                )
                res.append(jnp.dot(lhs[t], rhs, preferred_element_type=jnp.float32))
                gather(nxt + t, dsts[t], rows * j // nlt, rows * (j + 2) // nlt)
            for s in range(nse):
                col = (s * nlt + j) * LANES
                for c in range(nc):
                    r0 = (s * nc + c) * SUB
                    both = jnp.concatenate([r[r0:r0 + SUB] for r in res], axis=0)
                    w_ref[c, pl.ds(at, 2 * SUB), col:col + 2 * LANES] = both.astype(jnp.bfloat16)

    @pl.when(step == 0)
    def _():
        for b in range(nbuf):
            fetch(b).start()
        fill(head_ref, 0, HW)
        fill(tail_ref, HW + nfill * blk, HW)

    @pl.when(step < nfill)
    def _():
        fetch(step).wait()
        fill(buf.at[step % nbuf], HW + step * blk, blk)

        @pl.when(step + nbuf < nfill)
        def _():
            fetch(step + nbuf).start()

    @pl.when(step >= nfill)
    def _():
        base = (step - nfill) * inner
        last = steps * inner - 2

        @pl.when(step == nfill)
        def _():
            gather(0, g0)
            gather(1, g1)

        def four(i, carry):
            n = base + 4 * i
            matmul(base, 4 * i, (g0, g1), n + 2, (g2, g3))
            matmul(base, 4 * i + 2, (g2, g3), jnp.minimum(n + 4, last), (g0, g1))
            return carry

        lax.fori_loop(0, inner // 4, four, 0)


def combine(conn, se, grow, smat, recovery, head, tail, nse, inner=4, nbuf=6):
    nblk, blk, nb = recovery.shape
    ngrp, rows = grow.shape
    nel = ngrp * SUB
    ndof = rows // SUB
    nc = smat.shape[0]
    nlt = nb // LANES
    steps = ngrp // inner
    ts = nlt + 1
    gs = rows + 1
    kern = functools.partial(
        combine_kernel, nfill=nblk, blk=blk, nlt=nlt, nse=nse, nc=nc, ndof=ndof, inner=inner, ts=ts, gs=gs,
        nbuf=nbuf,
    )
    later = lambda i: jnp.maximum(i - nblk, 0)
    return pl.pallas_call(
        kern,
        out_shape=jax.ShapeDtypeStruct((nc, nel, nse * nb), jnp.bfloat16),
        grid_spec=pltpu.PrefetchScalarGridSpec(
            num_scalar_prefetch=2,
            grid=(nblk + steps,),
            in_specs=[
                pl.BlockSpec((ngrp, rows), lambda i, c, s: (0, 0)),
                pl.BlockSpec((nc, ngrp, rows), lambda i, c, s: (0, 0, 0)),
                pl.BlockSpec(memory_space=pl.ANY),
                pl.BlockSpec((HW + 16, nb), lambda i, c, s: (0, 0)),
                pl.BlockSpec((HW + 16, nb), lambda i, c, s: (0, 0)),
            ],
            out_specs=pl.BlockSpec((nc, SUB * inner, nse * nb), lambda i, c, s: (0, later(i), 0)),
            scratch_shapes=[
                pltpu.VMEM(((nblk * blk + 2 * HW) * ts, LANES), jnp.float32),
                pltpu.VMEM((nbuf, blk, nb), jnp.bfloat16),
                pltpu.SemaphoreType.DMA((nbuf,)),
            ] + [pltpu.VMEM((gs * nlt, LANES), jnp.float32)] * 4,
        ),
        compiler_params=pltpu.CompilerParams(dimension_semantics=("arbitrary",), vmem_limit_bytes=60 << 20),
        cost_estimate=pl.CostEstimate(flops=30 * 10**9, bytes_accessed=120 << 20, transcendentals=0),
        name="combine",
    )(conn, se, grow, smat, recovery, head, tail)


def pick_near_kernel(idx, *refs, nsrc, half, parts, chunk):
    srcs = refs[:nsrc]
    o_ref, tbl = refs[nsrc:nsrc + 2]
    bufs = refs[nsrc + 2:]
    step = pl.program_id(0)
    nd = tbl.shape[0]
    total = chunk * pl.num_programs(0)

    @pl.when(step == 0)
    def _():
        def one(i, carry):
            at = pl.multiple_of(i * LANES, LANES)
            rows = jnp.concatenate([s[:, pl.ds(at, LANES)] for s in srcs] * parts, axis=0)
            tbl[pl.ds(at, LANES), :] = rows.T.astype(jnp.float32)
            return carry

        lax.fori_loop(0, nd // LANES, one, 0, unroll=2)

    def some(i, carry):
        at = pl.multiple_of(i * 64, 64)
        for p in range(parts):
            for q in range(64):
                k = idx[p * total + step * chunk + at + q]
                bufs[p][pl.ds(at + q, 1), :] = tbl[pl.ds(k, 1), :]
        return carry

    lax.fori_loop(0, chunk // 64, some, 0)
    piece = lax.broadcasted_iota(jnp.int32, (chunk, LANES), 1) // (LANES // parts)
    out = bufs[0][...]
    for p in range(1, parts):
        out = jnp.where(piece == p, bufs[p][...], out)
    o_ref[...] = out.astype(jnp.bfloat16)


def pick_near(idx, srcs):
    half, nd = srcs[0].shape
    parts = LANES // (half * len(srcs))
    n = idx.shape[0] // parts
    chunk = min(n, 1024)
    return pl.pallas_call(
        functools.partial(pick_near_kernel, nsrc=len(srcs), half=half, parts=parts, chunk=chunk),
        out_shape=jax.ShapeDtypeStruct((n, LANES), jnp.bfloat16),
        grid_spec=pltpu.PrefetchScalarGridSpec(
            num_scalar_prefetch=1,
            grid=(n // chunk,),
            in_specs=[pl.BlockSpec((half, nd), lambda i, c: (0, 0)) for _ in srcs],
            out_specs=pl.BlockSpec((chunk, LANES), lambda i, c: (i, 0)),
            scratch_shapes=[pltpu.VMEM((nd, LANES), jnp.float32)]
            + [pltpu.VMEM((chunk, LANES), jnp.float32) for _ in range(parts)],
        ),
        compiler_params=pltpu.CompilerParams(
            dimension_semantics=("arbitrary",), vmem_limit_bytes=40 << 20
        ),
        name="pick_near",
    )(idx, *srcs)


def pick_far_kernel(idx, src, *refs, nout, order, half, chunk, per_out):
    outs = refs[:nout]
    tbl, buf = refs[nout:]
    step = pl.program_id(0)
    nd = tbl.shape[0]

    @pl.when(step == 0)
    def _():
        def one(i, carry):
            at = pl.multiple_of(i * LANES, LANES)
            rows = jnp.concatenate([src[r, :, pl.ds(at, LANES)] for r in order], axis=0)
            tbl[pl.ds(at, LANES), :] = rows.T.astype(jnp.float32)
            return carry

        lax.fori_loop(0, nd // LANES, one, 0, unroll=2)

    def some(i, carry):
        at = pl.multiple_of(i * 64, 64)
        for q in range(64):
            buf[pl.ds(at + q, 1), :] = tbl[pl.ds(idx[step * chunk + at + q], 1), :]
        return carry

    lax.fori_loop(0, chunk // 64, some, 0)
    for s in range(nout):
        @pl.when(step // per_out == s)
        def _():
            outs[s][...] = buf[...].astype(jnp.bfloat16)


def pick_far(idx, src, order):
    nrow, half, nd = src.shape
    nout, n = idx.shape
    chunk = min(n, 1024)
    per_out = n // chunk

    def place(s):
        return lambda i, c: (jnp.clip(i - s * per_out, 0, per_out - 1), 0)

    return pl.pallas_call(
        functools.partial(
            pick_far_kernel, nout=nout, order=order, half=half, chunk=chunk, per_out=per_out
        ),
        out_shape=[jax.ShapeDtypeStruct((n, LANES), jnp.bfloat16) for _ in range(nout)],
        grid_spec=pltpu.PrefetchScalarGridSpec(
            num_scalar_prefetch=1,
            grid=(nout * per_out,),
            in_specs=[pl.BlockSpec((nrow, half, nd), lambda i, c: (0, 0, 0))],
            out_specs=[pl.BlockSpec((chunk, LANES), place(s)) for s in range(nout)],
            scratch_shapes=[pltpu.VMEM((nd, LANES), jnp.float32), pltpu.VMEM((chunk, LANES), jnp.float32)],
        ),
        compiler_params=pltpu.CompilerParams(
            dimension_semantics=("arbitrary",), vmem_limit_bytes=40 << 20
        ),
        name="pick_far",
    )(idx.reshape(-1), src)


def arrange_kernel(near, o_ref, *, nh, per, npair, parts, tper):
    step_rows = near.shape[1]
    lane = lax.broadcasted_iota(jnp.int32, (step_rows, LANES), 1) // tper
    for h in range(nh):
        got = [near[h * per + j].astype(jnp.float32) for j in range(per)]
        for p in range(npair):
            for kp in range(parts):
                tile = None
                for j in range(per):
                    shift = (tper * j - (kp * (LANES // parts) + tper * p)) % LANES
                    moved = pltpu.roll(got[j], shift, 1) if shift else got[j]
                    tile = moved if tile is None else jnp.where(lane == j, moved, tile)
                col = (h * npair + p) * LANES
                o_ref[kp, :, col:col + LANES] = tile.astype(jnp.bfloat16)


def arrange(near, ngroup, tper, k):
    nrow, nk, _ = near.shape
    nh = tper * nrow // LANES
    npair = ngroup // 2
    parts = k // nk
    cols = nh * npair * LANES
    step_rows = min(nk, 256)
    out = pl.pallas_call(
        functools.partial(arrange_kernel, nh=nh, per=LANES // tper, npair=npair, parts=parts, tper=tper),
        out_shape=jax.ShapeDtypeStruct((parts, nk, cols), jnp.bfloat16),
        grid=(nk // step_rows,),
        in_specs=[pl.BlockSpec((nrow, step_rows, LANES), lambda i: (0, i, 0))],
        out_specs=pl.BlockSpec((parts, step_rows, cols), lambda i: (0, i, 0)),
        compiler_params=pltpu.CompilerParams(
            dimension_semantics=("arbitrary",), vmem_limit_bytes=40 << 20
        ),
        name="arrange",
    )(near)
    return out.reshape(k, cols)


def product_kernel(where, w_ref, *refs, ngroup, nh, half):
    mine = refs[:ngroup]
    theirs = refs[ngroup:2 * ngroup]
    near_hbm, o_ref, bt, sem = refs[2 * ngroup:]
    group = where[0]
    core = where[1]
    npair = ngroup // 2
    rows = bt.shape[0] // 2

    @pl.when(pl.program_id(0) == 0)
    def _():
        copies = [pltpu.make_async_copy(near_hbm, bt.at[:, ngroup * LANES:], sem.at[2 * ngroup])]
        for s in range(ngroup):
            cols = slice(s * LANES, (s + 1) * LANES)
            for d, ref in ((0, mine[s]), (1, theirs[s])):
                at = pl.multiple_of(jnp.where(core == d, 0, 1) * rows, rows)
                copies.append(pltpu.make_async_copy(ref, bt.at[pl.ds(at, rows), cols], sem.at[2 * s + d]))
        for c in copies:
            c.start()
        for c in copies:
            c.wait()

    res = jnp.dot(w_ref[...], bt[...], preferred_element_type=jnp.float32)
    slot = (lax.broadcasted_iota(jnp.int32, (res.shape[0], LANES), 1) // half) % 2
    for s in range(ngroup):
        far = res[:, s * LANES:(s + 1) * LANES]
        for h in range(nh):
            first = pltpu.roll(far, LANES - half * h, 1) if h else far
            at = (ngroup + h * npair + s // 2) * LANES
            second = res[:, at:at + LANES]
            if s % 2 == 0:
                second = pltpu.roll(second, half, 1)
            tile = jnp.where(slot == 0, first, second).astype(jnp.bfloat16)
            col = pl.multiple_of(((group ^ s) * nh + h) * LANES, LANES)
            o_ref[:, pl.ds(col, LANES)] = tile


def product(where, w, mine, theirs, near, half, snap):
    m, k = w.shape
    ngroup = len(mine)
    mb = 384
    return pl.pallas_call(
        functools.partial(product_kernel, ngroup=ngroup, nh=snap // (ngroup * LANES), half=half),
        out_shape=jax.ShapeDtypeStruct((m, snap), jnp.bfloat16),
        grid_spec=pltpu.PrefetchScalarGridSpec(
            num_scalar_prefetch=1,
            grid=(m // mb,),
            in_specs=[pl.BlockSpec((mb, k), lambda i, c: (i, 0))]
            + [pl.BlockSpec(memory_space=pl.ANY)] * (2 * ngroup + 1),
            out_specs=pl.BlockSpec((mb, snap), lambda i, c: (i, 0)),
            scratch_shapes=[
                pltpu.VMEM((k, snap), jnp.bfloat16),
                pltpu.SemaphoreType.DMA((2 * ngroup + 1,)),
            ],
        ),
        compiler_params=pltpu.CompilerParams(
            dimension_semantics=("arbitrary",), vmem_limit_bytes=56 << 20
        ),
        name="product",
    )(where, w, *mine, *theirs, near)


def body(snapshots, bnd_index, recovery, block_se, connect, stress_mat):
    ngroup = lax.axis_size("group")
    nrow = lax.axis_size("row")
    nse = bnd_index.shape[0] // ngroup
    nblk, blk, nb = recovery.shape
    nel, nc, ndof = stress_mat.shape
    tper = snapshots.shape[0]
    half = tper // 2
    snap = tper * ngroup * nrow
    group = lax.axis_index("group")
    core = lax.axis_index("row") % 2
    swap = lambda s: [(i, i ^ s) for i in range(ngroup)]
    other = [(i, i ^ 1) for i in range(nrow)]

    top = snapshots[:half]
    bottom = snapshots[half:]
    along_row = lax.all_gather(top, "row", axis=0, tiled=False)
    along_group = [bottom] + [lax.ppermute(bottom, "group", swap(s)) for s in range(1, ngroup)]

    ends = nrow - 1
    up = [(i, i + 1) for i in range(ends)]
    down = [(i + 1, i) for i in range(ends)]

    def with_se(part, se):
        return jnp.concatenate([part, jnp.full((16, nb), se.astype(part.dtype))])

    last_rows = with_se(recovery[nblk - 1, blk - HW:], block_se[nblk - 1])
    first_rows = with_se(recovery[0, :HW], block_se[0])

    ngrp = nel // SUB
    conn = connect.T.reshape(ndof, ngrp, SUB).transpose(1, 0, 2).reshape(ngrp, ndof * SUB)
    smat = stress_mat.transpose(1, 2, 0).astype(jnp.float32).reshape(nc, ndof, ngrp, SUB)
    smat = smat.transpose(0, 2, 1, 3).reshape(nc, ngrp, ndof * SUB)
    flat = conn.reshape(-1) * (nb // LANES + 1)
    where = jnp.stack([group, core]).astype(jnp.int32)

    rows = nse * nb // 2
    parted = bnd_index.reshape(ngroup, 2, rows)
    own_idx = lax.dynamic_index_in_dim(parted, group, 0, keepdims=False).reshape(-1)
    mid = lax.dynamic_index_in_dim(parted, core, 1, keepdims=False)
    far_idx = jnp.concatenate([
        lax.dynamic_index_in_dim(mid, group ^ s, 0, keepdims=False) for s in range(ngroup)
    ])

    own_idx, far_idx, flat, conn, smat, where, last_rows, first_rows = lax.optimization_barrier(
        (own_idx, far_idx, flat, conn, smat, where, last_rows, first_rows)
    )
    picked = pick_near(own_idx, along_group)
    picked, far_idx = lax.optimization_barrier((picked, far_idx))
    near = lax.all_gather(picked, "row", axis=0, tiled=False)
    head = lax.ppermute(last_rows, "row", up)
    tail = lax.ppermute(first_rows, "row", down)
    per = LANES // tper
    order = [per * h + j for j in range(per) for h in range(nrow // per)]
    far = pick_far(far_idx.reshape(ngroup, rows), along_row, order)
    mine = [far[0]] + [lax.ppermute(far[s], "group", swap(s)) for s in range(1, ngroup)]
    flat, mine[0] = lax.optimization_barrier((flat, mine[0]))
    w = combine(flat, block_se, conn, smat, recovery, head, tail, nse)
    *mine, w = lax.optimization_barrier((*mine, w))
    theirs = [lax.ppermute(x, "row", other) for x in mine]
    near, w = lax.optimization_barrier((near, w))
    near = arrange(near, ngroup, tper, nse * nb)
    out = product(where, w.reshape(nc * nel, nse * nb), mine, theirs, near, half, snap)
    return out.reshape(nc, nel, snap).transpose(1, 0, 2)


def solution(mesh):
    in_specs = (
        P(("group", "row"), None),
        P(),
        P(("group", "row"), None, None),
        P(("group", "row")),
        P(("group", "row"), None),
        P(("group", "row"), None, None),
    )
    out_specs = P(("group", "row"), None, None)
    return jax.shard_map(body, mesh=mesh, in_specs=in_specs, out_specs=out_specs, check_vma=False)
```

```python
import functools

import jax
import jax.numpy as jnp
from jax import lax
from jax.experimental import pallas as pl
from jax.experimental.pallas import tpu as pltpu
from jax.sharding import PartitionSpec as P

HW = 256
SUB = 8
LANES = 128


def combine_kernel(
    conn, se, grow_ref, s_ref, rec_hbm, head_ref, tail_ref, w_ref, tbl, buf, sem, g0, g1, g2, g3,
    *, nfill, blk, nlt, nse, nc, ndof, inner, ts, gs, nbuf
):
    step = pl.program_id(0)
    rows = SUB * ndof
    steps = pl.num_programs(0) - nfill

    def fetch(b):
        return pltpu.make_async_copy(rec_hbm.at[b], buf.at[b % nbuf], sem.at[b % nbuf])

    def fill(src, base, count):
        def one(i, carry):
            at = pl.multiple_of(i * 16, 16)
            for j in range(nlt):
                part = src[pl.ds(at, 16), j * LANES:(j + 1) * LANES].astype(jnp.float32)
                tbl[pl.ds((base + at) * ts + j, 16, stride=ts), :] = part
            return carry

        lax.fori_loop(0, count // 16, one, 0, unroll=4)

    def gather(group, dst, lo=0, hi=rows):
        first = group * rows
        for q in range(lo, hi):
            dst[pl.ds(q, nlt, stride=gs), :] = tbl[pl.ds(conn[first + q], nlt), :]

    own = (
        lax.broadcasted_iota(jnp.int32, (SUB, rows), 1) % SUB
        == lax.broadcasted_iota(jnp.int32, (SUB, rows), 0)
    )

    def halo_tag(ref):
        wide = -(-rows // LANES) * LANES
        return ref[HW:HW + 16, :wide].astype(jnp.float32)[:1, :rows].astype(jnp.int32)

    head_tag = halo_tag(head_ref)
    tail_tag = halo_tag(tail_ref)

    def left(i):
        where = (grow_ref[pl.ds(i, 1), :] + (blk - HW)) // blk
        tag = jnp.where(where == 0, head_tag, tail_tag)
        for b in range(nfill):
            tag = jnp.where(where == b + 1, se[b], tag)
        tag = jnp.where(own, jnp.broadcast_to(tag, (SUB, rows)), -1)
        parts = []
        for s in range(nse):
            hit = tag == s
            for c in range(nc):
                parts.append(jnp.where(hit, jnp.broadcast_to(s_ref[c, pl.ds(i, 1), :], (SUB, rows)), 0.0))
        return jnp.concatenate(parts, axis=0).astype(jnp.bfloat16)

    def matmul(first, i, srcs, nxt, dsts):
        lhs = [left(first + i), left(first + i + 1)]
        at = pl.multiple_of(i * SUB, 2 * SUB)
        for j in range(0, nlt, 2):
            res = []
            for t in range(2):
                src = srcs[t]
                rhs = jnp.concatenate(
                    [src[(j + d) * gs:(j + d) * gs + rows, :].astype(jnp.bfloat16) for d in range(2)], axis=1
                )
                res.append(jnp.dot(lhs[t], rhs, preferred_element_type=jnp.float32))
                gather(nxt + t, dsts[t], rows * j // nlt, rows * (j + 2) // nlt)
            for s in range(nse):
                col = (s * nlt + j) * LANES
                for c in range(nc):
                    r0 = (s * nc + c) * SUB
                    both = jnp.concatenate([r[r0:r0 + SUB] for r in res], axis=0)
                    w_ref[c, pl.ds(at, 2 * SUB), col:col + 2 * LANES] = both.astype(jnp.bfloat16)

    @pl.when(step == 0)
    def _():
        for b in range(nbuf):
            fetch(b).start()
        fill(head_ref, 0, HW)
        fill(tail_ref, HW + nfill * blk, HW)

    @pl.when(step < nfill)
    def _():
        fetch(step).wait()
        fill(buf.at[step % nbuf], HW + step * blk, blk)

        @pl.when(step + nbuf < nfill)
        def _():
            fetch(step + nbuf).start()

    @pl.when(step >= nfill)
    def _():
        base = (step - nfill) * inner
        last = steps * inner - 2

        @pl.when(step == nfill)
        def _():
            gather(0, g0)
            gather(1, g1)

        def four(i, carry):
            n = base + 4 * i
            matmul(base, 4 * i, (g0, g1), n + 2, (g2, g3))
            matmul(base, 4 * i + 2, (g2, g3), jnp.minimum(n + 4, last), (g0, g1))
            return carry

        lax.fori_loop(0, inner // 4, four, 0)


def combine(conn, se, grow, smat, recovery, head, tail, nse, inner=4, nbuf=6):
    nblk, blk, nb = recovery.shape
    ngrp, rows = grow.shape
    nel = ngrp * SUB
    ndof = rows // SUB
    nc = smat.shape[0]
    nlt = nb // LANES
    steps = ngrp // inner
    ts = nlt + 1
    gs = rows + 1
    kern = functools.partial(
        combine_kernel, nfill=nblk, blk=blk, nlt=nlt, nse=nse, nc=nc, ndof=ndof, inner=inner, ts=ts, gs=gs,
        nbuf=nbuf,
    )
    later = lambda i: jnp.maximum(i - nblk, 0)
    return pl.pallas_call(
        kern,
        out_shape=jax.ShapeDtypeStruct((nc, nel, nse * nb), jnp.bfloat16),
        grid_spec=pltpu.PrefetchScalarGridSpec(
            num_scalar_prefetch=2,
            grid=(nblk + steps,),
            in_specs=[
                pl.BlockSpec((ngrp, rows), lambda i, c, s: (0, 0)),
                pl.BlockSpec((nc, ngrp, rows), lambda i, c, s: (0, 0, 0)),
                pl.BlockSpec(memory_space=pl.ANY),
                pl.BlockSpec((HW + 16, nb), lambda i, c, s: (0, 0)),
                pl.BlockSpec((HW + 16, nb), lambda i, c, s: (0, 0)),
            ],
            out_specs=pl.BlockSpec((nc, SUB * inner, nse * nb), lambda i, c, s: (0, later(i), 0)),
            scratch_shapes=[
                pltpu.VMEM(((nblk * blk + 2 * HW) * ts, LANES), jnp.float32),
                pltpu.VMEM((nbuf, blk, nb), jnp.bfloat16),
                pltpu.SemaphoreType.DMA((nbuf,)),
            ] + [pltpu.VMEM((gs * nlt, LANES), jnp.float32)] * 4,
        ),
        compiler_params=pltpu.CompilerParams(dimension_semantics=("arbitrary",), vmem_limit_bytes=60 << 20),
        cost_estimate=pl.CostEstimate(flops=30 * 10**9, bytes_accessed=120 << 20, transcendentals=0),
        name="combine",
    )(conn, se, grow, smat, recovery, head, tail)


def pick_near_kernel(idx, *refs, nsrc, half, parts, chunk):
    srcs = refs[:nsrc]
    o_ref, tbl = refs[nsrc:nsrc + 2]
    bufs = refs[nsrc + 2:]
    step = pl.program_id(0)
    nd = tbl.shape[0]
    total = chunk * pl.num_programs(0)

    @pl.when(step == 0)
    def _():
        def one(i, carry):
            at = pl.multiple_of(i * LANES, LANES)
            rows = jnp.concatenate([s[:, pl.ds(at, LANES)] for s in srcs] * parts, axis=0)
            tbl[pl.ds(at, LANES), :] = rows.T.astype(jnp.float32)
            return carry

        lax.fori_loop(0, nd // LANES, one, 0, unroll=2)

    def some(i, carry):
        at = pl.multiple_of(i * 64, 64)
        for p in range(parts):
            for q in range(64):
                k = idx[p * total + step * chunk + at + q]
                bufs[p][pl.ds(at + q, 1), :] = tbl[pl.ds(k, 1), :]
        return carry

    lax.fori_loop(0, chunk // 64, some, 0)
    piece = lax.broadcasted_iota(jnp.int32, (chunk, LANES), 1) // (LANES // parts)
    out = bufs[0][...]
    for p in range(1, parts):
        out = jnp.where(piece == p, bufs[p][...], out)
    o_ref[...] = out.astype(jnp.bfloat16)


def pick_near(idx, srcs):
    half, nd = srcs[0].shape
    parts = LANES // (half * len(srcs))
    n = idx.shape[0] // parts
    chunk = min(n, 1024)
    return pl.pallas_call(
        functools.partial(pick_near_kernel, nsrc=len(srcs), half=half, parts=parts, chunk=chunk),
        out_shape=jax.ShapeDtypeStruct((n, LANES), jnp.bfloat16),
        grid_spec=pltpu.PrefetchScalarGridSpec(
            num_scalar_prefetch=1,
            grid=(n // chunk,),
            in_specs=[pl.BlockSpec((half, nd), lambda i, c: (0, 0)) for _ in srcs],
            out_specs=pl.BlockSpec((chunk, LANES), lambda i, c: (i, 0)),
            scratch_shapes=[pltpu.VMEM((nd, LANES), jnp.float32)]
            + [pltpu.VMEM((chunk, LANES), jnp.float32) for _ in range(parts)],
        ),
        compiler_params=pltpu.CompilerParams(
            dimension_semantics=("arbitrary",), vmem_limit_bytes=40 << 20
        ),
        name="pick_near",
    )(idx, *srcs)


def pick_far_kernel(idx, slots, *refs, nsrc, order, chunk):
    srcs = refs[:nsrc]
    o_ref, src, tbl, buf, sem = refs[nsrc:]
    step = pl.program_id(0)
    nd = tbl.shape[0]

    @pl.when(step == 0)
    def _():
        copies = [
            pltpu.make_async_copy(ref, src.at[slots[i]], sem.at[i]) for i, ref in enumerate(srcs)
        ]
        for copy in copies:
            copy.start()
        for copy in copies:
            copy.wait()

        def one(i, carry):
            at = pl.multiple_of(i * LANES, LANES)
            rows = jnp.concatenate([src[r, :, pl.ds(at, LANES)] for r in order], axis=0)
            tbl[pl.ds(at, LANES), :] = rows.T.astype(jnp.float32)
            return carry

        lax.fori_loop(0, nd // LANES, one, 0, unroll=2)

    def some(i, carry):
        at = pl.multiple_of(i * 64, 64)
        for q in range(64):
            buf[pl.ds(at + q, 1), :] = tbl[pl.ds(idx[step * chunk + at + q], 1), :]
        return carry

    lax.fori_loop(0, chunk // 64, some, 0)
    o_ref[...] = buf[...].astype(jnp.bfloat16)


def pick_far(idx, slots, srcs, order):
    nrow = len(srcs)
    half, nd = srcs[0].shape
    n = idx.shape[0]
    chunk = min(n, 1024)
    return pl.pallas_call(
        functools.partial(pick_far_kernel, nsrc=nrow, order=order, chunk=chunk),
        out_shape=jax.ShapeDtypeStruct((n, LANES), jnp.bfloat16),
        grid_spec=pltpu.PrefetchScalarGridSpec(
            num_scalar_prefetch=2,
            grid=(n // chunk,),
            in_specs=[pl.BlockSpec(memory_space=pl.ANY)] * nrow,
            out_specs=pl.BlockSpec((chunk, LANES), lambda i, c, d: (i, 0)),
            scratch_shapes=[
                pltpu.VMEM((nrow, half, nd), jnp.bfloat16),
                pltpu.VMEM((nd, LANES), jnp.float32),
                pltpu.VMEM((chunk, LANES), jnp.float32),
                pltpu.SemaphoreType.DMA((nrow,)),
            ],
        ),
        compiler_params=pltpu.CompilerParams(
            dimension_semantics=("arbitrary",), vmem_limit_bytes=40 << 20
        ),
        name="pick_far",
    )(idx, slots, *srcs)


def arrange_kernel(slots, *refs, nsrc, nh, per, npair, parts, tper):
    srcs = refs[:nsrc]
    o_ref, near, sem = refs[nsrc:]
    step_rows = o_ref.shape[1]
    step = pl.program_id(0)

    @pl.when(step == 0)
    def _():
        copies = [
            pltpu.make_async_copy(ref, near.at[slots[i]], sem.at[i]) for i, ref in enumerate(srcs)
        ]
        for copy in copies:
            copy.start()
        for copy in copies:
            copy.wait()

    lane = lax.broadcasted_iota(jnp.int32, (step_rows, LANES), 1) // tper
    at = pl.multiple_of(step * step_rows, step_rows)
    for h in range(nh):
        got = [near[h * per + j, pl.ds(at, step_rows), :].astype(jnp.float32) for j in range(per)]
        for p in range(npair):
            for kp in range(parts):
                tile = None
                for j in range(per):
                    shift = (tper * j - (kp * (LANES // parts) + tper * p)) % LANES
                    moved = pltpu.roll(got[j], shift, 1) if shift else got[j]
                    tile = moved if tile is None else jnp.where(lane == j, moved, tile)
                col = (h * npair + p) * LANES
                o_ref[kp, :, col:col + LANES] = tile.astype(jnp.bfloat16)


def arrange(slots, srcs, ngroup, tper, k):
    nrow = len(srcs)
    nk = srcs[0].shape[0]
    nh = tper * nrow // LANES
    npair = ngroup // 2
    parts = k // nk
    cols = nh * npair * LANES
    step_rows = min(nk, 256)
    out = pl.pallas_call(
        functools.partial(
            arrange_kernel, nsrc=nrow, nh=nh, per=LANES // tper, npair=npair, parts=parts, tper=tper
        ),
        out_shape=jax.ShapeDtypeStruct((parts, nk, cols), jnp.bfloat16),
        grid_spec=pltpu.PrefetchScalarGridSpec(
            num_scalar_prefetch=1,
            grid=(nk // step_rows,),
            in_specs=[pl.BlockSpec(memory_space=pl.ANY)] * nrow,
            out_specs=pl.BlockSpec((parts, step_rows, cols), lambda i, c: (0, i, 0)),
            scratch_shapes=[
                pltpu.VMEM((nrow, nk, LANES), jnp.bfloat16),
                pltpu.SemaphoreType.DMA((nrow,)),
            ],
        ),
        compiler_params=pltpu.CompilerParams(
            dimension_semantics=("arbitrary",), vmem_limit_bytes=40 << 20
        ),
        name="arrange",
    )(slots, *srcs)
    return out.reshape(k, cols)


def product_kernel(where, w_ref, mine, theirs, near_hbm, o_ref, bt, sem, *, ngroup, nh, half):
    group = where[0]
    core = where[1]
    npair = ngroup // 2
    rows = bt.shape[0] // 2

    @pl.when(pl.program_id(0) == 0)
    def _():
        copies = [pltpu.make_async_copy(near_hbm, bt.at[:, ngroup * LANES:], sem.at[2 * ngroup])]
        for s in range(ngroup):
            cols = slice(s * LANES, (s + 1) * LANES)
            for d, ref in ((0, mine), (1, theirs)):
                at = pl.multiple_of(jnp.where(core == d, 0, 1) * rows, rows)
                copies.append(
                    pltpu.make_async_copy(ref.at[group ^ s], bt.at[pl.ds(at, rows), cols], sem.at[2 * s + d])
                )
        for c in copies:
            c.start()
        for c in copies:
            c.wait()

    res = jnp.dot(w_ref[...], bt[...], preferred_element_type=jnp.float32)
    slot = (lax.broadcasted_iota(jnp.int32, (res.shape[0], LANES), 1) // half) % 2
    for s in range(ngroup):
        far = res[:, s * LANES:(s + 1) * LANES]
        for h in range(nh):
            first = pltpu.roll(far, LANES - half * h, 1) if h else far
            at = (ngroup + h * npair + s // 2) * LANES
            second = res[:, at:at + LANES]
            if s % 2 == 0:
                second = pltpu.roll(second, half, 1)
            tile = jnp.where(slot == 0, first, second).astype(jnp.bfloat16)
            col = pl.multiple_of(((group ^ s) * nh + h) * LANES, LANES)
            o_ref[:, pl.ds(col, LANES)] = tile


def product(where, w, mine, theirs, near, half, snap):
    m, k = w.shape
    ngroup = mine.shape[0]
    mb = 384
    return pl.pallas_call(
        functools.partial(product_kernel, ngroup=ngroup, nh=snap // (ngroup * LANES), half=half),
        out_shape=jax.ShapeDtypeStruct((m, snap), jnp.bfloat16),
        grid_spec=pltpu.PrefetchScalarGridSpec(
            num_scalar_prefetch=1,
            grid=(m // mb,),
            in_specs=[pl.BlockSpec((mb, k), lambda i, c: (i, 0))]
            + [pl.BlockSpec(memory_space=pl.ANY)] * 3,
            out_specs=pl.BlockSpec((mb, snap), lambda i, c: (i, 0)),
            scratch_shapes=[
                pltpu.VMEM((k, snap), jnp.bfloat16),
                pltpu.SemaphoreType.DMA((2 * ngroup + 1,)),
            ],
        ),
        compiler_params=pltpu.CompilerParams(
            dimension_semantics=("arbitrary",), vmem_limit_bytes=56 << 20
        ),
        name="product",
    )(where, w, mine, theirs, near)


def body(snapshots, bnd_index, recovery, block_se, connect, stress_mat):
    ngroup = lax.axis_size("group")
    nrow = lax.axis_size("row")
    nse = bnd_index.shape[0] // ngroup
    nblk, blk, nb = recovery.shape
    nel, nc, ndof = stress_mat.shape
    tper = snapshots.shape[0]
    half = tper // 2
    snap = tper * ngroup * nrow
    group = lax.axis_index("group")
    core = lax.axis_index("row") % 2
    swap = lambda s: [(i, i ^ s) for i in range(ngroup)]
    other = [(i, i ^ 1) for i in range(nrow)]

    top = snapshots[:half]
    bottom = snapshots[half:]
    row = lax.axis_index("row")
    nz = nrow // 2
    along = lambda s: [(i, (i + 2 * s) % nrow) for i in range(nrow)]
    to_other = lambda x: lax.ppermute(x, "row", other)
    tops = [top] + [lax.ppermute(top, "row", along(s)) for s in range(1, nz)]
    top_other = to_other(top)
    along_group = [bottom] + [lax.ppermute(bottom, "group", swap(s)) for s in range(1, ngroup)]

    ends = nrow - 1
    up = [(i, i + 1) for i in range(ends)]
    down = [(i + 1, i) for i in range(ends)]

    def with_se(part, se):
        return jnp.concatenate([part, jnp.full((16, nb), se.astype(part.dtype))])

    last_rows = with_se(recovery[nblk - 1, blk - HW:], block_se[nblk - 1])
    first_rows = with_se(recovery[0, :HW], block_se[0])

    ngrp = nel // SUB
    conn = connect.T.reshape(ndof, ngrp, SUB).transpose(1, 0, 2).reshape(ngrp, ndof * SUB)
    smat = stress_mat.transpose(1, 2, 0).astype(jnp.float32).reshape(nc, ndof, ngrp, SUB)
    smat = smat.transpose(0, 2, 1, 3).reshape(nc, ngrp, ndof * SUB)
    flat = conn.reshape(-1) * (nb // LANES + 1)
    where = jnp.stack([group, core]).astype(jnp.int32)
    sender = (row - 2 * jnp.arange(nz, dtype=jnp.int32)) % nrow
    slots = jnp.concatenate([sender, sender ^ 1]).astype(jnp.int32)

    rows = nse * nb // 2
    parted = bnd_index.reshape(ngroup, 2, rows)
    own_idx = lax.dynamic_index_in_dim(parted, group, 0, keepdims=False).reshape(-1)
    far_idx = lax.dynamic_index_in_dim(parted, core, 1, keepdims=False).reshape(-1)

    own_idx, far_idx, flat, conn, smat, where, slots, last_rows, first_rows = lax.optimization_barrier(
        (own_idx, far_idx, flat, conn, smat, where, slots, last_rows, first_rows)
    )
    picked = pick_near(own_idx, along_group)
    picked, far_idx, last_rows, first_rows, *tops = lax.optimization_barrier(
        (picked, far_idx, last_rows, first_rows, *tops)
    )
    head = lax.ppermute(last_rows, "row", up)
    tail = lax.ppermute(first_rows, "row", down)
    nears = [picked] + [lax.ppermute(picked, "row", along(s)) for s in range(1, nz)]
    tops = tops + [top_other] + [to_other(x) for x in tops[1:]]
    per = LANES // tper
    order = [per * h + j for j in range(per) for h in range(nrow // per)]
    far = pick_far(far_idx, slots, tops, order)
    mine = lax.all_to_all(far.reshape(ngroup, rows, LANES), "group", split_axis=0, concat_axis=0, tiled=True)
    flat, far = lax.optimization_barrier((flat, far))
    w = combine(flat, block_se, conn, smat, recovery, head, tail, nse)
    mine, nears, w = lax.optimization_barrier((mine, nears, w))
    nears = nears + [to_other(x) for x in nears]
    theirs = to_other(mine)
    near = arrange(slots, nears, ngroup, tper, nse * nb)
    out = product(where, w.reshape(nc * nel, nse * nb), mine, theirs, near, half, snap)
    return out.reshape(nc, nel, snap).transpose(1, 0, 2)


def solution(mesh):
    in_specs = (
        P(("group", "row"), None),
        P(),
        P(("group", "row"), None, None),
        P(("group", "row")),
        P(("group", "row"), None),
        P(("group", "row"), None, None),
    )
    out_specs = P(("group", "row"), None, None)
    return jax.shard_map(body, mesh=mesh, in_specs=in_specs, out_specs=out_specs, check_vma=False)
```

```python
import functools

import jax
import jax.numpy as jnp
from jax import lax
from jax.experimental import pallas as pl
from jax.experimental.pallas import tpu as pltpu
from jax.sharding import PartitionSpec as P

HW = 256
SUB = 8
LANES = 128


def combine_kernel(
    conn, se, grow_ref, s_ref, rec_hbm, head_ref, tail_ref, w_ref, tbl, buf, sem, g0, g1, g2, g3,
    *, nfill, blk, nlt, nse, nc, ndof, inner, ts, gs, nbuf
):
    step = pl.program_id(0)
    rows = SUB * ndof
    steps = pl.num_programs(0) - nfill

    def fetch(b):
        return pltpu.make_async_copy(rec_hbm.at[b], buf.at[b % nbuf], sem.at[b % nbuf])

    def fill(src, base, count):
        def one(i, carry):
            at = pl.multiple_of(i * 16, 16)
            for j in range(nlt):
                part = src[pl.ds(at, 16), j * LANES:(j + 1) * LANES].astype(jnp.float32)
                tbl[pl.ds((base + at) * ts + j, 16, stride=ts), :] = part
            return carry

        lax.fori_loop(0, count // 16, one, 0, unroll=4)

    def gather(group, dst, lo=0, hi=rows):
        first = group * rows
        for q in range(lo, hi):
            dst[pl.ds(q, nlt, stride=gs), :] = tbl[pl.ds(conn[first + q], nlt), :]

    own = (
        lax.broadcasted_iota(jnp.int32, (SUB, rows), 1) % SUB
        == lax.broadcasted_iota(jnp.int32, (SUB, rows), 0)
    )

    def halo_tag(ref, at):
        wide = -(-rows // LANES) * LANES
        return ref[at:at + 16, :wide].astype(jnp.float32)[:1, :rows].astype(jnp.int32)

    head_tag = halo_tag(head_ref, 0)
    tail_tag = halo_tag(tail_ref, HW)

    def left(i):
        where = (grow_ref[pl.ds(i, 1), :] + (blk - HW)) // blk
        tag = jnp.where(where == 0, head_tag, tail_tag)
        for b in range(nfill):
            tag = jnp.where(where == b + 1, se[b], tag)
        tag = jnp.where(own, jnp.broadcast_to(tag, (SUB, rows)), -1)
        parts = []
        for s in range(nse):
            hit = tag == s
            for c in range(nc):
                parts.append(jnp.where(hit, jnp.broadcast_to(s_ref[c, pl.ds(i, 1), :], (SUB, rows)), 0.0))
        return jnp.concatenate(parts, axis=0).astype(jnp.bfloat16)

    def matmul(first, i, srcs, nxt, dsts):
        lhs = [left(first + i), left(first + i + 1)]
        at = pl.multiple_of(i * SUB, 2 * SUB)
        for j in range(0, nlt, 2):
            res = []
            for t in range(2):
                src = srcs[t]
                rhs = jnp.concatenate(
                    [src[(j + d) * gs:(j + d) * gs + rows, :].astype(jnp.bfloat16) for d in range(2)], axis=1
                )
                res.append(jnp.dot(lhs[t], rhs, preferred_element_type=jnp.float32))
                gather(nxt + t, dsts[t], rows * j // nlt, rows * (j + 2) // nlt)
            for s in range(nse):
                col = (s * nlt + j) * LANES
                for c in range(nc):
                    r0 = (s * nc + c) * SUB
                    both = jnp.concatenate([r[r0:r0 + SUB] for r in res], axis=0)
                    w_ref[c, pl.ds(at, 2 * SUB), col:col + 2 * LANES] = both.astype(jnp.bfloat16)

    @pl.when(step == 0)
    def _():
        for b in range(nbuf):
            fetch(b).start()
        fill(head_ref.at[pl.ds(16, HW)], 0, HW)
        fill(tail_ref, HW + nfill * blk, HW)

    @pl.when(step < nfill)
    def _():
        fetch(step).wait()
        fill(buf.at[step % nbuf], HW + step * blk, blk)

        @pl.when(step + nbuf < nfill)
        def _():
            fetch(step + nbuf).start()

    @pl.when(step >= nfill)
    def _():
        base = (step - nfill) * inner
        last = steps * inner - 2

        @pl.when(step == nfill)
        def _():
            gather(0, g0)
            gather(1, g1)

        def four(i, carry):
            n = base + 4 * i
            matmul(base, 4 * i, (g0, g1), n + 2, (g2, g3))
            matmul(base, 4 * i + 2, (g2, g3), jnp.minimum(n + 4, last), (g0, g1))
            return carry

        lax.fori_loop(0, inner // 4, four, 0)


def combine(conn, se, grow, smat, recovery, head, tail, nse, inner=4, nbuf=6):
    nblk, blk, nb = recovery.shape
    ngrp, rows = grow.shape
    nel = ngrp * SUB
    ndof = rows // SUB
    nc = smat.shape[0]
    nlt = nb // LANES
    steps = ngrp // inner
    ts = nlt + 1
    gs = rows + 1
    kern = functools.partial(
        combine_kernel, nfill=nblk, blk=blk, nlt=nlt, nse=nse, nc=nc, ndof=ndof, inner=inner, ts=ts, gs=gs,
        nbuf=nbuf,
    )
    later = lambda i: jnp.maximum(i - nblk, 0)
    return pl.pallas_call(
        kern,
        out_shape=jax.ShapeDtypeStruct((nc, nel, nse * nb), jnp.bfloat16),
        grid_spec=pltpu.PrefetchScalarGridSpec(
            num_scalar_prefetch=2,
            grid=(nblk + steps,),
            in_specs=[
                pl.BlockSpec((ngrp, rows), lambda i, c, s: (0, 0)),
                pl.BlockSpec((nc, ngrp, rows), lambda i, c, s: (0, 0, 0)),
                pl.BlockSpec(memory_space=pl.ANY),
                pl.BlockSpec((HW + 16, nb), lambda i, c, s: (0, 0)),
                pl.BlockSpec((HW + 16, nb), lambda i, c, s: (0, 0)),
            ],
            out_specs=pl.BlockSpec((nc, SUB * inner, nse * nb), lambda i, c, s: (0, later(i), 0)),
            scratch_shapes=[
                pltpu.VMEM(((nblk * blk + 2 * HW) * ts, LANES), jnp.float32),
                pltpu.VMEM((nbuf, blk, nb), jnp.bfloat16),
                pltpu.SemaphoreType.DMA((nbuf,)),
            ] + [pltpu.VMEM((gs * nlt, LANES), jnp.float32)] * 4,
        ),
        compiler_params=pltpu.CompilerParams(dimension_semantics=("arbitrary",), vmem_limit_bytes=60 << 20),
        cost_estimate=pl.CostEstimate(flops=30 * 10**9, bytes_accessed=120 << 20, transcendentals=0),
        name="combine",
    )(conn, se, grow, smat, recovery, head, tail)


def pick_near_kernel(idx, *refs, nsrc, half, parts, chunk):
    srcs = refs[:nsrc]
    o_ref, tbl = refs[nsrc:nsrc + 2]
    bufs = refs[nsrc + 2:]
    step = pl.program_id(0)
    nd = tbl.shape[0]
    total = chunk * pl.num_programs(0)

    @pl.when(step == 0)
    def _():
        def one(i, carry):
            at = pl.multiple_of(i * LANES, LANES)
            rows = jnp.concatenate([s[:, pl.ds(at, LANES)] for s in srcs] * parts, axis=0)
            tbl[pl.ds(at, LANES), :] = rows.T.astype(jnp.float32)
            return carry

        lax.fori_loop(0, nd // LANES, one, 0, unroll=2)

    def some(i, carry):
        at = pl.multiple_of(i * 64, 64)
        for p in range(parts):
            for q in range(64):
                k = idx[p * total + step * chunk + at + q]
                bufs[p][pl.ds(at + q, 1), :] = tbl[pl.ds(k, 1), :]
        return carry

    lax.fori_loop(0, chunk // 64, some, 0)
    piece = lax.broadcasted_iota(jnp.int32, (chunk, LANES), 1) // (LANES // parts)
    out = bufs[0][...]
    for p in range(1, parts):
        out = jnp.where(piece == p, bufs[p][...], out)
    o_ref[...] = out.astype(jnp.bfloat16)


def pick_near(idx, srcs):
    half, nd = srcs[0].shape
    parts = LANES // (half * len(srcs))
    n = idx.shape[0] // parts
    chunk = min(n, 1024)
    return pl.pallas_call(
        functools.partial(pick_near_kernel, nsrc=len(srcs), half=half, parts=parts, chunk=chunk),
        out_shape=jax.ShapeDtypeStruct((n, LANES), jnp.bfloat16),
        grid_spec=pltpu.PrefetchScalarGridSpec(
            num_scalar_prefetch=1,
            grid=(n // chunk,),
            in_specs=[pl.BlockSpec((half, nd), lambda i, c: (0, 0)) for _ in srcs],
            out_specs=pl.BlockSpec((chunk, LANES), lambda i, c: (i, 0)),
            scratch_shapes=[pltpu.VMEM((nd, LANES), jnp.float32)]
            + [pltpu.VMEM((chunk, LANES), jnp.float32) for _ in range(parts)],
        ),
        compiler_params=pltpu.CompilerParams(
            dimension_semantics=("arbitrary",), vmem_limit_bytes=40 << 20
        ),
        name="pick_near",
    )(idx, *srcs)


def pick_far_kernel(idx, slots, *refs, nsrc, order, chunk):
    srcs = refs[:nsrc]
    o_ref, src, tbl, buf, sem = refs[nsrc:]
    step = pl.program_id(0)
    nd = tbl.shape[0]

    @pl.when(step == 0)
    def _():
        copies = [
            pltpu.make_async_copy(ref, src.at[slots[i]], sem.at[i]) for i, ref in enumerate(srcs)
        ]
        for copy in copies:
            copy.start()
        for copy in copies:
            copy.wait()

        def one(i, carry):
            at = pl.multiple_of(i * LANES, LANES)
            rows = jnp.concatenate([src[r, :, pl.ds(at, LANES)] for r in order], axis=0)
            tbl[pl.ds(at, LANES), :] = rows.T.astype(jnp.float32)
            return carry

        lax.fori_loop(0, nd // LANES, one, 0, unroll=2)

    def some(i, carry):
        at = pl.multiple_of(i * 64, 64)
        for q in range(64):
            buf[pl.ds(at + q, 1), :] = tbl[pl.ds(idx[step * chunk + at + q], 1), :]
        return carry

    lax.fori_loop(0, chunk // 64, some, 0)
    o_ref[...] = buf[...].astype(jnp.bfloat16)


def pick_far(idx, slots, srcs, order):
    nrow = len(srcs)
    half, nd = srcs[0].shape
    n = idx.shape[0]
    chunk = min(n, 1024)
    return pl.pallas_call(
        functools.partial(pick_far_kernel, nsrc=nrow, order=order, chunk=chunk),
        out_shape=jax.ShapeDtypeStruct((n, LANES), jnp.bfloat16),
        grid_spec=pltpu.PrefetchScalarGridSpec(
            num_scalar_prefetch=2,
            grid=(n // chunk,),
            in_specs=[pl.BlockSpec(memory_space=pltpu.VMEM)] * nrow,
            out_specs=pl.BlockSpec((chunk, LANES), lambda i, c, d: (i, 0)),
            scratch_shapes=[
                pltpu.VMEM((nrow, half, nd), jnp.bfloat16),
                pltpu.VMEM((nd, LANES), jnp.float32),
                pltpu.VMEM((chunk, LANES), jnp.float32),
                pltpu.SemaphoreType.DMA((nrow,)),
            ],
        ),
        compiler_params=pltpu.CompilerParams(
            dimension_semantics=("arbitrary",), vmem_limit_bytes=40 << 20
        ),
        name="pick_far",
    )(idx, slots, *srcs)


def arrange_kernel(slots, *refs, nsrc, nh, per, npair, parts, tper):
    srcs = refs[:nsrc]
    o_ref, near, sem = refs[nsrc:]
    step_rows = o_ref.shape[1]
    step = pl.program_id(0)

    @pl.when(step == 0)
    def _():
        copies = [
            pltpu.make_async_copy(ref, near.at[slots[i]], sem.at[i]) for i, ref in enumerate(srcs)
        ]
        for copy in copies:
            copy.start()
        for copy in copies:
            copy.wait()

    lane = lax.broadcasted_iota(jnp.int32, (step_rows, LANES), 1) // tper
    at = pl.multiple_of(step * step_rows, step_rows)
    for h in range(nh):
        got = [near[h * per + j, pl.ds(at, step_rows), :].astype(jnp.float32) for j in range(per)]
        for p in range(npair):
            for kp in range(parts):
                tile = None
                for j in range(per):
                    shift = (tper * j - (kp * (LANES // parts) + tper * p)) % LANES
                    moved = pltpu.roll(got[j], shift, 1) if shift else got[j]
                    tile = moved if tile is None else jnp.where(lane == j, moved, tile)
                col = (h * npair + p) * LANES
                o_ref[kp, :, col:col + LANES] = tile.astype(jnp.bfloat16)


def arrange(slots, srcs, ngroup, tper, k):
    nrow = len(srcs)
    nk = srcs[0].shape[0]
    nh = tper * nrow // LANES
    npair = ngroup // 2
    parts = k // nk
    cols = nh * npair * LANES
    step_rows = min(nk, 256)
    out = pl.pallas_call(
        functools.partial(
            arrange_kernel, nsrc=nrow, nh=nh, per=LANES // tper, npair=npair, parts=parts, tper=tper
        ),
        out_shape=jax.ShapeDtypeStruct((parts, nk, cols), jnp.bfloat16),
        grid_spec=pltpu.PrefetchScalarGridSpec(
            num_scalar_prefetch=1,
            grid=(nk // step_rows,),
            in_specs=[pl.BlockSpec(memory_space=pltpu.VMEM)] * nrow,
            out_specs=pl.BlockSpec((parts, step_rows, cols), lambda i, c: (0, i, 0)),
            scratch_shapes=[
                pltpu.VMEM((nrow, nk, LANES), jnp.bfloat16),
                pltpu.SemaphoreType.DMA((nrow,)),
            ],
        ),
        compiler_params=pltpu.CompilerParams(
            dimension_semantics=("arbitrary",), vmem_limit_bytes=40 << 20
        ),
        name="arrange",
    )(slots, *srcs)
    return out.reshape(k, cols)


def product_kernel(where, w_ref, mine, theirs, near_hbm, o_ref, bt, sem, *, ngroup, nh, half):
    group = where[0]
    core = where[1]
    npair = ngroup // 2
    rows = bt.shape[0] // 2

    @pl.when(pl.program_id(0) == 0)
    def _():
        copies = [pltpu.make_async_copy(near_hbm, bt.at[:, ngroup * LANES:], sem.at[2 * ngroup])]
        for s in range(ngroup):
            cols = slice(s * LANES, (s + 1) * LANES)
            for d, ref in ((0, mine), (1, theirs)):
                at = pl.multiple_of(jnp.where(core == d, 0, 1) * rows, rows)
                copies.append(
                    pltpu.make_async_copy(ref.at[group ^ s], bt.at[pl.ds(at, rows), cols], sem.at[2 * s + d])
                )
        for c in copies:
            c.start()
        for c in copies:
            c.wait()

    res = jnp.dot(w_ref[...], bt[...], preferred_element_type=jnp.float32)
    slot = (lax.broadcasted_iota(jnp.int32, (res.shape[0], LANES), 1) // half) % 2
    for s in range(ngroup):
        far = res[:, s * LANES:(s + 1) * LANES]
        for h in range(nh):
            first = pltpu.roll(far, LANES - half * h, 1) if h else far
            at = (ngroup + h * npair + s // 2) * LANES
            second = res[:, at:at + LANES]
            if s % 2 == 0:
                second = pltpu.roll(second, half, 1)
            tile = jnp.where(slot == 0, first, second).astype(jnp.bfloat16)
            col = pl.multiple_of(((group ^ s) * nh + h) * LANES, LANES)
            o_ref[:, pl.ds(col, LANES)] = tile


def product(where, w, mine, theirs, near, half, snap):
    m, k = w.shape
    ngroup = mine.shape[0]
    mb = 384
    return pl.pallas_call(
        functools.partial(product_kernel, ngroup=ngroup, nh=snap // (ngroup * LANES), half=half),
        out_shape=jax.ShapeDtypeStruct((m, snap), jnp.bfloat16),
        grid_spec=pltpu.PrefetchScalarGridSpec(
            num_scalar_prefetch=1,
            grid=(m // mb,),
            in_specs=[pl.BlockSpec((mb, k), lambda i, c: (i, 0))]
            + [pl.BlockSpec(memory_space=pltpu.VMEM)] * 3,
            out_specs=pl.BlockSpec((mb, snap), lambda i, c: (i, 0)),
            scratch_shapes=[
                pltpu.VMEM((k, snap), jnp.bfloat16),
                pltpu.SemaphoreType.DMA((2 * ngroup + 1,)),
            ],
        ),
        compiler_params=pltpu.CompilerParams(
            dimension_semantics=("arbitrary",), vmem_limit_bytes=36 << 20
        ),
        name="product",
    )(where, w, mine, theirs, near)


def body(snapshots, bnd_index, recovery, block_se, connect, stress_mat):
    ngroup = lax.axis_size("group")
    nrow = lax.axis_size("row")
    nse = bnd_index.shape[0] // ngroup
    nblk, blk, nb = recovery.shape
    nel, nc, ndof = stress_mat.shape
    tper = snapshots.shape[0]
    half = tper // 2
    snap = tper * ngroup * nrow
    group = lax.axis_index("group")
    core = lax.axis_index("row") % 2
    swap = lambda s: [(i, i ^ s) for i in range(ngroup)]
    other = [(i, i ^ 1) for i in range(nrow)]

    top = snapshots[:half]
    bottom = snapshots[half:]
    row = lax.axis_index("row")
    nz = nrow // 2
    along = lambda s: [(i, (i + 2 * s) % nrow) for i in range(nrow)]
    to_other = lambda x: lax.ppermute(x, "row", other)
    tops = [top] + [lax.ppermute(top, "row", along(s)) for s in range(1, nz)]
    top_other = to_other(top)
    along_group = [bottom] + [lax.ppermute(bottom, "group", swap(s)) for s in range(1, ngroup)]

    ends = nrow - 1
    up = [(i, i + 1) for i in range(ends)]
    down = [(i + 1, i) for i in range(ends)]

    def with_se(part, se, first):
        row_id = lax.broadcasted_iota(jnp.int32, part.shape, 0) - first
        return jnp.where((row_id >= 0) & (row_id < 16), se.astype(part.dtype), part)

    last_rows = with_se(recovery[nblk - 1, blk - HW - 16:], block_se[nblk - 1], 0)
    first_rows = with_se(recovery[0, :HW + 16], block_se[0], HW)

    ngrp = nel // SUB
    conn = connect.T.reshape(ndof, ngrp, SUB).transpose(1, 0, 2).reshape(ngrp, ndof * SUB)
    flat = conn.reshape(-1) * (nb // LANES + 1)
    where = jnp.stack([group, core]).astype(jnp.int32)
    sender = (row - 2 * jnp.arange(nz, dtype=jnp.int32)) % nrow
    slots = jnp.concatenate([sender, sender ^ 1]).astype(jnp.int32)

    rows = nse * nb // 2
    parted = bnd_index.reshape(ngroup, 2, rows)
    own_idx = lax.dynamic_index_in_dim(parted, group, 0, keepdims=False).reshape(-1)
    far_idx = lax.dynamic_index_in_dim(parted, core, 1, keepdims=False).reshape(-1)

    own_idx, far_idx, flat, conn, where, slots = lax.optimization_barrier(
        (own_idx, far_idx, flat, conn, where, slots)
    )
    picked = pick_near(own_idx, along_group)
    picked, far_idx, last_rows, first_rows, stress_mat, *tops = lax.optimization_barrier(
        (picked, far_idx, last_rows, first_rows, stress_mat, *tops)
    )
    near_other = to_other(picked)
    smat = stress_mat.transpose(1, 2, 0).astype(jnp.float32).reshape(nc, ndof, ngrp, SUB)
    smat = smat.transpose(0, 2, 1, 3).reshape(nc, ngrp, ndof * SUB)
    head = lax.ppermute(last_rows, "row", up)
    tail = lax.ppermute(first_rows, "row", down)
    nears = [picked] + [lax.ppermute(picked, "row", along(s)) for s in range(1, nz)]
    tops = tops + [top_other] + [to_other(x) for x in tops[1:]]
    per = LANES // tper
    order = [per * h + j for j in range(per) for h in range(nrow // per)]
    far = pick_far(far_idx, slots, tops, order)
    mine = lax.all_to_all(far.reshape(ngroup, rows, LANES), "group", split_axis=0, concat_axis=0, tiled=True)
    flat, far = lax.optimization_barrier((flat, far))
    w = combine(flat, block_se, conn, smat, recovery, head, tail, nse)
    mine, nears, w = lax.optimization_barrier((mine, nears, w))
    nears = nears + [near_other] + [to_other(x) for x in nears[1:]]
    mine, nears = lax.optimization_barrier((mine, nears))
    theirs = to_other(mine)
    near = arrange(slots, nears, ngroup, tper, nse * nb)
    out = product(where, w.reshape(nc * nel, nse * nb), mine, theirs, near, half, snap)
    return out.reshape(nc, nel, snap).transpose(1, 0, 2)


def solution(mesh):
    in_specs = (
        P(("group", "row"), None),
        P(),
        P(("group", "row"), None, None),
        P(("group", "row")),
        P(("group", "row"), None),
        P(("group", "row"), None, None),
    )
    out_specs = P(("group", "row"), None, None)
    return jax.shard_map(body, mesh=mesh, in_specs=in_specs, out_specs=out_specs, check_vma=False)
```

```python
import functools

import jax
import jax.numpy as jnp
from jax import lax
from jax.experimental import pallas as pl
from jax.experimental.pallas import tpu as pltpu
from jax.sharding import PartitionSpec as P

HW = 256
SUB = 8
LANES = 128


def combine_kernel(
    conn, se, grow_ref, s_ref, rec_hbm, head_ref, tail_ref, w_ref, tbl, buf, sem, g0, g1, g2, g3,
    *, nfill, blk, nlt, nse, nc, ndof, inner, ts, gs, nbuf
):
    step = pl.program_id(0)
    rows = SUB * ndof
    steps = pl.num_programs(0) - nfill

    def fetch(b):
        return pltpu.make_async_copy(rec_hbm.at[b], buf.at[b % nbuf], sem.at[b % nbuf])

    def fill(src, base, count):
        def one(i, carry):
            at = pl.multiple_of(i * 16, 16)
            for j in range(nlt):
                part = src[pl.ds(at, 16), j * LANES:(j + 1) * LANES].astype(jnp.float32)
                tbl[pl.ds((base + at) * ts + j, 16, stride=ts), :] = part
            return carry

        lax.fori_loop(0, count // 16, one, 0, unroll=4)

    def gather(group, dst, lo=0, hi=rows):
        first = group * rows
        for q in range(lo, hi):
            dst[pl.ds(q, nlt, stride=gs), :] = tbl[pl.ds(conn[first + q], nlt), :]

    own = (
        lax.broadcasted_iota(jnp.int32, (SUB, rows), 1) % SUB
        == lax.broadcasted_iota(jnp.int32, (SUB, rows), 0)
    )

    def halo_tag(ref, at):
        wide = -(-rows // LANES) * LANES
        return ref[at:at + 16, :wide].astype(jnp.float32)[:1, :rows].astype(jnp.int32)

    head_tag = halo_tag(head_ref, 0)
    tail_tag = halo_tag(tail_ref, HW)

    def left(i):
        where = (grow_ref[pl.ds(i, 1), :] + (blk - HW)) // blk
        tag = jnp.where(where == 0, head_tag, tail_tag)
        for b in range(nfill):
            tag = jnp.where(where == b + 1, se[b], tag)
        tag = jnp.where(own, jnp.broadcast_to(tag, (SUB, rows)), -1)
        parts = []
        for s in range(nse):
            hit = tag == s
            for c in range(nc):
                parts.append(jnp.where(hit, jnp.broadcast_to(s_ref[c, pl.ds(i, 1), :], (SUB, rows)), 0.0))
        return jnp.concatenate(parts, axis=0).astype(jnp.bfloat16)

    def matmul(first, i, srcs, nxt, dsts):
        lhs = [left(first + i), left(first + i + 1)]
        at = pl.multiple_of(i * SUB, 2 * SUB)
        for j in range(0, nlt, 2):
            res = []
            for t in range(2):
                src = srcs[t]
                rhs = jnp.concatenate(
                    [src[(j + d) * gs:(j + d) * gs + rows, :].astype(jnp.bfloat16) for d in range(2)], axis=1
                )
                res.append(jnp.dot(lhs[t], rhs, preferred_element_type=jnp.float32))
                gather(nxt + t, dsts[t], rows * j // nlt, rows * (j + 2) // nlt)
            for s in range(nse):
                col = (s * nlt + j) * LANES
                for c in range(nc):
                    r0 = (s * nc + c) * SUB
                    both = jnp.concatenate([r[r0:r0 + SUB] for r in res], axis=0)
                    w_ref[c, pl.ds(at, 2 * SUB), col:col + 2 * LANES] = both.astype(jnp.bfloat16)

    @pl.when(step == 0)
    def _():
        for b in range(nbuf):
            fetch(b).start()
        fill(head_ref.at[pl.ds(16, HW)], 0, HW)
        fill(tail_ref, HW + nfill * blk, HW)

    @pl.when(step < nfill)
    def _():
        fetch(step).wait()
        fill(buf.at[step % nbuf], HW + step * blk, blk)

        @pl.when(step + nbuf < nfill)
        def _():
            fetch(step + nbuf).start()

    @pl.when(step >= nfill)
    def _():
        base = (step - nfill) * inner
        last = steps * inner - 2

        @pl.when(step == nfill)
        def _():
            gather(0, g0)
            gather(1, g1)

        def four(i, carry):
            n = base + 4 * i
            matmul(base, 4 * i, (g0, g1), n + 2, (g2, g3))
            matmul(base, 4 * i + 2, (g2, g3), jnp.minimum(n + 4, last), (g0, g1))
            return carry

        lax.fori_loop(0, inner // 4, four, 0)


def combine(conn, se, grow, smat, recovery, head, tail, nse, inner=4, nbuf=6):
    nblk, blk, nb = recovery.shape
    ngrp, rows = grow.shape
    nel = ngrp * SUB
    ndof = rows // SUB
    nc = smat.shape[0]
    nlt = nb // LANES
    steps = ngrp // inner
    ts = nlt + 1
    gs = rows + 1
    kern = functools.partial(
        combine_kernel, nfill=nblk, blk=blk, nlt=nlt, nse=nse, nc=nc, ndof=ndof, inner=inner, ts=ts, gs=gs,
        nbuf=nbuf,
    )
    later = lambda i: jnp.maximum(i - nblk, 0)
    return pl.pallas_call(
        kern,
        out_shape=jax.ShapeDtypeStruct((nc, nel, nse * nb), jnp.bfloat16),
        grid_spec=pltpu.PrefetchScalarGridSpec(
            num_scalar_prefetch=2,
            grid=(nblk + steps,),
            in_specs=[
                pl.BlockSpec((ngrp, rows), lambda i, c, s: (0, 0)),
                pl.BlockSpec((nc, ngrp, rows), lambda i, c, s: (0, 0, 0)),
                pl.BlockSpec(memory_space=pl.ANY),
                pl.BlockSpec((HW + 16, nb), lambda i, c, s: (0, 0)),
                pl.BlockSpec((HW + 16, nb), lambda i, c, s: (0, 0)),
            ],
            out_specs=pl.BlockSpec((nc, SUB * inner, nse * nb), lambda i, c, s: (0, later(i), 0)),
            scratch_shapes=[
                pltpu.VMEM(((nblk * blk + 2 * HW) * ts, LANES), jnp.float32),
                pltpu.VMEM((nbuf, blk, nb), jnp.bfloat16),
                pltpu.SemaphoreType.DMA((nbuf,)),
            ] + [pltpu.VMEM((gs * nlt, LANES), jnp.float32)] * 4,
        ),
        compiler_params=pltpu.CompilerParams(dimension_semantics=("arbitrary",), vmem_limit_bytes=60 << 20),
        cost_estimate=pl.CostEstimate(flops=30 * 10**9, bytes_accessed=120 << 20, transcendentals=0),
        name="combine",
    )(conn, se, grow, smat, recovery, head, tail)


def pick_near_kernel(idx, src, o_ref, tbl, *bufs, parts, chunk):
    step = pl.program_id(0)
    nd = tbl.shape[0]
    total = chunk * pl.num_programs(0)

    @pl.when(step == 0)
    def _():
        def one(i, carry):
            at = pl.multiple_of(i * LANES, LANES)
            rows = jnp.concatenate([src[g, :, pl.ds(at, LANES)] for g in range(src.shape[0])] * parts, axis=0)
            tbl[pl.ds(at, LANES), :] = rows.T.astype(jnp.float32)
            return carry

        lax.fori_loop(0, nd // LANES, one, 0, unroll=2)

    def some(i, carry):
        at = pl.multiple_of(i * 64, 64)
        for p in range(parts):
            for q in range(64):
                k = idx[p * total + step * chunk + at + q]
                bufs[p][pl.ds(at + q, 1), :] = tbl[pl.ds(k, 1), :]
        return carry

    lax.fori_loop(0, chunk // 64, some, 0)
    piece = lax.broadcasted_iota(jnp.int32, (chunk, LANES), 1) // (LANES // parts)
    out = bufs[0][...]
    for p in range(1, parts):
        out = jnp.where(piece == p, bufs[p][...], out)
    o_ref[...] = out.astype(jnp.bfloat16)


def pick_near(idx, src):
    ngroup, half, nd = src.shape
    parts = LANES // (half * ngroup)
    n = idx.shape[0] // parts
    chunk = min(n, 1024)
    return pl.pallas_call(
        functools.partial(pick_near_kernel, parts=parts, chunk=chunk),
        out_shape=jax.ShapeDtypeStruct((n, LANES), jnp.bfloat16),
        grid_spec=pltpu.PrefetchScalarGridSpec(
            num_scalar_prefetch=1,
            grid=(n // chunk,),
            in_specs=[pl.BlockSpec((ngroup, half, nd), lambda i, c: (0, 0, 0))],
            out_specs=pl.BlockSpec((chunk, LANES), lambda i, c: (i, 0)),
            scratch_shapes=[pltpu.VMEM((nd, LANES), jnp.float32)]
            + [pltpu.VMEM((chunk, LANES), jnp.float32) for _ in range(parts)],
        ),
        compiler_params=pltpu.CompilerParams(
            dimension_semantics=("arbitrary",), vmem_limit_bytes=40 << 20
        ),
        name="pick_near",
    )(idx, src)


def pick_far_kernel(idx, slots, *refs, nsrc, order, chunk):
    srcs = refs[:nsrc]
    o_ref, src, tbl, buf, sem = refs[nsrc:]
    step = pl.program_id(0)
    nd = tbl.shape[0]

    @pl.when(step == 0)
    def _():
        copies = [
            pltpu.make_async_copy(ref, src.at[slots[i]], sem.at[i]) for i, ref in enumerate(srcs)
        ]
        for copy in copies:
            copy.start()
        for copy in copies:
            copy.wait()

        def one(i, carry):
            at = pl.multiple_of(i * LANES, LANES)
            rows = jnp.concatenate([src[r, :, pl.ds(at, LANES)] for r in order], axis=0)
            tbl[pl.ds(at, LANES), :] = rows.T.astype(jnp.float32)
            return carry

        lax.fori_loop(0, nd // LANES, one, 0, unroll=2)

    def some(i, carry):
        at = pl.multiple_of(i * 64, 64)
        for q in range(64):
            buf[pl.ds(at + q, 1), :] = tbl[pl.ds(idx[step * chunk + at + q], 1), :]
        return carry

    lax.fori_loop(0, chunk // 64, some, 0)
    o_ref[...] = buf[...].astype(jnp.bfloat16)


def pick_far(idx, slots, srcs, order):
    nrow = len(srcs)
    half, nd = srcs[0].shape
    n = idx.shape[0]
    chunk = min(n, 1024)
    return pl.pallas_call(
        functools.partial(pick_far_kernel, nsrc=nrow, order=order, chunk=chunk),
        out_shape=jax.ShapeDtypeStruct((n, LANES), jnp.bfloat16),
        grid_spec=pltpu.PrefetchScalarGridSpec(
            num_scalar_prefetch=2,
            grid=(n // chunk,),
            in_specs=[pl.BlockSpec(memory_space=pltpu.VMEM)] * nrow,
            out_specs=pl.BlockSpec((chunk, LANES), lambda i, c, d: (i, 0)),
            scratch_shapes=[
                pltpu.VMEM((nrow, half, nd), jnp.bfloat16),
                pltpu.VMEM((nd, LANES), jnp.float32),
                pltpu.VMEM((chunk, LANES), jnp.float32),
                pltpu.SemaphoreType.DMA((nrow,)),
            ],
        ),
        compiler_params=pltpu.CompilerParams(
            dimension_semantics=("arbitrary",), vmem_limit_bytes=40 << 20
        ),
        name="pick_far",
    )(idx, slots, *srcs)


def arrange_kernel(slots, *refs, nsrc, nh, per, npair, parts, tper):
    srcs = refs[:nsrc]
    o_ref, near, sem = refs[nsrc:]
    step_rows = o_ref.shape[1]
    step = pl.program_id(0)

    @pl.when(step == 0)
    def _():
        copies = [
            pltpu.make_async_copy(ref, near.at[slots[i]], sem.at[i]) for i, ref in enumerate(srcs)
        ]
        for copy in copies:
            copy.start()
        for copy in copies:
            copy.wait()

    lane = lax.broadcasted_iota(jnp.int32, (step_rows, LANES), 1) // tper
    at = pl.multiple_of(step * step_rows, step_rows)
    for h in range(nh):
        got = [near[h * per + j, pl.ds(at, step_rows), :].astype(jnp.float32) for j in range(per)]
        for p in range(npair):
            for kp in range(parts):
                tile = None
                for j in range(per):
                    shift = (tper * j - (kp * (LANES // parts) + tper * p)) % LANES
                    moved = pltpu.roll(got[j], shift, 1) if shift else got[j]
                    tile = moved if tile is None else jnp.where(lane == j, moved, tile)
                col = (h * npair + p) * LANES
                o_ref[kp, :, col:col + LANES] = tile.astype(jnp.bfloat16)


def arrange(slots, srcs, ngroup, tper, k):
    nrow = len(srcs)
    nk = srcs[0].shape[0]
    nh = tper * nrow // LANES
    npair = ngroup // 2
    parts = k // nk
    cols = nh * npair * LANES
    step_rows = min(nk, 256)
    out = pl.pallas_call(
        functools.partial(
            arrange_kernel, nsrc=nrow, nh=nh, per=LANES // tper, npair=npair, parts=parts, tper=tper
        ),
        out_shape=jax.ShapeDtypeStruct((parts, nk, cols), jnp.bfloat16),
        grid_spec=pltpu.PrefetchScalarGridSpec(
            num_scalar_prefetch=1,
            grid=(nk // step_rows,),
            in_specs=[pl.BlockSpec(memory_space=pltpu.VMEM)] * nrow,
            out_specs=pl.BlockSpec((parts, step_rows, cols), lambda i, c: (0, i, 0)),
            scratch_shapes=[
                pltpu.VMEM((nrow, nk, LANES), jnp.bfloat16),
                pltpu.SemaphoreType.DMA((nrow,)),
            ],
        ),
        compiler_params=pltpu.CompilerParams(
            dimension_semantics=("arbitrary",), vmem_limit_bytes=40 << 20
        ),
        name="arrange",
    )(slots, *srcs)
    return out.reshape(k, cols)


def product_kernel(core, w_ref, mine, theirs, near_hbm, o_ref, bt, sem, *, ngroup, nh, half):
    npair = ngroup // 2
    rows = bt.shape[0] // 2

    @pl.when(pl.program_id(0) == 0)
    def _():
        copies = [pltpu.make_async_copy(near_hbm, bt.at[:, ngroup * LANES:], sem.at[2 * ngroup])]
        for s in range(ngroup):
            cols = slice(s * LANES, (s + 1) * LANES)
            for d, ref in ((0, mine), (1, theirs)):
                at = pl.multiple_of(jnp.where(core[0] == d, 0, 1) * rows, rows)
                copies.append(
                    pltpu.make_async_copy(ref.at[s], bt.at[pl.ds(at, rows), cols], sem.at[2 * s + d])
                )
        for c in copies:
            c.start()
        for c in copies:
            c.wait()

    res = jnp.dot(w_ref[...], bt[...], preferred_element_type=jnp.float32)
    slot = (lax.broadcasted_iota(jnp.int32, (res.shape[0], LANES), 1) // half) % 2
    for s in range(ngroup):
        far = res[:, s * LANES:(s + 1) * LANES]
        for h in range(nh):
            first = pltpu.roll(far, LANES - half * h, 1) if h else far
            at = (ngroup + h * npair + s // 2) * LANES
            second = res[:, at:at + LANES]
            if s % 2 == 0:
                second = pltpu.roll(second, half, 1)
            tile = jnp.where(slot == 0, first, second).astype(jnp.bfloat16)
            col = (s * nh + h) * LANES
            o_ref[:, col:col + LANES] = tile


def product(where, w, mine, theirs, near, half, snap):
    m, k = w.shape
    ngroup = mine.shape[0]
    mb = 384
    return pl.pallas_call(
        functools.partial(product_kernel, ngroup=ngroup, nh=snap // (ngroup * LANES), half=half),
        out_shape=jax.ShapeDtypeStruct((m, snap), jnp.bfloat16),
        grid_spec=pltpu.PrefetchScalarGridSpec(
            num_scalar_prefetch=1,
            grid=(m // mb,),
            in_specs=[pl.BlockSpec((mb, k), lambda i, c: (i, 0))]
            + [pl.BlockSpec(memory_space=pltpu.VMEM)] * 3,
            out_specs=pl.BlockSpec((mb, snap), lambda i, c: (i, 0)),
            scratch_shapes=[
                pltpu.VMEM((k, snap), jnp.bfloat16),
                pltpu.SemaphoreType.DMA((2 * ngroup + 1,)),
            ],
        ),
        compiler_params=pltpu.CompilerParams(
            dimension_semantics=("arbitrary",), vmem_limit_bytes=36 << 20
        ),
        name="product",
    )(where, w, mine, theirs, near)


def body(snapshots, bnd_index, recovery, block_se, connect, stress_mat):
    ngroup = lax.axis_size("group")
    nrow = lax.axis_size("row")
    nse = bnd_index.shape[0] // ngroup
    nblk, blk, nb = recovery.shape
    nel, nc, ndof = stress_mat.shape
    tper = snapshots.shape[0]
    half = tper // 2
    snap = tper * ngroup * nrow
    group = lax.axis_index("group")
    core = lax.axis_index("row") % 2
    other = [(i, i ^ 1) for i in range(nrow)]

    top = snapshots[:half]
    bottom = snapshots[half:]
    row = lax.axis_index("row")
    nz = nrow // 2
    along = lambda s: [(i, (i + 2 * s) % nrow) for i in range(nrow)]
    to_other = lambda x: lax.ppermute(x, "row", other)
    tops = [top] + [lax.ppermute(top, "row", along(s)) for s in range(1, nz)]
    top_other = to_other(top)
    along_group = lax.all_to_all(
        jnp.broadcast_to(bottom, (ngroup, *bottom.shape)), "group", split_axis=0, concat_axis=0, tiled=True
    )

    ends = nrow - 1
    up = [(i, i + 1) for i in range(ends)]
    down = [(i + 1, i) for i in range(ends)]

    def with_se(part, se, first):
        row_id = lax.broadcasted_iota(jnp.int32, part.shape, 0) - first
        return jnp.where((row_id >= 0) & (row_id < 16), se.astype(part.dtype), part)

    last_rows = with_se(recovery[nblk - 1, blk - HW - 16:], block_se[nblk - 1], 0)
    first_rows = with_se(recovery[0, :HW + 16], block_se[0], HW)

    ngrp = nel // SUB
    conn = connect.T.reshape(ndof, ngrp, SUB).transpose(1, 0, 2).reshape(ngrp, ndof * SUB)
    smat = stress_mat.transpose(1, 2, 0).astype(jnp.float32).reshape(nc, ndof, ngrp, SUB)
    smat = smat.transpose(0, 2, 1, 3).reshape(nc, ngrp, ndof * SUB)
    flat = conn.reshape(-1) * (nb // LANES + 1)
    where = core.reshape(1).astype(jnp.int32)
    sender = (row - 2 * jnp.arange(nz, dtype=jnp.int32)) % nrow
    slots = jnp.concatenate([sender, sender ^ 1]).astype(jnp.int32)

    rows = nse * nb // 2
    parted = bnd_index.reshape(ngroup, 2, rows)
    own_idx = lax.dynamic_index_in_dim(parted, group, 0, keepdims=False).reshape(-1)
    far_idx = lax.dynamic_index_in_dim(parted, core, 1, keepdims=False).reshape(-1)

    own_idx, far_idx, flat, conn, smat, where, slots, last_rows, first_rows = lax.optimization_barrier(
        (own_idx, far_idx, flat, conn, smat, where, slots, last_rows, first_rows)
    )
    picked = pick_near(own_idx, along_group)
    picked, far_idx, last_rows, first_rows, *tops = lax.optimization_barrier(
        (picked, far_idx, last_rows, first_rows, *tops)
    )
    near_other = to_other(picked)
    head = lax.ppermute(last_rows, "row", up)
    tail = lax.ppermute(first_rows, "row", down)
    nears = [picked] + [lax.ppermute(picked, "row", along(s)) for s in range(1, nz)]
    tops = tops + [top_other] + [to_other(x) for x in tops[1:]]
    per = LANES // tper
    order = [per * h + j for j in range(per) for h in range(nrow // per)]
    far = pick_far(far_idx, slots, tops, order)
    mine = lax.all_to_all(far.reshape(ngroup, rows, LANES), "group", split_axis=0, concat_axis=0, tiled=True)
    flat, far = lax.optimization_barrier((flat, far))
    w = combine(flat, block_se, conn, smat, recovery, head, tail, nse)
    mine, nears, w = lax.optimization_barrier((mine, nears, w))
    nears = nears + [near_other] + [to_other(x) for x in nears[1:]]
    mine, nears = lax.optimization_barrier((mine, nears))
    theirs = to_other(mine)
    near = arrange(slots, nears, ngroup, tper, nse * nb)
    out = product(where, w.reshape(nc * nel, nse * nb), mine, theirs, near, half, snap)
    return out.reshape(nc, nel, snap).transpose(1, 0, 2)


def solution(mesh):
    in_specs = (
        P(("group", "row"), None),
        P(),
        P(("group", "row"), None, None),
        P(("group", "row")),
        P(("group", "row"), None),
        P(("group", "row"), None, None),
    )
    out_specs = P(("group", "row"), None, None)
    return jax.shard_map(body, mesh=mesh, in_specs=in_specs, out_specs=out_specs, check_vma=False)
```

```python
import functools

import jax
import jax.numpy as jnp
from jax import lax
from jax.experimental import pallas as pl
from jax.experimental.pallas import tpu as pltpu
from jax.sharding import PartitionSpec as P

HW = 256
SUB = 8
LANES = 128


def combine_kernel(
    conn, se, grow_ref, s_ref, rec_hbm, head_ref, tail_ref, w_ref, tbl, buf, sem, g0, g1, g2, g3,
    *, nfill, blk, nlt, nse, nc, ndof, inner, ts, gs, nbuf
):
    step = pl.program_id(0)
    rows = SUB * ndof
    steps = pl.num_programs(0) - nfill

    def fetch(b):
        return pltpu.make_async_copy(rec_hbm.at[b], buf.at[b % nbuf], sem.at[b % nbuf])

    def fill(src, base, count):
        def one(i, carry):
            at = pl.multiple_of(i * 16, 16)
            for j in range(nlt):
                part = src[pl.ds(at, 16), j * LANES:(j + 1) * LANES].astype(jnp.float32)
                tbl[pl.ds((base + at) * ts + j, 16, stride=ts), :] = part
            return carry

        lax.fori_loop(0, count // 16, one, 0, unroll=4)

    def gather(group, dst, lo=0, hi=rows):
        first = group * rows
        for q in range(lo, hi):
            dst[pl.ds(q, nlt, stride=gs), :] = tbl[pl.ds(conn[first + q], nlt), :]

    own = (
        lax.broadcasted_iota(jnp.int32, (SUB, rows), 1) % SUB
        == lax.broadcasted_iota(jnp.int32, (SUB, rows), 0)
    )

    def halo_tag(ref, at):
        wide = -(-rows // LANES) * LANES
        return ref[at:at + 16, :wide].astype(jnp.float32)[:1, :rows].astype(jnp.int32)

    head_tag = halo_tag(head_ref, 0)
    tail_tag = halo_tag(tail_ref, HW)

    def left(i):
        where = (grow_ref[pl.ds(i, 1), :] + (blk - HW)) // blk
        tag = jnp.where(where == 0, head_tag, tail_tag)
        for b in range(nfill):
            tag = jnp.where(where == b + 1, se[b], tag)
        tag = jnp.where(own, jnp.broadcast_to(tag, (SUB, rows)), -1)
        parts = []
        for s in range(nse):
            hit = tag == s
            for c in range(nc):
                parts.append(jnp.where(hit, jnp.broadcast_to(s_ref[c, pl.ds(i, 1), :], (SUB, rows)), 0.0))
        return jnp.concatenate(parts, axis=0).astype(jnp.bfloat16)

    def matmul(first, i, srcs, nxt, dsts):
        lhs = [left(first + i), left(first + i + 1)]
        at = pl.multiple_of(i * SUB, 2 * SUB)
        for j in range(0, nlt, 2):
            res = []
            for t in range(2):
                src = srcs[t]
                rhs = jnp.concatenate(
                    [src[(j + d) * gs:(j + d) * gs + rows, :].astype(jnp.bfloat16) for d in range(2)], axis=1
                )
                res.append(jnp.dot(lhs[t], rhs, preferred_element_type=jnp.float32))
                gather(nxt + t, dsts[t], rows * j // nlt, rows * (j + 2) // nlt)
            for s in range(nse):
                col = (s * nlt + j) * LANES
                for c in range(nc):
                    r0 = (s * nc + c) * SUB
                    both = jnp.concatenate([r[r0:r0 + SUB] for r in res], axis=0)
                    w_ref[c, pl.ds(at, 2 * SUB), col:col + 2 * LANES] = both.astype(jnp.bfloat16)

    @pl.when(step == 0)
    def _():
        for b in range(nbuf):
            fetch(b).start()
        fill(head_ref.at[pl.ds(16, HW)], 0, HW)
        fill(tail_ref, HW + nfill * blk, HW)

    @pl.when(step < nfill)
    def _():
        fetch(step).wait()
        fill(buf.at[step % nbuf], HW + step * blk, blk)

        @pl.when(step + nbuf < nfill)
        def _():
            fetch(step + nbuf).start()

    @pl.when(step >= nfill)
    def _():
        base = (step - nfill) * inner
        last = steps * inner - 2

        @pl.when(step == nfill)
        def _():
            gather(0, g0)
            gather(1, g1)

        def four(i, carry):
            n = base + 4 * i
            matmul(base, 4 * i, (g0, g1), n + 2, (g2, g3))
            matmul(base, 4 * i + 2, (g2, g3), jnp.minimum(n + 4, last), (g0, g1))
            return carry

        lax.fori_loop(0, inner // 4, four, 0)


def combine(conn, se, grow, smat, recovery, head, tail, nse, inner=4, nbuf=6):
    nblk, blk, nb = recovery.shape
    ngrp, rows = grow.shape
    nel = ngrp * SUB
    ndof = rows // SUB
    nc = smat.shape[0]
    nlt = nb // LANES
    steps = ngrp // inner
    ts = nlt + 1
    gs = rows + 1
    kern = functools.partial(
        combine_kernel, nfill=nblk, blk=blk, nlt=nlt, nse=nse, nc=nc, ndof=ndof, inner=inner, ts=ts, gs=gs,
        nbuf=nbuf,
    )
    later = lambda i: jnp.maximum(i - nblk, 0)
    return pl.pallas_call(
        kern,
        out_shape=jax.ShapeDtypeStruct((nc, nel, nse * nb), jnp.bfloat16),
        grid_spec=pltpu.PrefetchScalarGridSpec(
            num_scalar_prefetch=2,
            grid=(nblk + steps,),
            in_specs=[
                pl.BlockSpec((ngrp, rows), lambda i, c, s: (0, 0)),
                pl.BlockSpec((nc, ngrp, rows), lambda i, c, s: (0, 0, 0)),
                pl.BlockSpec(memory_space=pl.ANY),
                pl.BlockSpec((HW + 16, nb), lambda i, c, s: (0, 0)),
                pl.BlockSpec((HW + 16, nb), lambda i, c, s: (0, 0)),
            ],
            out_specs=pl.BlockSpec((nc, SUB * inner, nse * nb), lambda i, c, s: (0, later(i), 0)),
            scratch_shapes=[
                pltpu.VMEM(((nblk * blk + 2 * HW) * ts, LANES), jnp.float32),
                pltpu.VMEM((nbuf, blk, nb), jnp.bfloat16),
                pltpu.SemaphoreType.DMA((nbuf,)),
            ] + [pltpu.VMEM((gs * nlt, LANES), jnp.float32)] * 4,
        ),
        compiler_params=pltpu.CompilerParams(dimension_semantics=("arbitrary",), vmem_limit_bytes=60 << 20),
        cost_estimate=pl.CostEstimate(flops=30 * 10**9, bytes_accessed=120 << 20, transcendentals=0),
        name="combine",
    )(conn, se, grow, smat, recovery, head, tail)


def pick_near_kernel(idx, src, grow_hbm, smat_hbm, o_ref, tbl, *bufs, parts, chunk):
    step = pl.program_id(0)
    nd = tbl.shape[0]
    total = chunk * pl.num_programs(0)

    @pl.when(step == 0)
    def _():
        def one(i, carry):
            at = pl.multiple_of(i * LANES, LANES)
            rows = jnp.concatenate([src[g, :, pl.ds(at, LANES)] for g in range(src.shape[0])] * parts, axis=0)
            tbl[pl.ds(at, LANES), :] = rows.T.astype(jnp.float32)
            return carry

        lax.fori_loop(0, nd // LANES, one, 0, unroll=2)

    def some(i, carry):
        at = pl.multiple_of(i * 64, 64)
        for p in range(parts):
            for q in range(64):
                k = idx[p * total + step * chunk + at + q]
                bufs[p][pl.ds(at + q, 1), :] = tbl[pl.ds(k, 1), :]
        return carry

    lax.fori_loop(0, chunk // 64, some, 0)
    piece = lax.broadcasted_iota(jnp.int32, (chunk, LANES), 1) // (LANES // parts)
    out = bufs[0][...]
    for p in range(1, parts):
        out = jnp.where(piece == p, bufs[p][...], out)
    o_ref[...] = out.astype(jnp.bfloat16)


def pick_near(idx, src, grow, smat):
    ngroup, half, nd = src.shape
    parts = LANES // (half * ngroup)
    n = idx.shape[0] // parts
    chunk = min(n, 1024)
    return pl.pallas_call(
        functools.partial(pick_near_kernel, parts=parts, chunk=chunk),
        out_shape=jax.ShapeDtypeStruct((n, LANES), jnp.bfloat16),
        grid_spec=pltpu.PrefetchScalarGridSpec(
            num_scalar_prefetch=1,
            grid=(n // chunk,),
            in_specs=[
                pl.BlockSpec((ngroup, half, nd), lambda i, c: (0, 0, 0)),
                pl.BlockSpec(memory_space=pl.ANY),
                pl.BlockSpec(memory_space=pl.ANY),
            ],
            out_specs=pl.BlockSpec((chunk, LANES), lambda i, c: (i, 0)),
            scratch_shapes=[pltpu.VMEM((nd, LANES), jnp.float32)]
            + [pltpu.VMEM((chunk, LANES), jnp.float32) for _ in range(parts)],
        ),
        compiler_params=pltpu.CompilerParams(
            dimension_semantics=("arbitrary",), vmem_limit_bytes=40 << 20
        ),
        name="pick_near",
    )(idx, src, grow, smat)


def pick_far_kernel(idx, slots, *refs, nsrc, order, chunk):
    srcs = refs[:nsrc]
    o_ref, src, tbl, buf, sem = refs[nsrc:]
    step = pl.program_id(0)
    nd = tbl.shape[0]

    @pl.when(step == 0)
    def _():
        copies = [
            pltpu.make_async_copy(ref, src.at[slots[i]], sem.at[i]) for i, ref in enumerate(srcs)
        ]
        for copy in copies:
            copy.start()
        for copy in copies:
            copy.wait()

        def one(i, carry):
            at = pl.multiple_of(i * LANES, LANES)
            rows = jnp.concatenate([src[r, :, pl.ds(at, LANES)] for r in order], axis=0)
            tbl[pl.ds(at, LANES), :] = rows.T.astype(jnp.float32)
            return carry

        lax.fori_loop(0, nd // LANES, one, 0, unroll=2)

    def some(i, carry):
        at = pl.multiple_of(i * 64, 64)
        for q in range(64):
            buf[pl.ds(at + q, 1), :] = tbl[pl.ds(idx[step * chunk + at + q], 1), :]
        return carry

    lax.fori_loop(0, chunk // 64, some, 0)
    o_ref[...] = buf[...].astype(jnp.bfloat16)


def pick_far(idx, slots, srcs, order):
    nrow = len(srcs)
    half, nd = srcs[0].shape
    n = idx.shape[0]
    chunk = min(n, 1024)
    return pl.pallas_call(
        functools.partial(pick_far_kernel, nsrc=nrow, order=order, chunk=chunk),
        out_shape=jax.ShapeDtypeStruct((n, LANES), jnp.bfloat16),
        grid_spec=pltpu.PrefetchScalarGridSpec(
            num_scalar_prefetch=2,
            grid=(n // chunk,),
            in_specs=[pl.BlockSpec(memory_space=pltpu.VMEM)] * nrow,
            out_specs=pl.BlockSpec((chunk, LANES), lambda i, c, d: (i, 0)),
            scratch_shapes=[
                pltpu.VMEM((nrow, half, nd), jnp.bfloat16),
                pltpu.VMEM((nd, LANES), jnp.float32),
                pltpu.VMEM((chunk, LANES), jnp.float32),
                pltpu.SemaphoreType.DMA((nrow,)),
            ],
        ),
        compiler_params=pltpu.CompilerParams(
            dimension_semantics=("arbitrary",), vmem_limit_bytes=40 << 20
        ),
        name="pick_far",
    )(idx, slots, *srcs)


def arrange_kernel(slots, *refs, nsrc, nh, per, npair, parts, tper):
    srcs = refs[:nsrc]
    o_ref, near, sem = refs[nsrc:]
    step_rows = o_ref.shape[1]
    step = pl.program_id(0)

    cut = near.shape[1] // 2

    def copies(part):
        where = pl.ds(part * cut, cut)
        return [
            pltpu.make_async_copy(ref.at[where], near.at[slots[i], where], sem.at[part, i])
            for i, ref in enumerate(srcs)
        ]

    @pl.when(step == 0)
    def _():
        for copy in copies(0) + copies(1):
            copy.start()
        for copy in copies(0):
            copy.wait()

    @pl.when(step * step_rows == cut)
    def _():
        for copy in copies(1):
            copy.wait()

    lane = lax.broadcasted_iota(jnp.int32, (step_rows, LANES), 1) // tper
    at = pl.multiple_of(step * step_rows, step_rows)
    for h in range(nh):
        got = [near[h * per + j, pl.ds(at, step_rows), :].astype(jnp.float32) for j in range(per)]
        for p in range(npair):
            for kp in range(parts):
                tile = None
                for j in range(per):
                    shift = (tper * j - (kp * (LANES // parts) + tper * p)) % LANES
                    moved = pltpu.roll(got[j], shift, 1) if shift else got[j]
                    tile = moved if tile is None else jnp.where(lane == j, moved, tile)
                col = (h * npair + p) * LANES
                o_ref[kp, :, col:col + LANES] = tile.astype(jnp.bfloat16)


def arrange(slots, srcs, ngroup, tper, k):
    nrow = len(srcs)
    nk = srcs[0].shape[0]
    nh = tper * nrow // LANES
    npair = ngroup // 2
    parts = k // nk
    cols = nh * npair * LANES
    step_rows = min(nk // 2, 256)
    out = pl.pallas_call(
        functools.partial(
            arrange_kernel, nsrc=nrow, nh=nh, per=LANES // tper, npair=npair, parts=parts, tper=tper
        ),
        out_shape=jax.ShapeDtypeStruct((parts, nk, cols), jnp.bfloat16),
        grid_spec=pltpu.PrefetchScalarGridSpec(
            num_scalar_prefetch=1,
            grid=(nk // step_rows,),
            in_specs=[pl.BlockSpec(memory_space=pltpu.VMEM)] * nrow,
            out_specs=pl.BlockSpec((parts, step_rows, cols), lambda i, c: (0, i, 0)),
            scratch_shapes=[
                pltpu.VMEM((nrow, nk, LANES), jnp.bfloat16),
                pltpu.SemaphoreType.DMA((2, nrow)),
            ],
        ),
        compiler_params=pltpu.CompilerParams(
            dimension_semantics=("arbitrary",), vmem_limit_bytes=40 << 20
        ),
        name="arrange",
    )(slots, *srcs)
    return out.reshape(k, cols)


def product_kernel(core, w_ref, mine, theirs, near, o_ref, bt, sem, *, ngroup, nh, half):
    npair = ngroup // 2
    rows = bt.shape[0] // 2

    copies = []
    for s in range(ngroup):
        cols = slice(s * LANES, (s + 1) * LANES)
        for d, ref in ((0, mine), (1, theirs)):
            at = pl.multiple_of(jnp.where(core[0] == d, 0, 1) * rows, rows)
            copies.append(pltpu.make_async_copy(ref.at[s], bt.at[pl.ds(at, rows), cols], sem.at[2 * s + d]))

    @pl.when(pl.program_id(0) == 0)
    def _():
        for c in copies:
            c.start()

    res_near = jnp.dot(w_ref[...], near[...], preferred_element_type=jnp.float32)

    @pl.when(pl.program_id(0) == 0)
    def _():
        for c in copies:
            c.wait()

    res = jnp.dot(w_ref[...], bt[...], preferred_element_type=jnp.float32)
    slot = (lax.broadcasted_iota(jnp.int32, (res.shape[0], LANES), 1) // half) % 2
    for s in range(ngroup):
        far = res[:, s * LANES:(s + 1) * LANES]
        for h in range(nh):
            first = pltpu.roll(far, LANES - half * h, 1) if h else far
            at = (h * npair + s // 2) * LANES
            second = res_near[:, at:at + LANES]
            if s % 2 == 0:
                second = pltpu.roll(second, half, 1)
            tile = jnp.where(slot == 0, first, second).astype(jnp.bfloat16)
            col = (s * nh + h) * LANES
            o_ref[:, col:col + LANES] = tile


def product(where, w, mine, theirs, near, half, snap):
    m, k = w.shape
    ngroup = mine.shape[0]
    mb = 384
    return pl.pallas_call(
        functools.partial(product_kernel, ngroup=ngroup, nh=snap // (ngroup * LANES), half=half),
        out_shape=jax.ShapeDtypeStruct((m, snap), jnp.bfloat16),
        grid_spec=pltpu.PrefetchScalarGridSpec(
            num_scalar_prefetch=1,
            grid=(m // mb,),
            in_specs=[pl.BlockSpec((mb, k), lambda i, c: (i, 0))]
            + [pl.BlockSpec(memory_space=pltpu.VMEM)] * 3,
            out_specs=pl.BlockSpec((mb, snap), lambda i, c: (i, 0)),
            scratch_shapes=[
                pltpu.VMEM((k, ngroup * LANES), jnp.bfloat16),
                pltpu.SemaphoreType.DMA((2 * ngroup,)),
            ],
        ),
        compiler_params=pltpu.CompilerParams(
            dimension_semantics=("arbitrary",), vmem_limit_bytes=36 << 20
        ),
        name="product",
    )(where, w, mine, theirs, near)


def body(snapshots, bnd_index, recovery, block_se, connect, stress_mat):
    ngroup = lax.axis_size("group")
    nrow = lax.axis_size("row")
    nse = bnd_index.shape[0] // ngroup
    nblk, blk, nb = recovery.shape
    nel, nc, ndof = stress_mat.shape
    tper = snapshots.shape[0]
    half = tper // 2
    snap = tper * ngroup * nrow
    group = lax.axis_index("group")
    core = lax.axis_index("row") % 2
    other = [(i, i ^ 1) for i in range(nrow)]

    top = snapshots[:half]
    bottom = snapshots[half:]
    row = lax.axis_index("row")
    nz = nrow // 2
    along = lambda s: [(i, (i + 2 * s) % nrow) for i in range(nrow)]
    to_other = lambda x: lax.ppermute(x, "row", other)
    tops = [top] + [lax.ppermute(top, "row", along(s)) for s in range(1, nz)]
    top_other = to_other(top)
    along_group = lax.all_to_all(
        jnp.broadcast_to(bottom, (ngroup, *bottom.shape)), "group", split_axis=0, concat_axis=0, tiled=True
    )

    ends = nrow - 1
    up = [(i, i + 1) for i in range(ends)]
    down = [(i + 1, i) for i in range(ends)]

    def with_se(part, se, first):
        row_id = lax.broadcasted_iota(jnp.int32, part.shape, 0) - first
        return jnp.where((row_id >= 0) & (row_id < 16), se.astype(part.dtype), part)

    last_rows = with_se(recovery[nblk - 1, blk - HW - 16:], block_se[nblk - 1], 0)
    first_rows = with_se(recovery[0, :HW + 16], block_se[0], HW)

    ngrp = nel // SUB
    conn = connect.T.reshape(ndof, ngrp, SUB).transpose(1, 0, 2).reshape(ngrp, ndof * SUB)
    smat = stress_mat.transpose(1, 2, 0).astype(jnp.float32).reshape(nc, ndof, ngrp, SUB)
    smat = smat.transpose(0, 2, 1, 3).reshape(nc, ngrp, ndof * SUB)
    flat = conn.reshape(-1) * (nb // LANES + 1)
    where = core.reshape(1).astype(jnp.int32)
    sender = (row - 2 * jnp.arange(nz, dtype=jnp.int32)) % nrow
    slots = jnp.concatenate([sender, sender ^ 1]).astype(jnp.int32)

    rows = nse * nb // 2
    parted = bnd_index.reshape(ngroup, 2, rows)
    own_idx = lax.dynamic_index_in_dim(parted, group, 0, keepdims=False).reshape(-1)
    far_idx = lax.dynamic_index_in_dim(parted, core, 1, keepdims=False).reshape(-1)

    own_idx, far_idx, flat, conn, smat, where, slots, last_rows, first_rows = lax.optimization_barrier(
        (own_idx, far_idx, flat, conn, smat, where, slots, last_rows, first_rows)
    )
    picked = pick_near(own_idx, along_group, conn, smat)
    picked, far_idx, last_rows, first_rows, *tops = lax.optimization_barrier(
        (picked, far_idx, last_rows, first_rows, *tops)
    )
    near_other = to_other(picked)
    head = lax.ppermute(last_rows, "row", up)
    tail = lax.ppermute(first_rows, "row", down)
    nears = [picked] + [lax.ppermute(picked, "row", along(s)) for s in range(1, nz)]
    tops = tops + [top_other] + [to_other(x) for x in tops[1:]]
    per = LANES // tper
    order = [per * h + j for j in range(per) for h in range(nrow // per)]
    far = pick_far(far_idx, slots, tops, order)
    mine = lax.all_to_all(far.reshape(ngroup, rows, LANES), "group", split_axis=0, concat_axis=0, tiled=True)
    flat, far = lax.optimization_barrier((flat, far))
    w = combine(flat, block_se, conn, smat, recovery, head, tail, nse)
    mine, nears, w = lax.optimization_barrier((mine, nears, w))
    nears = nears + [near_other] + [to_other(x) for x in nears[1:]]
    mine, nears = lax.optimization_barrier((mine, nears))
    theirs = to_other(mine)
    near = arrange(slots, nears, ngroup, tper, nse * nb)
    out = product(where, w.reshape(nc * nel, nse * nb), mine, theirs, near, half, snap)
    return out.reshape(nc, nel, snap).transpose(1, 0, 2)


def solution(mesh):
    in_specs = (
        P(("group", "row"), None),
        P(),
        P(("group", "row"), None, None),
        P(("group", "row")),
        P(("group", "row"), None),
        P(("group", "row"), None, None),
    )
    out_specs = P(("group", "row"), None, None)
    return jax.shard_map(body, mesh=mesh, in_specs=in_specs, out_specs=out_specs, check_vma=False)
```

```python
import functools

import jax
import jax.numpy as jnp
from jax import lax
from jax.experimental import pallas as pl
from jax.experimental.pallas import tpu as pltpu
from jax.sharding import PartitionSpec as P

HW = 256
SUB = 8
LANES = 128


def combine_kernel(
    conn, se, grow_ref, s_ref, rec_hbm, head_ref, tail_ref, w_ref, tbl, buf, sem, g0, g1, g2, g3,
    *, nfill, blk, nlt, nse, nc, ndof, inner, ts, gs, nbuf
):
    step = pl.program_id(0)
    rows = SUB * ndof
    steps = pl.num_programs(0) - nfill

    def fetch(b):
        return pltpu.make_async_copy(rec_hbm.at[b], buf.at[b % nbuf], sem.at[b % nbuf])

    def fill(src, base, count):
        def one(i, carry):
            at = pl.multiple_of(i * 16, 16)
            for j in range(nlt):
                part = src[pl.ds(at, 16), j * LANES:(j + 1) * LANES].astype(jnp.float32)
                tbl[pl.ds((base + at) * ts + j, 16, stride=ts), :] = part
            return carry

        lax.fori_loop(0, count // 16, one, 0, unroll=4)

    def gather(group, dst, lo=0, hi=rows):
        first = group * rows
        for q in range(lo, hi):
            dst[pl.ds(q, nlt, stride=gs), :] = tbl[pl.ds(conn[first + q], nlt), :]

    own = (
        lax.broadcasted_iota(jnp.int32, (SUB, rows), 1) % SUB
        == lax.broadcasted_iota(jnp.int32, (SUB, rows), 0)
    )

    def halo_tag(ref, at):
        wide = -(-rows // LANES) * LANES
        return ref[at:at + 16, :wide].astype(jnp.float32)[:1, :rows].astype(jnp.int32)

    head_tag = halo_tag(head_ref, 0)
    tail_tag = halo_tag(tail_ref, HW)

    def left(i):
        where = (grow_ref[pl.ds(i, 1), :] + (blk - HW)) // blk
        tag = jnp.where(where == 0, head_tag, tail_tag)
        for b in range(nfill):
            tag = jnp.where(where == b + 1, se[b], tag)
        tag = jnp.where(own, jnp.broadcast_to(tag, (SUB, rows)), -1)
        parts = []
        for s in range(nse):
            hit = tag == s
            for c in range(nc):
                parts.append(jnp.where(hit, jnp.broadcast_to(s_ref[c, pl.ds(i, 1), :], (SUB, rows)), 0.0))
        return jnp.concatenate(parts, axis=0).astype(jnp.bfloat16)

    def matmul(first, i, srcs, nxt, dsts):
        lhs = [left(first + i), left(first + i + 1)]
        at = pl.multiple_of(i * SUB, 2 * SUB)
        for j in range(0, nlt, 2):
            res = []
            for t in range(2):
                src = srcs[t]
                rhs = jnp.concatenate(
                    [src[(j + d) * gs:(j + d) * gs + rows, :].astype(jnp.bfloat16) for d in range(2)], axis=1
                )
                res.append(jnp.dot(lhs[t], rhs, preferred_element_type=jnp.float32))
                gather(nxt + t, dsts[t], rows * j // nlt, rows * (j + 2) // nlt)
            for s in range(nse):
                col = (s * nlt + j) * LANES
                for c in range(nc):
                    r0 = (s * nc + c) * SUB
                    both = jnp.concatenate([r[r0:r0 + SUB] for r in res], axis=0)
                    w_ref[c, pl.ds(at, 2 * SUB), col:col + 2 * LANES] = both.astype(jnp.bfloat16)

    @pl.when(step == 0)
    def _():
        for b in range(nbuf):
            fetch(b).start()
        fill(head_ref.at[pl.ds(16, HW)], 0, HW)
        fill(tail_ref, HW + nfill * blk, HW)

    @pl.when(step < nfill)
    def _():
        fetch(step).wait()
        fill(buf.at[step % nbuf], HW + step * blk, blk)

        @pl.when(step + nbuf < nfill)
        def _():
            fetch(step + nbuf).start()

    @pl.when(step >= nfill)
    def _():
        base = (step - nfill) * inner
        last = steps * inner - 2

        @pl.when(step == nfill)
        def _():
            gather(0, g0)
            gather(1, g1)

        def four(i, carry):
            n = base + 4 * i
            matmul(base, 4 * i, (g0, g1), n + 2, (g2, g3))
            matmul(base, 4 * i + 2, (g2, g3), jnp.minimum(n + 4, last), (g0, g1))
            return carry

        lax.fori_loop(0, inner // 4, four, 0)


def combine(conn, se, grow, smat, recovery, head, tail, nse, inner=4, nbuf=6):
    nblk, blk, nb = recovery.shape
    ngrp, rows = grow.shape
    nel = ngrp * SUB
    ndof = rows // SUB
    nc = smat.shape[0]
    nlt = nb // LANES
    steps = ngrp // inner
    ts = nlt + 1
    gs = rows + 1
    kern = functools.partial(
        combine_kernel, nfill=nblk, blk=blk, nlt=nlt, nse=nse, nc=nc, ndof=ndof, inner=inner, ts=ts, gs=gs,
        nbuf=nbuf,
    )
    later = lambda i: jnp.maximum(i - nblk, 0)
    return pl.pallas_call(
        kern,
        out_shape=jax.ShapeDtypeStruct((nc, nel, nse * nb), jnp.bfloat16),
        grid_spec=pltpu.PrefetchScalarGridSpec(
            num_scalar_prefetch=2,
            grid=(nblk + steps,),
            in_specs=[
                pl.BlockSpec((ngrp, rows), lambda i, c, s: (0, 0)),
                pl.BlockSpec((nc, ngrp, rows), lambda i, c, s: (0, 0, 0)),
                pl.BlockSpec(memory_space=pl.ANY),
                pl.BlockSpec((HW + 16, nb), lambda i, c, s: (0, 0)),
                pl.BlockSpec((HW + 16, nb), lambda i, c, s: (0, 0)),
            ],
            out_specs=pl.BlockSpec((nc, SUB * inner, nse * nb), lambda i, c, s: (0, later(i), 0)),
            scratch_shapes=[
                pltpu.VMEM(((nblk * blk + 2 * HW) * ts, LANES), jnp.float32),
                pltpu.VMEM((nbuf, blk, nb), jnp.bfloat16),
                pltpu.SemaphoreType.DMA((nbuf,)),
            ] + [pltpu.VMEM((gs * nlt, LANES), jnp.float32)] * 4,
        ),
        compiler_params=pltpu.CompilerParams(dimension_semantics=("arbitrary",), vmem_limit_bytes=60 << 20),
        cost_estimate=pl.CostEstimate(flops=30 * 10**9, bytes_accessed=120 << 20, transcendentals=0),
        name="combine",
    )(conn, se, grow, smat, recovery, head, tail)


def pick_near_kernel(idx, src, grow_hbm, smat_hbm, o_ref, tbl, *bufs, parts, chunk):
    step = pl.program_id(0)
    nd = tbl.shape[0]
    total = chunk * pl.num_programs(0)

    @pl.when(step == 0)
    def _():
        def one(i, carry):
            at = pl.multiple_of(i * LANES, LANES)
            rows = jnp.concatenate([src[g, :, pl.ds(at, LANES)] for g in range(src.shape[0])] * parts, axis=0)
            tbl[pl.ds(at, LANES), :] = rows.T.astype(jnp.float32)
            return carry

        lax.fori_loop(0, nd // LANES, one, 0, unroll=2)

    def some(i, carry):
        at = pl.multiple_of(i * 64, 64)
        for p in range(parts):
            for q in range(64):
                k = idx[p * total + step * chunk + at + q]
                bufs[p][pl.ds(at + q, 1), :] = tbl[pl.ds(k, 1), :]
        return carry

    lax.fori_loop(0, chunk // 64, some, 0)
    piece = lax.broadcasted_iota(jnp.int32, (chunk, LANES), 1) // (LANES // parts)
    out = bufs[0][...]
    for p in range(1, parts):
        out = jnp.where(piece == p, bufs[p][...], out)
    o_ref[...] = out.astype(jnp.bfloat16)


def pick_near(idx, src, grow, smat):
    ngroup, half, nd = src.shape
    parts = LANES // (half * ngroup)
    n = idx.shape[0] // parts
    chunk = min(n, 1024)
    return pl.pallas_call(
        functools.partial(pick_near_kernel, parts=parts, chunk=chunk),
        out_shape=jax.ShapeDtypeStruct((n, LANES), jnp.bfloat16),
        grid_spec=pltpu.PrefetchScalarGridSpec(
            num_scalar_prefetch=1,
            grid=(n // chunk,),
            in_specs=[
                pl.BlockSpec((ngroup, half, nd), lambda i, c: (0, 0, 0)),
                pl.BlockSpec(memory_space=pl.ANY),
                pl.BlockSpec(memory_space=pl.ANY),
            ],
            out_specs=pl.BlockSpec((chunk, LANES), lambda i, c: (i, 0)),
            scratch_shapes=[pltpu.VMEM((nd, LANES), jnp.float32)]
            + [pltpu.VMEM((chunk, LANES), jnp.float32) for _ in range(parts)],
        ),
        compiler_params=pltpu.CompilerParams(
            dimension_semantics=("arbitrary",), vmem_limit_bytes=40 << 20
        ),
        name="pick_near",
    )(idx, src, grow, smat)


def pick_far_kernel(idx, slots, *refs, nsrc, order, chunk):
    srcs = refs[:nsrc]
    o_ref, src, tbl, buf, sem = refs[nsrc:]
    step = pl.program_id(0)
    nd = tbl.shape[0]

    @pl.when(step == 0)
    def _():
        copies = [
            pltpu.make_async_copy(ref, src.at[slots[i]], sem.at[i]) for i, ref in enumerate(srcs)
        ]
        for copy in copies:
            copy.start()
        for copy in copies:
            copy.wait()

        def one(i, carry):
            at = pl.multiple_of(i * LANES, LANES)
            rows = jnp.concatenate([src[r, :, pl.ds(at, LANES)] for r in order], axis=0)
            tbl[pl.ds(at, LANES), :] = rows.T.astype(jnp.float32)
            return carry

        lax.fori_loop(0, nd // LANES, one, 0, unroll=2)

    def some(i, carry):
        at = pl.multiple_of(i * 64, 64)
        for q in range(64):
            buf[pl.ds(at + q, 1), :] = tbl[pl.ds(idx[step * chunk + at + q], 1), :]
        return carry

    lax.fori_loop(0, chunk // 64, some, 0)
    o_ref[...] = buf[...].astype(jnp.bfloat16)


def pick_far(idx, slots, srcs, order):
    nrow = len(srcs)
    half, nd = srcs[0].shape
    n = idx.shape[0]
    chunk = min(n, 1024)
    return pl.pallas_call(
        functools.partial(pick_far_kernel, nsrc=nrow, order=order, chunk=chunk),
        out_shape=jax.ShapeDtypeStruct((n, LANES), jnp.bfloat16),
        grid_spec=pltpu.PrefetchScalarGridSpec(
            num_scalar_prefetch=2,
            grid=(n // chunk,),
            in_specs=[pl.BlockSpec(memory_space=pltpu.VMEM)] * nrow,
            out_specs=pl.BlockSpec((chunk, LANES), lambda i, c, d: (i, 0)),
            scratch_shapes=[
                pltpu.VMEM((nrow, half, nd), jnp.bfloat16),
                pltpu.VMEM((nd, LANES), jnp.float32),
                pltpu.VMEM((chunk, LANES), jnp.float32),
                pltpu.SemaphoreType.DMA((nrow,)),
            ],
        ),
        compiler_params=pltpu.CompilerParams(
            dimension_semantics=("arbitrary",), vmem_limit_bytes=40 << 20
        ),
        name="pick_far",
    )(idx, slots, *srcs)


def arrange_kernel(slots, *refs, nsrc, nh, per, npair, parts, tper):
    srcs = refs[:nsrc]
    o_ref, near, sem = refs[nsrc:]
    step_rows = o_ref.shape[1]
    step = pl.program_id(0)

    cut = near.shape[1] // 2

    def copies(part):
        where = pl.ds(part * cut, cut)
        return [
            pltpu.make_async_copy(ref.at[where], near.at[slots[i], where], sem.at[part, i])
            for i, ref in enumerate(srcs)
        ]

    @pl.when(step == 0)
    def _():
        for copy in copies(0) + copies(1):
            copy.start()
        for copy in copies(0):
            copy.wait()

    @pl.when(step * step_rows == cut)
    def _():
        for copy in copies(1):
            copy.wait()

    lane = lax.broadcasted_iota(jnp.int32, (step_rows, LANES), 1) // tper
    at = pl.multiple_of(step * step_rows, step_rows)
    for h in range(nh):
        got = [near[h * per + j, pl.ds(at, step_rows), :].astype(jnp.float32) for j in range(per)]
        for p in range(npair):
            for kp in range(parts):
                tile = None
                for j in range(per):
                    shift = (tper * j - (kp * (LANES // parts) + tper * p)) % LANES
                    moved = pltpu.roll(got[j], shift, 1) if shift else got[j]
                    tile = moved if tile is None else jnp.where(lane == j, moved, tile)
                col = (h * npair + p) * LANES
                o_ref[kp, :, col:col + LANES] = tile.astype(jnp.bfloat16)


def arrange(slots, srcs, ngroup, tper, k):
    nrow = len(srcs)
    nk = srcs[0].shape[0]
    nh = tper * nrow // LANES
    npair = ngroup // 2
    parts = k // nk
    cols = nh * npair * LANES
    step_rows = min(nk // 2, 256)
    out = pl.pallas_call(
        functools.partial(
            arrange_kernel, nsrc=nrow, nh=nh, per=LANES // tper, npair=npair, parts=parts, tper=tper
        ),
        out_shape=jax.ShapeDtypeStruct((parts, nk, cols), jnp.bfloat16),
        grid_spec=pltpu.PrefetchScalarGridSpec(
            num_scalar_prefetch=1,
            grid=(nk // step_rows,),
            in_specs=[pl.BlockSpec(memory_space=pltpu.VMEM)] * nrow,
            out_specs=pl.BlockSpec((parts, step_rows, cols), lambda i, c: (0, i, 0)),
            scratch_shapes=[
                pltpu.VMEM((nrow, nk, LANES), jnp.bfloat16),
                pltpu.SemaphoreType.DMA((2, nrow)),
            ],
        ),
        compiler_params=pltpu.CompilerParams(
            dimension_semantics=("arbitrary",), vmem_limit_bytes=40 << 20
        ),
        name="arrange",
    )(slots, *srcs)
    return out.reshape(k, cols)


def product_kernel(core, w_ref, mine, theirs, near, o_ref, bt, sem, *, ngroup, nh, half):
    npair = ngroup // 2
    rows = bt.shape[0] // 2

    copies = []
    for s in range(ngroup):
        cols = slice(s * LANES, (s + 1) * LANES)
        for d, ref in ((0, mine), (1, theirs)):
            at = pl.multiple_of(jnp.where(core[0] == d, 0, 1) * rows, rows)
            copies.append(pltpu.make_async_copy(ref.at[s], bt.at[pl.ds(at, rows), cols], sem.at[2 * s + d]))

    @pl.when(pl.program_id(0) == 0)
    def _():
        for c in copies:
            c.start()

    res_near = jnp.dot(w_ref[...], near[...], preferred_element_type=jnp.float32)

    @pl.when(pl.program_id(0) == 0)
    def _():
        for c in copies:
            c.wait()

    res = jnp.dot(w_ref[...], bt[...], preferred_element_type=jnp.float32)
    slot = (lax.broadcasted_iota(jnp.int32, (res.shape[0], LANES), 1) // half) % 2
    for s in range(ngroup):
        far = res[:, s * LANES:(s + 1) * LANES]
        for h in range(nh):
            first = pltpu.roll(far, LANES - half * h, 1) if h else far
            at = (h * npair + s // 2) * LANES
            second = res_near[:, at:at + LANES]
            if s % 2 == 0:
                second = pltpu.roll(second, half, 1)
            tile = jnp.where(slot == 0, first, second).astype(jnp.bfloat16)
            col = (s * nh + h) * LANES
            o_ref[:, col:col + LANES] = tile


def product(where, w, mine, theirs, near, half, snap):
    m, k = w.shape
    ngroup = mine.shape[0]
    mb = 512
    return pl.pallas_call(
        functools.partial(product_kernel, ngroup=ngroup, nh=snap // (ngroup * LANES), half=half),
        out_shape=jax.ShapeDtypeStruct((m, snap), jnp.bfloat16),
        grid_spec=pltpu.PrefetchScalarGridSpec(
            num_scalar_prefetch=1,
            grid=(m // mb,),
            in_specs=[pl.BlockSpec((mb, k), lambda i, c: (i, 0))]
            + [pl.BlockSpec(memory_space=pltpu.VMEM)] * 3,
            out_specs=pl.BlockSpec((mb, snap), lambda i, c: (i, 0)),
            scratch_shapes=[
                pltpu.VMEM((k, ngroup * LANES), jnp.bfloat16),
                pltpu.SemaphoreType.DMA((2 * ngroup,)),
            ],
        ),
        compiler_params=pltpu.CompilerParams(
            dimension_semantics=("arbitrary",), vmem_limit_bytes=36 << 20
        ),
        name="product",
    )(where, w, mine, theirs, near)


def body(snapshots, bnd_index, recovery, block_se, connect, stress_mat):
    ngroup = lax.axis_size("group")
    nrow = lax.axis_size("row")
    nse = bnd_index.shape[0] // ngroup
    nblk, blk, nb = recovery.shape
    nel, nc, ndof = stress_mat.shape
    tper = snapshots.shape[0]
    half = tper // 2
    snap = tper * ngroup * nrow
    group = lax.axis_index("group")
    core = lax.axis_index("row") % 2
    other = [(i, i ^ 1) for i in range(nrow)]

    top = snapshots[:half]
    bottom = snapshots[half:]
    row = lax.axis_index("row")
    nz = nrow // 2
    along = lambda s: [(i, (i + 2 * s) % nrow) for i in range(nrow)]
    to_other = lambda x: lax.ppermute(x, "row", other)
    tops = [top] + [lax.ppermute(top, "row", along(s)) for s in range(1, nz)]
    top_other = to_other(top)
    along_group = lax.all_to_all(
        jnp.broadcast_to(bottom, (ngroup, *bottom.shape)), "group", split_axis=0, concat_axis=0, tiled=True
    )

    ends = nrow - 1
    up = [(i, i + 1) for i in range(ends)]
    down = [(i + 1, i) for i in range(ends)]

    def with_se(part, se, first):
        row_id = lax.broadcasted_iota(jnp.int32, part.shape, 0) - first
        return jnp.where((row_id >= 0) & (row_id < 16), se.astype(part.dtype), part)

    last_rows = with_se(recovery[nblk - 1, blk - HW - 16:], block_se[nblk - 1], 0)
    first_rows = with_se(recovery[0, :HW + 16], block_se[0], HW)

    ngrp = nel // SUB
    conn = connect.T.reshape(ndof, ngrp, SUB).transpose(1, 0, 2).reshape(ngrp, ndof * SUB)
    smat = stress_mat.transpose(1, 2, 0).astype(jnp.float32).reshape(nc, ndof, ngrp, SUB)
    smat = smat.transpose(0, 2, 1, 3).reshape(nc, ngrp, ndof * SUB)
    flat = conn.reshape(-1) * (nb // LANES + 1)
    where = core.reshape(1).astype(jnp.int32)
    sender = (row - 2 * jnp.arange(nz, dtype=jnp.int32)) % nrow
    slots = jnp.concatenate([sender, sender ^ 1]).astype(jnp.int32)

    rows = nse * nb // 2
    parted = bnd_index.reshape(ngroup, 2, rows)
    own_idx = lax.dynamic_index_in_dim(parted, group, 0, keepdims=False).reshape(-1)
    far_idx = lax.dynamic_index_in_dim(parted, core, 1, keepdims=False).reshape(-1)

    own_idx, far_idx, flat, conn, smat, where, slots, last_rows, first_rows = lax.optimization_barrier(
        (own_idx, far_idx, flat, conn, smat, where, slots, last_rows, first_rows)
    )
    picked = pick_near(own_idx, along_group, conn, smat)
    picked, far_idx, last_rows, first_rows, *tops = lax.optimization_barrier(
        (picked, far_idx, last_rows, first_rows, *tops)
    )
    near_other = to_other(picked)
    head = lax.ppermute(last_rows, "row", up)
    tail = lax.ppermute(first_rows, "row", down)
    nears = [picked] + [lax.ppermute(picked, "row", along(s)) for s in range(1, nz)]
    tops = tops + [top_other] + [to_other(x) for x in tops[1:]]
    per = LANES // tper
    order = [per * h + j for j in range(per) for h in range(nrow // per)]
    far = pick_far(far_idx, slots, tops, order)
    mine = lax.all_to_all(far.reshape(ngroup, rows, LANES), "group", split_axis=0, concat_axis=0, tiled=True)
    flat, far = lax.optimization_barrier((flat, far))
    w = combine(flat, block_se, conn, smat, recovery, head, tail, nse)
    mine, nears, w = lax.optimization_barrier((mine, nears, w))
    nears = nears + [near_other] + [to_other(x) for x in nears[1:]]
    mine, nears = lax.optimization_barrier((mine, nears))
    theirs = to_other(mine)
    near = arrange(slots, nears, ngroup, tper, nse * nb)
    out = product(where, w.reshape(nc * nel, nse * nb), mine, theirs, near, half, snap)
    return out.reshape(nc, nel, snap).transpose(1, 0, 2)


def solution(mesh):
    in_specs = (
        P(("group", "row"), None),
        P(),
        P(("group", "row"), None, None),
        P(("group", "row")),
        P(("group", "row"), None),
        P(("group", "row"), None, None),
    )
    out_specs = P(("group", "row"), None, None)
    return jax.shard_map(body, mesh=mesh, in_specs=in_specs, out_specs=out_specs, check_vma=False)
```

```python
import functools

import jax
import jax.numpy as jnp
from jax import lax
from jax.experimental import pallas as pl
from jax.experimental.pallas import tpu as pltpu
from jax.sharding import PartitionSpec as P

HW = 256
SUB = 8
LANES = 128


def combine_kernel(
    conn, se, grow_ref, s_ref, rec_hbm, head_ref, tail_ref, w_ref, tbl, buf, sem, g0, g1, g2, g3,
    *, nfill, blk, nlt, nse, nc, ndof, inner, ts, gs, nbuf
):
    step = pl.program_id(0)
    rows = SUB * ndof
    steps = pl.num_programs(0) - nfill

    def fetch(b):
        return pltpu.make_async_copy(rec_hbm.at[b], buf.at[b % nbuf], sem.at[b % nbuf])

    def fill(src, base, count):
        def one(i, carry):
            at = pl.multiple_of(i * 16, 16)
            for j in range(nlt):
                part = src[pl.ds(at, 16), j * LANES:(j + 1) * LANES].astype(jnp.float32)
                tbl[pl.ds((base + at) * ts + j, 16, stride=ts), :] = part
            return carry

        lax.fori_loop(0, count // 16, one, 0, unroll=4)

    def gather(group, dst, lo=0, hi=rows):
        first = group * rows
        for q in range(lo, hi):
            dst[pl.ds(q, nlt, stride=gs), :] = tbl[pl.ds(conn[first + q], nlt), :]

    own = (
        lax.broadcasted_iota(jnp.int32, (SUB, rows), 1) % SUB
        == lax.broadcasted_iota(jnp.int32, (SUB, rows), 0)
    )

    def halo_tag(ref, at):
        wide = -(-rows // LANES) * LANES
        return ref[at:at + 16, :wide].astype(jnp.float32)[:1, :rows].astype(jnp.int32)

    head_tag = halo_tag(head_ref, 0)
    tail_tag = halo_tag(tail_ref, HW)

    def left(i):
        where = (grow_ref[pl.ds(i, 1), :] + (blk - HW)) // blk
        tag = jnp.where(where == 0, head_tag, tail_tag)
        for b in range(nfill):
            tag = jnp.where(where == b + 1, se[b], tag)
        tag = jnp.where(own, jnp.broadcast_to(tag, (SUB, rows)), -1)
        parts = []
        for s in range(nse):
            hit = tag == s
            for c in range(nc):
                parts.append(jnp.where(hit, jnp.broadcast_to(s_ref[c, pl.ds(i, 1), :], (SUB, rows)), 0.0))
        return jnp.concatenate(parts, axis=0).astype(jnp.bfloat16)

    def matmul(first, i, srcs, nxt, dsts):
        lhs = [left(first + i), left(first + i + 1)]
        at = pl.multiple_of(i * SUB, 2 * SUB)
        for j in range(0, nlt, 2):
            res = []
            for t in range(2):
                src = srcs[t]
                rhs = jnp.concatenate(
                    [src[(j + d) * gs:(j + d) * gs + rows, :].astype(jnp.bfloat16) for d in range(2)], axis=1
                )
                res.append(jnp.dot(lhs[t], rhs, preferred_element_type=jnp.float32))
                gather(nxt + t, dsts[t], rows * j // nlt, rows * (j + 2) // nlt)
            for s in range(nse):
                col = (s * nlt + j) * LANES
                for c in range(nc):
                    r0 = (s * nc + c) * SUB
                    both = jnp.concatenate([r[r0:r0 + SUB] for r in res], axis=0)
                    w_ref[c, pl.ds(at, 2 * SUB), col:col + 2 * LANES] = both.astype(jnp.bfloat16)

    @pl.when(step == 0)
    def _():
        for b in range(nbuf):
            fetch(b).start()
        fill(head_ref.at[pl.ds(16, HW)], 0, HW)
        fill(tail_ref, HW + nfill * blk, HW)

    @pl.when(step < nfill)
    def _():
        fetch(step).wait()
        fill(buf.at[step % nbuf], HW + step * blk, blk)

        @pl.when(step + nbuf < nfill)
        def _():
            fetch(step + nbuf).start()

    @pl.when(step >= nfill)
    def _():
        base = (step - nfill) * inner
        last = steps * inner - 2

        @pl.when(step == nfill)
        def _():
            gather(0, g0)
            gather(1, g1)

        def four(i, carry):
            n = base + 4 * i
            matmul(base, 4 * i, (g0, g1), n + 2, (g2, g3))
            matmul(base, 4 * i + 2, (g2, g3), jnp.minimum(n + 4, last), (g0, g1))
            return carry

        lax.fori_loop(0, inner // 4, four, 0)


def combine(conn, se, grow, smat, recovery, head, tail, nse, inner=4, nbuf=6):
    nblk, blk, nb = recovery.shape
    ngrp, rows = grow.shape
    nel = ngrp * SUB
    ndof = rows // SUB
    nc = smat.shape[0]
    nlt = nb // LANES
    steps = ngrp // inner
    ts = nlt + 1
    gs = rows + 1
    kern = functools.partial(
        combine_kernel, nfill=nblk, blk=blk, nlt=nlt, nse=nse, nc=nc, ndof=ndof, inner=inner, ts=ts, gs=gs,
        nbuf=nbuf,
    )
    later = lambda i: jnp.maximum(i - nblk, 0)
    return pl.pallas_call(
        kern,
        out_shape=jax.ShapeDtypeStruct((nc, nel, nse * nb), jnp.bfloat16),
        grid_spec=pltpu.PrefetchScalarGridSpec(
            num_scalar_prefetch=2,
            grid=(nblk + steps,),
            in_specs=[
                pl.BlockSpec((ngrp, rows), lambda i, c, s: (0, 0)),
                pl.BlockSpec((nc, ngrp, rows), lambda i, c, s: (0, 0, 0)),
                pl.BlockSpec(memory_space=pl.ANY),
                pl.BlockSpec((HW + 16, nb), lambda i, c, s: (0, 0)),
                pl.BlockSpec((HW + 16, nb), lambda i, c, s: (0, 0)),
            ],
            out_specs=pl.BlockSpec((nc, SUB * inner, nse * nb), lambda i, c, s: (0, later(i), 0)),
            scratch_shapes=[
                pltpu.VMEM(((nblk * blk + 2 * HW) * ts, LANES), jnp.float32),
                pltpu.VMEM((nbuf, blk, nb), jnp.bfloat16),
                pltpu.SemaphoreType.DMA((nbuf,)),
            ] + [pltpu.VMEM((gs * nlt, LANES), jnp.float32)] * 4,
        ),
        compiler_params=pltpu.CompilerParams(dimension_semantics=("arbitrary",), vmem_limit_bytes=60 << 20),
        cost_estimate=pl.CostEstimate(flops=30 * 10**9, bytes_accessed=120 << 20, transcendentals=0),
        name="combine",
    )(conn, se, grow, smat, recovery, head, tail)


def pick_near_kernel(idx, src, grow_hbm, smat_hbm, o_ref, tbl, *bufs, parts, chunk):
    step = pl.program_id(0)
    nd = tbl.shape[0]
    total = chunk * pl.num_programs(0)

    @pl.when(step == 0)
    def _():
        def one(i, carry):
            at = pl.multiple_of(i * LANES, LANES)
            rows = jnp.concatenate([src[g, :, pl.ds(at, LANES)] for g in range(src.shape[0])] * parts, axis=0)
            tbl[pl.ds(at, LANES), :] = rows.T.astype(jnp.float32)
            return carry

        lax.fori_loop(0, nd // LANES, one, 0, unroll=2)

    def some(i, carry):
        at = pl.multiple_of(i * 64, 64)
        for p in range(parts):
            for q in range(64):
                k = idx[p * total + step * chunk + at + q]
                bufs[p][pl.ds(at + q, 1), :] = tbl[pl.ds(k, 1), :]
        return carry

    lax.fori_loop(0, chunk // 64, some, 0)
    piece = lax.broadcasted_iota(jnp.int32, (chunk, LANES), 1) // (LANES // parts)
    out = bufs[0][...]
    for p in range(1, parts):
        out = jnp.where(piece == p, bufs[p][...], out)
    o_ref[...] = out.astype(jnp.bfloat16)


def pick_near(idx, src, grow, smat):
    ngroup, half, nd = src.shape
    parts = LANES // (half * ngroup)
    n = idx.shape[0] // parts
    chunk = min(n, 1024)
    return pl.pallas_call(
        functools.partial(pick_near_kernel, parts=parts, chunk=chunk),
        out_shape=jax.ShapeDtypeStruct((n, LANES), jnp.bfloat16),
        grid_spec=pltpu.PrefetchScalarGridSpec(
            num_scalar_prefetch=1,
            grid=(n // chunk,),
            in_specs=[
                pl.BlockSpec((ngroup, half, nd), lambda i, c: (0, 0, 0)),
                pl.BlockSpec(memory_space=pl.ANY),
                pl.BlockSpec(memory_space=pl.ANY),
            ],
            out_specs=pl.BlockSpec((chunk, LANES), lambda i, c: (i, 0)),
            scratch_shapes=[pltpu.VMEM((nd, LANES), jnp.float32)]
            + [pltpu.VMEM((chunk, LANES), jnp.float32) for _ in range(parts)],
        ),
        compiler_params=pltpu.CompilerParams(
            dimension_semantics=("arbitrary",), vmem_limit_bytes=40 << 20
        ),
        name="pick_near",
    )(idx, src, grow, smat)


def pick_far_kernel(idx, slots, *refs, nsrc, order, chunk):
    srcs = refs[:nsrc]
    o_ref, src, tbl, buf, sem = refs[nsrc:]
    step = pl.program_id(0)
    nd = tbl.shape[0]

    @pl.when(step == 0)
    def _():
        copies = [
            pltpu.make_async_copy(ref, src.at[slots[i]], sem.at[i]) for i, ref in enumerate(srcs)
        ]
        for copy in copies:
            copy.start()
        for copy in copies:
            copy.wait()

        def one(i, carry):
            at = pl.multiple_of(i * LANES, LANES)
            rows = jnp.concatenate([src[r, :, pl.ds(at, LANES)] for r in order], axis=0)
            tbl[pl.ds(at, LANES), :] = rows.T.astype(jnp.float32)
            return carry

        lax.fori_loop(0, nd // LANES, one, 0, unroll=2)

    def some(i, carry):
        at = pl.multiple_of(i * 64, 64)
        for q in range(64):
            buf[pl.ds(at + q, 1), :] = tbl[pl.ds(idx[step * chunk + at + q], 1), :]
        return carry

    lax.fori_loop(0, chunk // 64, some, 0)
    o_ref[...] = buf[...].astype(jnp.bfloat16)


def pick_far(idx, slots, srcs, order):
    nrow = len(srcs)
    half, nd = srcs[0].shape
    n = idx.shape[0]
    chunk = min(n, 1024)
    return pl.pallas_call(
        functools.partial(pick_far_kernel, nsrc=nrow, order=order, chunk=chunk),
        out_shape=jax.ShapeDtypeStruct((n, LANES), jnp.bfloat16),
        grid_spec=pltpu.PrefetchScalarGridSpec(
            num_scalar_prefetch=2,
            grid=(n // chunk,),
            in_specs=[pl.BlockSpec(memory_space=pltpu.VMEM)] * nrow,
            out_specs=pl.BlockSpec((chunk, LANES), lambda i, c, d: (i, 0)),
            scratch_shapes=[
                pltpu.VMEM((nrow, half, nd), jnp.bfloat16),
                pltpu.VMEM((nd, LANES), jnp.float32),
                pltpu.VMEM((chunk, LANES), jnp.float32),
                pltpu.SemaphoreType.DMA((nrow,)),
            ],
        ),
        compiler_params=pltpu.CompilerParams(
            dimension_semantics=("arbitrary",), vmem_limit_bytes=40 << 20
        ),
        name="pick_far",
    )(idx, slots, *srcs)


def arrange_kernel(slots, *refs, nsrc, nh, per, npair, parts, tper):
    srcs = refs[:nsrc]
    o_ref, near, sem = refs[nsrc:]
    step_rows = o_ref.shape[1]
    step = pl.program_id(0)

    cut = near.shape[1] // 2

    def copies(part):
        where = pl.ds(part * cut, cut)
        return [
            pltpu.make_async_copy(ref.at[where], near.at[slots[i], where], sem.at[part, i])
            for i, ref in enumerate(srcs)
        ]

    @pl.when(step == 0)
    def _():
        for copy in copies(0) + copies(1):
            copy.start()
        for copy in copies(0):
            copy.wait()

    @pl.when(step * step_rows == cut)
    def _():
        for copy in copies(1):
            copy.wait()

    lane = lax.broadcasted_iota(jnp.int32, (step_rows, LANES), 1) // tper
    at = pl.multiple_of(step * step_rows, step_rows)
    for h in range(nh):
        got = [near[h * per + j, pl.ds(at, step_rows), :].astype(jnp.float32) for j in range(per)]
        for p in range(npair):
            for kp in range(parts):
                tile = None
                for j in range(per):
                    shift = (tper * j - (kp * (LANES // parts) + tper * p)) % LANES
                    moved = pltpu.roll(got[j], shift, 1) if shift else got[j]
                    tile = moved if tile is None else jnp.where(lane == j, moved, tile)
                col = (h * npair + p) * LANES
                o_ref[kp, :, col:col + LANES] = tile.astype(jnp.bfloat16)


def arrange(slots, srcs, ngroup, tper, k):
    nrow = len(srcs)
    nk = srcs[0].shape[0]
    nh = tper * nrow // LANES
    npair = ngroup // 2
    parts = k // nk
    cols = nh * npair * LANES
    step_rows = min(nk // 2, 512)
    out = pl.pallas_call(
        functools.partial(
            arrange_kernel, nsrc=nrow, nh=nh, per=LANES // tper, npair=npair, parts=parts, tper=tper
        ),
        out_shape=jax.ShapeDtypeStruct((parts, nk, cols), jnp.bfloat16),
        grid_spec=pltpu.PrefetchScalarGridSpec(
            num_scalar_prefetch=1,
            grid=(nk // step_rows,),
            in_specs=[pl.BlockSpec(memory_space=pltpu.VMEM)] * nrow,
            out_specs=pl.BlockSpec((parts, step_rows, cols), lambda i, c: (0, i, 0)),
            scratch_shapes=[
                pltpu.VMEM((nrow, nk, LANES), jnp.bfloat16),
                pltpu.SemaphoreType.DMA((2, nrow)),
            ],
        ),
        compiler_params=pltpu.CompilerParams(
            dimension_semantics=("arbitrary",), vmem_limit_bytes=40 << 20
        ),
        name="arrange",
    )(slots, *srcs)
    return out.reshape(k, cols)


def product_kernel(core, w_ref, mine, theirs, near, o_ref, bt, sem, *, ngroup, nh, half):
    npair = ngroup // 2
    rows = bt.shape[0] // 2

    copies = []
    for s in range(ngroup):
        cols = slice(s * LANES, (s + 1) * LANES)
        for d, ref in ((0, mine), (1, theirs)):
            at = pl.multiple_of(jnp.where(core[0] == d, 0, 1) * rows, rows)
            copies.append(pltpu.make_async_copy(ref.at[s], bt.at[pl.ds(at, rows), cols], sem.at[2 * s + d]))

    @pl.when(pl.program_id(0) == 0)
    def _():
        for c in copies:
            c.start()

    res_near = jnp.dot(w_ref[...], near[...], preferred_element_type=jnp.float32)

    @pl.when(pl.program_id(0) == 0)
    def _():
        for c in copies:
            c.wait()

    res = jnp.dot(w_ref[...], bt[...], preferred_element_type=jnp.float32)
    slot = (lax.broadcasted_iota(jnp.int32, (res.shape[0], LANES), 1) // half) % 2
    for s in range(ngroup):
        far = res[:, s * LANES:(s + 1) * LANES]
        for h in range(nh):
            first = pltpu.roll(far, LANES - half * h, 1) if h else far
            at = (h * npair + s // 2) * LANES
            second = res_near[:, at:at + LANES]
            if s % 2 == 0:
                second = pltpu.roll(second, half, 1)
            tile = jnp.where(slot == 0, first, second).astype(jnp.bfloat16)
            col = (s * nh + h) * LANES
            o_ref[:, col:col + LANES] = tile


def product(where, w, mine, theirs, near, half, snap):
    m, k = w.shape
    ngroup = mine.shape[0]
    mb = 512
    return pl.pallas_call(
        functools.partial(product_kernel, ngroup=ngroup, nh=snap // (ngroup * LANES), half=half),
        out_shape=jax.ShapeDtypeStruct((m, snap), jnp.bfloat16),
        grid_spec=pltpu.PrefetchScalarGridSpec(
            num_scalar_prefetch=1,
            grid=(m // mb,),
            in_specs=[pl.BlockSpec((mb, k), lambda i, c: (i, 0))]
            + [pl.BlockSpec(memory_space=pltpu.VMEM)] * 3,
            out_specs=pl.BlockSpec((mb, snap), lambda i, c: (i, 0)),
            scratch_shapes=[
                pltpu.VMEM((k, ngroup * LANES), jnp.bfloat16),
                pltpu.SemaphoreType.DMA((2 * ngroup,)),
            ],
        ),
        compiler_params=pltpu.CompilerParams(
            dimension_semantics=("arbitrary",), vmem_limit_bytes=36 << 20
        ),
        name="product",
    )(where, w, mine, theirs, near)


def body(snapshots, bnd_index, recovery, block_se, connect, stress_mat):
    ngroup = lax.axis_size("group")
    nrow = lax.axis_size("row")
    nse = bnd_index.shape[0] // ngroup
    nblk, blk, nb = recovery.shape
    nel, nc, ndof = stress_mat.shape
    tper = snapshots.shape[0]
    half = tper // 2
    snap = tper * ngroup * nrow
    group = lax.axis_index("group")
    core = lax.axis_index("row") % 2
    other = [(i, i ^ 1) for i in range(nrow)]

    top = snapshots[:half]
    bottom = snapshots[half:]
    row = lax.axis_index("row")
    nz = nrow // 2
    along = lambda s: [(i, (i + 2 * s) % nrow) for i in range(nrow)]
    to_other = lambda x: lax.ppermute(x, "row", other)
    tops = [top] + [lax.ppermute(top, "row", along(s)) for s in range(1, nz)]
    top_other = to_other(top)
    along_group = lax.all_to_all(
        jnp.broadcast_to(bottom, (ngroup, *bottom.shape)), "group", split_axis=0, concat_axis=0, tiled=True
    )

    ends = nrow - 1
    up = [(i, i + 1) for i in range(ends)]
    down = [(i + 1, i) for i in range(ends)]

    def with_se(part, se, first):
        row_id = lax.broadcasted_iota(jnp.int32, part.shape, 0) - first
        return jnp.where((row_id >= 0) & (row_id < 16), se.astype(part.dtype), part)

    last_rows = with_se(recovery[nblk - 1, blk - HW - 16:], block_se[nblk - 1], 0)
    first_rows = with_se(recovery[0, :HW + 16], block_se[0], HW)

    ngrp = nel // SUB
    conn = connect.T.reshape(ndof, ngrp, SUB).transpose(1, 0, 2).reshape(ngrp, ndof * SUB)
    smat = stress_mat.transpose(1, 2, 0).astype(jnp.float32).reshape(nc, ndof, ngrp, SUB)
    smat = smat.transpose(0, 2, 1, 3).reshape(nc, ngrp, ndof * SUB)
    flat = conn.reshape(-1) * (nb // LANES + 1)
    where = core.reshape(1).astype(jnp.int32)
    sender = (row - 2 * jnp.arange(nz, dtype=jnp.int32)) % nrow
    slots = jnp.concatenate([sender, sender ^ 1]).astype(jnp.int32)

    rows = nse * nb // 2
    parted = bnd_index.reshape(ngroup, 2, rows)
    own_idx = lax.dynamic_index_in_dim(parted, group, 0, keepdims=False).reshape(-1)
    far_idx = lax.dynamic_index_in_dim(parted, core, 1, keepdims=False).reshape(-1)

    own_idx, far_idx, flat, conn, smat, where, slots, last_rows, first_rows = lax.optimization_barrier(
        (own_idx, far_idx, flat, conn, smat, where, slots, last_rows, first_rows)
    )
    picked = pick_near(own_idx, along_group, conn, smat)
    picked, far_idx, last_rows, first_rows, *tops = lax.optimization_barrier(
        (picked, far_idx, last_rows, first_rows, *tops)
    )
    near_other = to_other(picked)
    head = lax.ppermute(last_rows, "row", up)
    tail = lax.ppermute(first_rows, "row", down)
    nears = [picked] + [lax.ppermute(picked, "row", along(s)) for s in range(1, nz)]
    tops = tops + [top_other] + [to_other(x) for x in tops[1:]]
    per = LANES // tper
    order = [per * h + j for j in range(per) for h in range(nrow // per)]
    far = pick_far(far_idx, slots, tops, order)
    mine = lax.all_to_all(far.reshape(ngroup, rows, LANES), "group", split_axis=0, concat_axis=0, tiled=True)
    flat, far = lax.optimization_barrier((flat, far))
    w = combine(flat, block_se, conn, smat, recovery, head, tail, nse)
    mine, nears, w = lax.optimization_barrier((mine, nears, w))
    nears = nears + [near_other] + [to_other(x) for x in nears[1:]]
    mine, nears = lax.optimization_barrier((mine, nears))
    theirs = to_other(mine)
    near = arrange(slots, nears, ngroup, tper, nse * nb)
    out = product(where, w.reshape(nc * nel, nse * nb), mine, theirs, near, half, snap)
    return out.reshape(nc, nel, snap).transpose(1, 0, 2)


def solution(mesh):
    in_specs = (
        P(("group", "row"), None),
        P(),
        P(("group", "row"), None, None),
        P(("group", "row")),
        P(("group", "row"), None),
        P(("group", "row"), None, None),
    )
    out_specs = P(("group", "row"), None, None)
    return jax.shard_map(body, mesh=mesh, in_specs=in_specs, out_specs=out_specs, check_vma=False)
```
